32 devices in a mesh: dp: 16 (over z, x, core), tensor: 2 (over y).
Axes of the slice: x: 2, y: 2, z: 4, core: 2. Of those that a mesh axis runs over, the one named last changes fastest.
Arguments:
- hidden: bfloat16 [2048, 4096], P('dp', 'tensor'), may hold values from -6 to 6
- norm_gain: float32 [4096], replicated, may hold values from 0.1 to 1.9
- w_query: bfloat16 [4096, 4096], P('dp', 'tensor'), may hold values from -0.09375 to 0.09375
- w_key: bfloat16 [4096, 1024], P('dp', 'tensor'), may hold values from -0.09375 to 0.09375
- w_value: bfloat16 [4096, 1024], P('dp', 'tensor'), may hold values from -0.09375 to 0.09375
- upstream: bfloat16 [2048, 4096], P('dp', 'tensor'), may hold values from -6 to 6
- cached: float32 [16, 4096], P(None, 'tensor'), may hold values from -192 to 192
- lengths: int32 [16], replicated, may hold values from 1 to 512, 2048 in all
Outputs:
- grad_hidden: bfloat16 [2048, 4096], P('dp', 'tensor')
- grad_wkey: float32 [4096, 1024], P('dp', 'tensor')
The draws below stay inside these ranges and needn't reach their ends.
Inputs may be any that keep to these rules, and one draw needn't show every extreme that they name: The 16 documents are laid end to end and fill the stream; their lengths sum to 2048 and the longest has exactly 512 tokens.
All inputs are finite; a program needn't handle non-finite values.
Results may differ from the reference program's by a relative error of at most 0.015.
Values may be sent and summed in bfloat16 or wider, within the bound.
No kernel may reach another device: no remote copies, remote signals or barrier semaphores. Data moves between devices by JAX's collectives and lax.ppermute only.
A program may use at most 128 MiB of HBM per device.

```python
import math
import jax
import jax.numpy as jnp
import numpy as np
from jax import lax

D = 4096
QH = 32
KVH = 8
HD = 128
TOK_DEV = 128
TOKENS = 2048
NDOCS = 16
LONGEST = 512
N_TENSOR = 2


def raised(values, own_key, source, target, parts, factor):
    def block_of(position):
        return (jnp.arange(values.shape[position]) // (values.shape[position] // parts)).reshape((-1,) + (1,) * (values.ndim - 1 - position))

    one_side = jax.random.permutation(own_key, parts)[block_of(target)]
    other_side = (block_of(target) + parts // 2) % parts
    return jnp.where((block_of(source) == one_side) | (block_of(source) == other_side), factor * values, values)


def block_levels(rng, dims, pieces, smallest, top_value):
    loudness, own = 1.0, jax.random.fold_in(rng, 6)
    for axis_at, blocks in pieces:
        draws = jnp.exp(jax.random.uniform(jax.random.fold_in(own, axis_at), (blocks,), jnp.float32, smallest / len(pieces), top_value / len(pieces)))
        loudness = loudness * jnp.repeat(draws, dims[axis_at] // blocks).reshape([-1 if axis == axis_at else 1 for axis in range(len(dims))])
    return loudness


def profile(number_of, total, bound, slope):
    loads = [(1 << 20) // math.isqrt(standing ** slope) + 1 for standing in range(2, number_of + 1)]
    spare, counts = total - bound - (number_of - 1), [1] * (number_of - 1)
    while spare > 0:
        free = [i for i in range(number_of - 1) if counts[i] < bound]
        mass, left = sum([loads[i] for i in free]), spare
        for i in free:
            more = min(bound - counts[i], max(1, left * loads[i] // mass), spare)
            counts[i] = counts[i] + more
            spare = spare - more
    return np.array([bound] + counts)


def ragged(rng, amount, total, bound, skew):
    if amount == 2:
        one = jax.random.randint(rng, (), max(1, total - bound), min(bound, total - 1) + 1)
        return jnp.stack([one, total - one])
    sizes = jnp.asarray(profile(amount, total, bound, skew), jnp.int32)
    couples = (amount - 1) // 2
    source_of, receiver = sizes[1:1 + 2 * couples:2], sizes[2:2 + 2 * couples:2]
    room = jnp.minimum(source_of - 1, bound - receiver)
    shifted = jax.random.randint(jax.random.fold_in(rng, 1), (couples,), 0, 1 << 20) % (room + 1)
    sizes = sizes.at[1:1 + 2 * couples:2].set(source_of - shifted).at[2:2 + 2 * couples:2].set(receiver + shifted)
    return sizes[jax.random.permutation(jax.random.fold_in(rng, 2), amount)]


def gaussian(own_key, extent, deviation, most, split=(), kind=jnp.bfloat16):
    drawn = deviation * jax.random.normal(own_key, extent, jnp.float32)
    if split:
        drawn = drawn * block_levels(own_key, extent, split, -0.22, 0.18)
    return jnp.clip(drawn, -most, most).astype(kind)


def bell_draw_with(rng, extent, deviation, limit, pieces, heavy, held_as=jnp.bfloat16):
    result = deviation * jax.random.normal(rng, extent, jnp.float32)
    if pieces:
        result = result * block_levels(rng, extent, pieces, -0.22, 0.18)
    return jnp.clip(raised(result, jax.random.fold_in(rng, 3), *heavy), -limit, limit).astype(held_as)


def setup_inputs(seed: int = 0) -> dict:
    splits = jax.random.split(jax.random.key(seed), 9)
    return {
        "hidden": bell_draw_with(splits[0], (TOKENS, D), 1.0, 6.0, ((0, 16), (1, 2)), (0, 1, 16, 2.0)),
        "norm_gain": jnp.clip(1.0 + 0.18 * jax.random.normal(splits[1], (D,), jnp.float32), 0.1, 1.9),
        "w_query": gaussian(splits[2], (D, QH * HD), D ** -0.5, 0.09375, ((0, 16), (1, 2))),
        "w_key": gaussian(splits[3], (D, KVH * HD), D ** -0.5, 0.09375, ((0, 16), (1, 2))),
        "w_value": gaussian(splits[4], (D, KVH * HD), D ** -0.5, 0.09375, ((0, 16), (1, 2))),
        "upstream": gaussian(splits[5], (TOKENS, QH * HD), 1.0, 6.0, ((0, 16), (1, 2))),
        "cached": gaussian(splits[6], (NDOCS, QH * HD), 32.0, 192.0, ((1, 2),), jnp.float32),
        "lengths": ragged(splits[7], NDOCS, TOKENS, LONGEST, 2).astype(jnp.int32),
    }


EPSILON = 1e-05
ROPE_BASE = 500000.0

def document_info(lengths, positions_global):
    doc_ends = jnp.cumsum(lengths).astype(jnp.int32)
    documents = lax.optimization_barrier(jnp.sum((positions_global[:, None] >= doc_ends[None, :]).astype(jnp.int32), axis=1)).astype(jnp.int32)
    doc_slots = jnp.arange(lengths.shape[0], dtype=jnp.int32)
    onehot = documents[:, None] == doc_slots[None, :]
    doc_len = lax.optimization_barrier(jnp.sum(jnp.where(onehot, lengths[None, :], 0), axis=1)).astype(jnp.int32)
    doc_end = lax.optimization_barrier(jnp.sum(jnp.where(onehot, doc_ends[None, :], 0), axis=1)).astype(jnp.int32)
    return (documents, doc_len, positions_global - doc_end + doc_len, onehot)

def block_mask(lengths, query_positions, key_positions):
    query_docs = document_info(lengths, query_positions)[0]
    key_docs = document_info(lengths, key_positions)[0]
    return (key_positions[None, :] >= 0) & (key_docs[None, :] == query_docs[:, None]) & (key_positions[None, :] <= query_positions[:, None])

def rope_tables(positions):
    half_width = HD // 2
    frequency = ROPE_BASE ** (-(jnp.arange(half_width, dtype=jnp.float32) * 2.0 / HD))
    angles = positions.astype(jnp.float32)[:, None] * frequency[None, :]
    angles = jnp.concatenate([angles, angles], axis=1)
    return (jnp.cos(angles), jnp.sin(angles))

def rotate(values, cosine_table, sine_table):
    half_width = values.shape[-1] // 2
    turned = jnp.concatenate([-values[..., half_width:], values[..., :half_width]], axis=-1)
    return values * cosine_table[:, None, :] + turned * sine_table[:, None, :]

def unrotate(gradient, cosine_table, sine_table):
    half_width = gradient.shape[-1] // 2
    scaled = gradient * sine_table[:, None, :]
    back_part = jnp.concatenate([scaled[..., half_width:], -scaled[..., :half_width]], axis=-1)
    return gradient * cosine_table[:, None, :] + back_part

def contract(left, right):
    return lax.dot_general(left, right, (((1,), (1,)), ((), ())), preferred_element_type=jnp.float32)

def attend_head(queries, key_rows, value_rows, out_grad, allowed, kept_keys):
    score_scale = HD ** (-0.5)
    scores = contract(queries, key_rows) * score_scale
    weights = jnp.where(allowed, jnp.exp(scores), 0.0)
    totals = lax.optimization_barrier(jnp.sum(weights, axis=1, keepdims=True))
    softmax = weights / totals
    prob_grad = contract(out_grad, value_rows)
    row_delta = lax.optimization_barrier(jnp.sum(softmax * prob_grad, axis=1, keepdims=True))
    score_grad = (softmax * (prob_grad - row_delta)).astype(jnp.bfloat16)
    query_grad = jnp.dot(score_grad, key_rows, preferred_element_type=jnp.float32) * score_scale
    first_kept = key_rows.shape[0] - kept_keys
    key_grad = lax.dot_general(score_grad[:, first_kept:], queries, (((0,), (0,)), ((), ())), preferred_element_type=jnp.float32) * score_scale
    value_grad = lax.dot_general(softmax[:, first_kept:].astype(jnp.bfloat16), out_grad, (((0,), (0,)), ((), ())), preferred_element_type=jnp.float32)
    return (query_grad, key_grad, value_grad, totals, row_delta)

def reference(hidden, norm_gain, w_query, w_key, w_value, upstream, cached, lengths):
    group_size = QH // KVH
    hidden_wide = hidden.astype(jnp.float32)
    inverse_scale = lax.rsqrt(lax.optimization_barrier(jnp.mean(hidden_wide * hidden_wide, axis=1, keepdims=True)) + EPSILON)
    normed = (hidden_wide * inverse_scale * norm_gain[None, :]).astype(jnp.bfloat16)
    all_positions = jnp.arange(TOKENS, dtype=jnp.int32)
    documents, doc_len, positions, onehot = document_info(lengths, all_positions)
    cosine_table, sine_table = rope_tables(positions)
    queries = rotate(jnp.dot(normed, w_query, preferred_element_type=jnp.float32).reshape(TOKENS, QH, HD), cosine_table, sine_table).astype(jnp.bfloat16)
    key_rows = rotate(jnp.dot(normed, w_key, preferred_element_type=jnp.float32).reshape(TOKENS, KVH, HD), cosine_table, sine_table).astype(jnp.bfloat16)
    value_rows = jnp.dot(normed, w_value, preferred_element_type=jnp.float32).astype(jnp.bfloat16).reshape(TOKENS, KVH, HD)
    pooled = cached[documents] / doc_len.astype(jnp.float32)[:, None]
    out_grad = (upstream.astype(jnp.float32) + pooled).astype(jnp.bfloat16).reshape(TOKENS, QH, HD)
    key_wide = jnp.pad(jnp.repeat(key_rows, group_size, axis=1), ((LONGEST, 0), (0, 0), (0, 0)))
    value_wide = jnp.pad(jnp.repeat(value_rows, group_size, axis=1), ((LONGEST, 0), (0, 0), (0, 0)))
    window = LONGEST + TOK_DEV

    def block(carry, offset):
        key_total, value_total = carry
        block_queries = jnp.transpose(lax.dynamic_slice_in_dim(queries, offset, TOK_DEV, 0), (1, 0, 2))
        block_grads = jnp.transpose(lax.dynamic_slice_in_dim(out_grad, offset, TOK_DEV, 0), (1, 0, 2))
        block_keys = jnp.transpose(lax.dynamic_slice_in_dim(key_wide, offset, window, 0), (1, 0, 2))
        block_values = jnp.transpose(lax.dynamic_slice_in_dim(value_wide, offset, window, 0), (1, 0, 2))
        query_positions = offset + jnp.arange(TOK_DEV, dtype=jnp.int32)
        key_positions = offset - LONGEST + jnp.arange(window, dtype=jnp.int32)
        allowed = block_mask(lengths, query_positions, key_positions)

        def one_head(operands):
            return attend_head(operands[0], operands[1], operands[2], operands[3], allowed, window)
        query_grad, key_grad, value_grad, totals, row_delta = lax.map(one_head, (block_queries, block_keys, block_values, block_grads))
        query_grad = jnp.transpose(query_grad, (1, 0, 2))
        key_grad = jnp.transpose(key_grad, (1, 0, 2)).reshape(window, KVH, group_size, HD).sum(axis=2)
        value_grad = jnp.transpose(value_grad, (1, 0, 2)).reshape(window, KVH, group_size, HD).sum(axis=2)
        key_total = lax.dynamic_update_slice_in_dim(key_total, lax.dynamic_slice_in_dim(key_total, offset, window, 0) + key_grad, offset, 0)
        value_total = lax.dynamic_update_slice_in_dim(value_total, lax.dynamic_slice_in_dim(value_total, offset, window, 0) + value_grad, offset, 0)
        return ((key_total, value_total), query_grad)
    offsets = jnp.arange(TOKENS // TOK_DEV, dtype=jnp.int32) * TOK_DEV
    empty = jnp.zeros((LONGEST + TOKENS, KVH, HD), jnp.float32)
    (key_total, value_total), query_grad = lax.scan(block, (empty, empty), offsets)
    query_grad = query_grad.reshape(TOKENS, QH, HD)
    query_done = unrotate(query_grad, cosine_table, sine_table).astype(jnp.bfloat16).reshape(TOKENS, QH * HD)
    key_done = unrotate(key_total[LONGEST:], cosine_table, sine_table).astype(jnp.bfloat16).reshape(TOKENS, KVH * HD)
    value_done = value_total[LONGEST:].astype(jnp.bfloat16).reshape(TOKENS, KVH * HD)
    query_width = QH * HD // N_TENSOR
    key_width = KVH * HD // N_TENSOR
    summed = jnp.zeros((TOKENS, D), jnp.float32)
    for member in range(N_TENSOR):
        query_cols = slice(member * query_width, (member + 1) * query_width)
        key_cols = slice(member * key_width, (member + 1) * key_width)
        portion = contract(query_done[:, query_cols], w_query[:, query_cols]) + contract(key_done[:, key_cols], w_key[:, key_cols]) + contract(value_done[:, key_cols], w_value[:, key_cols])
        summed = summed + lax.optimization_barrier(portion.astype(jnp.bfloat16)).astype(jnp.float32)
    projection = lax.optimization_barrier(jnp.sum(summed * norm_gain[None, :] * hidden_wide, axis=1, keepdims=True))
    grad_hidden = (inverse_scale * norm_gain[None, :] * summed - hidden_wide * (inverse_scale * inverse_scale * inverse_scale) * projection / D).astype(jnp.bfloat16)
    grad_wkey = lax.dot_general(normed, key_done, (((0,), (0,)), ((), ())), preferred_element_type=jnp.float32)
    return (grad_hidden, grad_wkey)
```

```python
from functools import partial

import jax
import jax.numpy as jnp
from jax import lax
from jax.experimental import pallas as pl
from jax.experimental.pallas import tpu as pltpu
from jax.sharding import PartitionSpec as P

D = 4096
HD = 128
HOPS = 4
LONGEST = 512


EPSILON = 1e-05
ROPE_BASE = 500000.0


def from_behind(block, axis, distance):
    devices = range(lax.axis_size(axis))
    route = [(i - distance, i) for i in devices if i - distance in devices]
    return lax.ppermute(block, axis, route)


def document_info(lengths, positions_global):
    doc_ends = jnp.cumsum(lengths)
    documents = jnp.sum((positions_global[:, None] >= doc_ends[None, :]).astype(jnp.int32), axis=1)
    doc_slots = jnp.arange(lengths.shape[0], dtype=jnp.int32)
    onehot = documents[:, None] == doc_slots[None, :]
    doc_len = jnp.sum(jnp.where(onehot, lengths[None, :], 0), axis=1)
    doc_end = jnp.sum(jnp.where(onehot, doc_ends[None, :], 0), axis=1)
    return (documents, doc_len, positions_global - doc_end + doc_len, onehot)


def block_mask(lengths, query_positions, key_positions):
    query_docs = document_info(lengths, query_positions)[0]
    key_docs = document_info(lengths, key_positions)[0]
    return (
        (key_positions[None, :] >= 0)
        & (key_docs[None, :] == query_docs[:, None])
        & (key_positions[None, :] <= query_positions[:, None])
    )


def rope_tables(positions):
    half_width = HD // 2
    frequency = ROPE_BASE ** (-(jnp.arange(half_width, dtype=jnp.float32) * 2.0 / HD))
    angles = positions.astype(jnp.float32)[:, None] * frequency[None, :]
    angles = jnp.concatenate([angles, angles], axis=1)
    return (jnp.cos(angles), jnp.sin(angles))


def rotate(values, cosine_table, sine_table):
    half_width = values.shape[-1] // 2
    turned = jnp.concatenate([-values[..., half_width:], values[..., :half_width]], axis=-1)
    return values * cosine_table[:, None, :] + turned * sine_table[:, None, :]


def unrotate(gradient, cosine_table, sine_table):
    half_width = gradient.shape[-1] // 2
    scaled = gradient * sine_table[:, None, :]
    back_part = jnp.concatenate([scaled[..., half_width:], -scaled[..., :half_width]], axis=-1)
    return gradient * cosine_table[:, None, :] + back_part


def contract(left, right):
    return lax.dot_general(
        left, right, (((1,), (1,)), ((), ())), preferred_element_type=jnp.float32
    )


def attend_head(queries, key_rows, value_rows, out_grad, allowed):
    score_scale = HD ** (-0.5)
    scores = contract(queries, key_rows) * score_scale
    weights = jnp.where(allowed, jnp.exp(scores), 0.0)
    totals = jnp.sum(weights, axis=1, keepdims=True)
    softmax = weights / totals
    prob_grad = contract(out_grad, value_rows)
    row_delta = jnp.sum(softmax * prob_grad, axis=1, keepdims=True)
    score_grad = (softmax * (prob_grad - row_delta)).astype(jnp.bfloat16)
    query_grad = jnp.dot(score_grad, key_rows, preferred_element_type=jnp.float32) * score_scale
    key_grad = (
        lax.dot_general(
            score_grad, queries, (((0,), (0,)), ((), ())), preferred_element_type=jnp.float32
        )
        * score_scale
    )
    value_grad = lax.dot_general(
        softmax.astype(jnp.bfloat16),
        out_grad,
        (((0,), (0,)), ((), ())),
        preferred_element_type=jnp.float32,
    )
    return (query_grad, key_grad, value_grad, totals, row_delta)


def fold_heads(per_head, kv_count, group_size):
    summed = per_head.reshape(kv_count, group_size, per_head.shape[1], HD).sum(axis=1)
    return jnp.transpose(summed, (1, 0, 2))


def plain_device(hidden, norm_gain, w_query, w_key, w_value, upstream, cached, lengths):
    gathered = lax.all_gather(hidden, "tensor", axis=1, tiled=True)
    row_count = gathered.shape[0]
    query_cols = w_query.shape[1]
    key_cols = w_key.shape[1]
    head_count = query_cols // HD
    kv_count = key_cols // HD
    group_size = head_count // kv_count
    hidden_wide = gathered.astype(jnp.float32)
    inverse_scale = lax.rsqrt(jnp.mean(hidden_wide * hidden_wide, axis=1, keepdims=True) + EPSILON)
    normed = (hidden_wide * inverse_scale * norm_gain[None, :]).astype(jnp.bfloat16)
    dp_index = lax.axis_index("dp")
    own_positions = dp_index * row_count + jnp.arange(row_count, dtype=jnp.int32)
    documents, doc_len, positions, onehot = document_info(lengths, own_positions)
    cosine_table, sine_table = rope_tables(positions)
    full_query, full_key, full_value = (
        lax.all_gather(w_query, "dp", axis=0, tiled=True),
        lax.all_gather(w_key, "dp", axis=0, tiled=True),
        lax.all_gather(w_value, "dp", axis=0, tiled=True),
    )
    query_proj = jnp.dot(normed, full_query, preferred_element_type=jnp.float32)
    key_proj = jnp.dot(normed, full_key, preferred_element_type=jnp.float32)
    value_proj = jnp.dot(normed, full_value, preferred_element_type=jnp.float32)
    queries = rotate(
        query_proj.reshape(row_count, head_count, HD), cosine_table, sine_table
    ).astype(jnp.bfloat16)
    key_rows = rotate(key_proj.reshape(row_count, kv_count, HD), cosine_table, sine_table).astype(
        jnp.bfloat16
    )
    value_rows = value_proj.astype(jnp.bfloat16).reshape(row_count, kv_count, HD)
    pooled = (
        jnp.dot(onehot.astype(jnp.float32), cached, precision=lax.Precision.HIGHEST)
        / doc_len.astype(jnp.float32)[:, None]
    )
    out_grad = (
        (upstream.astype(jnp.float32) + pooled)
        .astype(jnp.bfloat16)
        .reshape(row_count, head_count, HD)
    )
    key_list = []
    value_list = []
    for distance in range(HOPS, 0, -1):
        earlier_key, earlier_value = from_behind((key_rows, value_rows), "dp", distance)
        key_list.append(earlier_key)
        value_list.append(earlier_value)
    key_window = jnp.concatenate(key_list + [key_rows], axis=0)
    value_window = jnp.concatenate(value_list + [value_rows], axis=0)
    window = key_window.shape[0]
    window_positions = dp_index * row_count - HOPS * row_count + jnp.arange(window, dtype=jnp.int32)
    allowed = block_mask(lengths, own_positions, window_positions)
    head_queries = jnp.transpose(queries, (1, 0, 2))
    head_grads = jnp.transpose(out_grad, (1, 0, 2))
    head_keys = jnp.transpose(jnp.repeat(key_window, group_size, axis=1), (1, 0, 2))
    head_values = jnp.transpose(jnp.repeat(value_window, group_size, axis=1), (1, 0, 2))

    def one_head(operands):
        return attend_head(operands[0], operands[1], operands[2], operands[3], allowed)

    query_grad, key_grad, value_grad, totals, row_delta = lax.map(
        one_head, (head_queries, head_keys, head_values, head_grads)
    )
    key_sum = fold_heads(key_grad, kv_count, group_size)
    value_sum = fold_heads(value_grad, kv_count, group_size)
    own_key = key_sum[HOPS * row_count :]
    own_value = value_sum[HOPS * row_count :]
    for distance in range(1, HOPS + 1):
        lower = (HOPS - distance) * row_count
        back_key, back_value = (
            from_behind(
                key_sum[lower : lower + row_count].astype(jnp.bfloat16), "dp", -distance
            ).astype(jnp.float32),
            from_behind(
                value_sum[lower : lower + row_count].astype(jnp.bfloat16), "dp", -distance
            ).astype(jnp.float32),
        )
        own_key = own_key + back_key
        own_value = own_value + back_value
    query_done = (
        unrotate(jnp.transpose(query_grad, (1, 0, 2)), cosine_table, sine_table)
        .astype(jnp.bfloat16)
        .reshape(row_count, query_cols)
    )
    key_done = (
        unrotate(own_key, cosine_table, sine_table)
        .astype(jnp.bfloat16)
        .reshape(row_count, key_cols)
    )
    value_done = own_value.astype(jnp.bfloat16).reshape(row_count, key_cols)
    portion = (
        contract(query_done, full_query)
        + contract(key_done, full_key)
        + contract(value_done, full_value)
    )
    own_hidden = hidden.astype(jnp.float32)
    own_cols = hidden.shape[1]
    gain_offset = lax.axis_index("tensor") * own_cols
    own_gain = lax.dynamic_slice_in_dim(norm_gain, gain_offset, own_cols, 0)
    normed_grad = lax.psum_scatter(
        portion.astype(jnp.bfloat16), "tensor", scatter_dimension=1, tiled=True
    ).astype(jnp.float32)
    projection = lax.psum(
        jnp.sum(normed_grad * own_gain[None, :] * own_hidden, axis=1, keepdims=True), "tensor"
    )
    grad_hidden = (
        inverse_scale * own_gain[None, :] * normed_grad
        - own_hidden * (inverse_scale * inverse_scale * inverse_scale) * projection / D
    ).astype(jnp.bfloat16)
    grad_wkey = lax.psum_scatter(
        lax.dot_general(
            normed, key_done, (((0,), (0,)), ((), ())), preferred_element_type=jnp.float32
        ),
        "dp",
        scatter_dimension=0,
        tiled=True,
    )
    return (grad_hidden, grad_wkey)


def norm_kernel(where, near_ref, far_ref, gain_ref, *outs):
    pieces, inv_ref = outs[:-1], outs[-1]
    ring, group, tensor = where[0], where[1], where[2]
    ring_size = len(pieces)
    members = where.shape[0] - 3
    step = pieces[0].shape[1] // members

    def write(ref):
        total = jnp.zeros((ref.shape[2], 1), jnp.float32)
        for half in range(2):
            wide = ref[0, half].astype(jnp.float32)
            total = total + jnp.sum(wide * wide, axis=1, keepdims=True)
        inverse = lax.rsqrt(total / D + EPSILON)
        inv_ref[...] = jnp.broadcast_to(inverse, inv_ref.shape)
        planes_per_half = ring_size // 2
        for s in range(ring_size):
            plane = lax.rem(ring - s + ring_size, ring_size)
            half = lax.rem(plane // planes_per_half + tensor, 2)
            for d in range(members):
                inner = lax.rem(plane, planes_per_half) * (members * step) + where[3 + d] * step
                inner = pl.multiple_of(inner, step)
                outer = pl.multiple_of((plane * members + where[3 + d]) * step, step)
                wide = ref[0, half, :, pl.ds(inner, step)].astype(jnp.float32)
                scaled = wide * inverse * gain_ref[:, pl.ds(outer, step)]
                pieces[s][:, d * step : (d + 1) * step] = scaled.astype(jnp.bfloat16)

    @pl.when(pl.program_id(1) == 0)
    def _():
        write(near_ref)

    @pl.when(pl.program_id(1) == 1)
    def _():
        write(far_ref)


def norm_pieces(where, near, far, gain, ring_size):
    rows, half = near.shape[2], near.shape[3]
    members = where.shape[0] - 3
    tokens = members * rows
    width = 2 * half // ring_size
    spec = pl.BlockSpec((1, 2, rows, half), lambda u, v, w: (u, 0, 0, 0))

    def out_row(u, v, w):
        return (w[3 + 2 * u + v], 0)

    return pl.pallas_call(
        norm_kernel,
        grid_spec=pltpu.PrefetchScalarGridSpec(
            num_scalar_prefetch=1,
            grid=(2, 2),
            in_specs=[spec, spec, pl.BlockSpec((1, 2 * half), lambda u, v, w: (0, 0))],
            out_specs=[pl.BlockSpec((rows, width), out_row)] * ring_size
            + [pl.BlockSpec((rows, 128), out_row)],
        ),
        out_shape=[jax.ShapeDtypeStruct((tokens, width), jnp.bfloat16)] * ring_size
        + [jax.ShapeDtypeStruct((tokens, 128), jnp.float32)],
        cost_estimate=pl.CostEstimate(
            flops=8 * tokens * 2 * half, bytes_accessed=8 * tokens * half, transcendentals=tokens
        ),
    )(where, near, far, gain)


def attend_kernel(heads, rows, q_ref, g_ref, k_ref, kt_ref, v_ref, cos_ref, sin_ref, low_ref,
                  dq_ref, dkv_ref, qs, gs, ps, ds):
    scale = HD ** (-0.5)
    window = ps.shape[0]

    @pl.when(pl.program_id(0) == 0)
    def _():
        dkv_ref[...] = jnp.zeros_like(dkv_ref)

    base = pl.multiple_of(pl.program_id(0) * rows, rows)
    cosine, sine = cos_ref[...], sin_ref[...]
    for h in range(heads):
        lanes = slice(h * HD, (h + 1) * HD)
        there = slice(h * rows, (h + 1) * rows)
        u = q_ref[:, lanes]
        qs[there, :] = (u * cosine + pltpu.roll(u, HD // 2, 1) * sine).astype(jnp.bfloat16)
        gs[there, :] = g_ref[:, lanes]
    keys = k_ref[pl.ds(base, window), :]
    values = v_ref[pl.ds(base, window), :]
    scores = contract(keys, qs[...]) * scale
    prob_grads = contract(values, gs[...])
    key_at = lax.broadcasted_iota(jnp.int32, (window, rows), 0)
    query_at = lax.broadcasted_iota(jnp.int32, (window, rows), 1) + (window - rows)
    allowed = (key_at >= low_ref[...] - base) & (key_at <= query_at)
    for h in range(heads):
        there = slice(h * rows, (h + 1) * rows)
        weights = jnp.where(allowed, jnp.exp(scores[:, there]), 0.0)
        softmax = weights * (1.0 / jnp.sum(weights, axis=0, keepdims=True))
        prob_grad = prob_grads[:, there]
        row_delta = jnp.sum(softmax * prob_grad, axis=0, keepdims=True)
        ps[:, there] = softmax.astype(jnp.bfloat16)
        ds[:, there] = (softmax * (prob_grad - row_delta)).astype(jnp.bfloat16)
    dkv_ref[pl.ds(base, window), :HD] += (
        jnp.dot(ds[...], qs[...], preferred_element_type=jnp.float32) * scale
    )
    dkv_ref[pl.ds(base, window), HD:] += jnp.dot(
        ps[...], gs[...], preferred_element_type=jnp.float32
    )
    turned = jnp.dot(
        kt_ref[:, pl.ds(base, window)], ds[...], preferred_element_type=jnp.float32
    )
    for h in range(heads):
        there = slice(h * rows, (h + 1) * rows)
        grad = turned[:, there].T * scale
        back = grad * cosine - pltpu.roll(grad, HD // 2, 1) * sine
        dq_ref[:, h * HD : (h + 1) * HD] = back.astype(jnp.bfloat16)


def attend(q_proj, grads, keys, keys_turned, values, cosine, sine, low):
    tokens, width = q_proj.shape
    heads, rows = width // HD, 128
    total = keys.shape[0]
    window = total - tokens + rows
    whole = lambda a: pl.BlockSpec(a.shape, lambda i: (0, 0))
    by_rows = lambda w: pl.BlockSpec((rows, w), lambda i: (i, 0))
    return pl.pallas_call(
        partial(attend_kernel, heads, rows),
        grid=(tokens // rows,),
        in_specs=[by_rows(width), by_rows(width), whole(keys), whole(keys_turned), whole(values),
                  by_rows(HD), by_rows(HD), pl.BlockSpec((1, rows), lambda i: (0, i))],
        out_specs=[by_rows(width), pl.BlockSpec((total, 2 * HD), lambda i: (0, 0))],
        out_shape=[jax.ShapeDtypeStruct((tokens, width), jnp.bfloat16),
                   jax.ShapeDtypeStruct((total, 2 * HD), jnp.float32)],
        scratch_shapes=[pltpu.VMEM((heads * rows, HD), jnp.bfloat16)] * 2
        + [pltpu.VMEM((window, heads * rows), jnp.bfloat16)] * 2,
        cost_estimate=pl.CostEstimate(
            flops=10 * tokens * window * width, bytes_accessed=12 * tokens * width,
            transcendentals=tokens * window * heads,
        ),
    )(q_proj, grads, keys, keys_turned, values, cosine, sine, low)


def spread_kernel(chunks, ring_size, where, *refs):
    grads = refs[:chunks]
    weights = refs[chunks : chunks + chunks * ring_size]
    out_ref = refs[-1]
    ring, tensor = where[0], where[2]
    members = where.shape[0] - 3
    step = weights[0].shape[0] // members
    rows = out_ref.shape[3]
    planes_per_half = ring_size // 2
    s = pl.program_id(0)
    plane = lax.rem(ring - s + ring_size, ring_size)
    half = lax.rem(plane // planes_per_half + tensor, 2)
    for piece in range(ring_size):

        @pl.when(s == piece)
        def _():
            for d in range(members):
                inner = lax.rem(plane, planes_per_half) * (members * step) + where[3 + d] * step
                inner = pl.multiple_of(inner, step)
                total = None
                for c in range(chunks):
                    term = contract(
                        grads[c][...], weights[c * ring_size + piece][d * step : (d + 1) * step, :]
                    )
                    total = term if total is None else total + term
                total = total.astype(jnp.bfloat16)
                for owner in range(members):
                    for v in range(2):
                        for u in range(members // 2):

                            @pl.when(where[3 + owner] == 2 * u + v)
                            def _():
                                out_ref[v, u, half, :, pl.ds(inner, step)] = total[
                                    owner * rows : (owner + 1) * rows, :
                                ]


def spread(where, grads, weights, ring_size):
    tokens = grads[0].shape[0]
    members = where.shape[0] - 3
    rows = tokens // members
    width = weights[0].shape[0] * ring_size
    whole = lambda a: pl.BlockSpec(a.shape, lambda i, w: (0, 0))
    shape = (2, members // 2, 2, rows, width // 2)
    return pl.pallas_call(
        partial(spread_kernel, len(grads), ring_size),
        grid_spec=pltpu.PrefetchScalarGridSpec(
            num_scalar_prefetch=1,
            grid=(ring_size,),
            in_specs=[whole(a) for a in grads] + [whole(a) for a in weights],
            out_specs=pl.BlockSpec(shape, lambda i, w: (0, 0, 0, 0, 0)),
        ),
        out_shape=jax.ShapeDtypeStruct(shape, jnp.bfloat16),
        cost_estimate=pl.CostEstimate(
            flops=2 * tokens * width * sum(a.shape[1] for a in grads),
            bytes_accessed=4 * tokens * width,
            transcendentals=0,
        ),
    )(where, *grads, *weights)


def grouped_device(hidden, norm_gain, w_query, w_key, w_value, upstream, cached, lengths):
    rows, half = hidden.shape
    kv_count = w_key.shape[1] // HD
    query_width = w_query.shape[1] // kv_count
    members = kv_count
    devices, tensors = lax.axis_size("dp"), lax.axis_size("tensor")
    ring_size = devices // members
    tokens = members * rows
    weight_rows = w_key.shape[0]
    me, tensor = lax.axis_index("dp"), lax.axis_index("tensor")
    ring, group = me // members, me % members
    partners = [jnp.bitwise_xor(group, d) for d in range(members)]
    where = jnp.stack([ring, group, tensor] + partners).astype(jnp.int32)

    def to_partner(block, d):
        return lax.ppermute(block, "dp", [(i, i ^ d) for i in range(devices)])

    def to_side(block):
        return lax.ppermute(block, "tensor", [(i, i ^ 1) for i in range(tensors)])

    def to_corner(block, d):
        route = [(i * 2 + t, (i ^ d) * 2 + (t ^ 1)) for i in range(devices) for t in range(2)]
        return lax.ppermute(block, ("dp", "tensor"), route)

    def along(block, distance):
        return lax.ppermute(
            block, "dp", [(i, (i + distance * members) % devices) for i in range(devices)]
        )

    def columns(array, owner, width):
        return lax.dynamic_slice_in_dim(array, owner * width, width, 1)

    def pack_kv(owner):
        return jnp.concatenate([columns(w_key, owner, HD), columns(w_value, owner, HD)], axis=1)

    def pack_q(owner):
        return jnp.concatenate(
            [columns(w_query, owner, query_width), columns(upstream, owner, query_width)], axis=0
        )

    kv_parts = [pack_kv(group)] + [to_partner(pack_kv(partners[d]), d) for d in range(1, members)]
    q_parts = [pack_q(group)] + [to_partner(pack_q(partners[d]), d) for d in range(1, members)]
    kv_own = jnp.concatenate(kv_parts, axis=0)
    q_own = jnp.concatenate([p[:weight_rows] for p in q_parts], axis=0)
    chunk_width = 2 * HD
    q_chunks = query_width // chunk_width

    across = to_partner(hidden, 2)
    near = jnp.stack(
        [jnp.stack([hidden, to_side(hidden)]), jnp.stack([across, to_corner(hidden, 2)])]
    )
    far = to_partner(near, 1)
    *normed, inverse = norm_pieces(where, near, far, norm_gain[None, :], ring_size)

    def circulate(own):
        pieces = [own]
        for _ in range(ring_size - 1):
            pieces.append(along(pieces[-1], 1))
        return pieces

    def project(pieces):
        total = None
        for s in range(ring_size):
            term = jnp.dot(normed[s], pieces[s], preferred_element_type=jnp.float32)
            total = term if total is None else total + term
        return total

    first = ring * tokens
    token_positions = first + jnp.arange(tokens, dtype=jnp.int32)
    _, doc_len, positions, onehot = document_info(lengths, token_positions)
    cosine, sine = rope_tables(positions)
    sign = jnp.where(jnp.arange(HD) < HD // 2, -1.0, 1.0).astype(jnp.float32)
    sine = sine * sign[None, :]
    low = (token_positions - positions - first + LONGEST)[None, :]

    def place(parts):
        stacked = jnp.stack(parts)
        return [
            lax.dynamic_index_in_dim(stacked, jnp.bitwise_xor(group, o), 0, keepdims=False)
            for o in range(members)
        ]

    up_own = jnp.concatenate(place([p[weight_rows:] for p in q_parts]), axis=0)
    pooled = (
        jnp.dot(
            onehot.astype(jnp.float32),
            columns(cached, group, query_width),
            precision=lax.Precision.HIGHEST,
        )
        / doc_len.astype(jnp.float32)[:, None]
    )
    out_grad = (up_own.astype(jnp.float32) + pooled).astype(jnp.bfloat16)

    kv_pieces = circulate(kv_own)
    q_pieces = [
        circulate(q_own[:, c * chunk_width : (c + 1) * chunk_width]) for c in range(q_chunks)
    ]
    kv_proj = project(kv_pieces)
    key_proj = kv_proj[:, :HD]
    key_own = key_proj * cosine + jnp.roll(key_proj, HD // 2, axis=1) * sine
    kv_rows = jnp.concatenate([key_own, kv_proj[:, HD:]], axis=1).astype(jnp.bfloat16)
    halo = lax.ppermute(kv_rows, "dp", [(i, i + members) for i in range(devices - members)])
    kv_all = jnp.concatenate([halo, kv_rows], axis=0)
    keys, values = kv_all[:, :HD], kv_all[:, HD:]
    keys_turned = keys.T
    query_dones, kv_sum = [], None
    for c in range(q_chunks):
        query_done, kv_grad = attend(
            project(q_pieces[c]),
            out_grad[:, c * chunk_width : (c + 1) * chunk_width],
            keys, keys_turned, values, cosine, sine, low,
        )
        query_dones.append(query_done)
        kv_sum = kv_grad if kv_sum is None else kv_sum + kv_grad
    back = lax.ppermute(
        kv_sum[:LONGEST].astype(jnp.bfloat16),
        "dp",
        [(i + members, i) for i in range(devices - members)],
    )
    kv_total = kv_sum[LONGEST:] + back.astype(jnp.float32)
    key_grad = kv_total[:, :HD]
    key_done = (key_grad * cosine - jnp.roll(key_grad, HD // 2, axis=1) * sine).astype(jnp.bfloat16)
    kv_done = jnp.concatenate([key_done, kv_total[:, HD:].astype(jnp.bfloat16)], axis=1)

    key_dones = jnp.concatenate(
        place([key_done] + [to_partner(key_done, d) for d in range(1, members)]), axis=1
    )
    grad_wkey = None
    for s in range(ring_size):
        term = lax.dot_general(
            normed[s][:, :weight_rows],
            key_dones,
            (((0,), (0,)), ((), ())),
            preferred_element_type=jnp.float32,
        )
        if s:
            term = along(term.astype(jnp.bfloat16), -s).astype(jnp.float32)
        grad_wkey = term if grad_wkey is None else grad_wkey + term

    weights = [piece for pieces in q_pieces + [kv_pieces] for piece in pieces]
    owned = spread(where, query_dones + [kv_done], weights, ring_size)
    wide = lambda a: a.astype(jnp.float32)
    narrow = lambda a: a.astype(jnp.bfloat16)
    both = narrow(wide(owned[0]) + wide(to_partner(owned[1], 1)))
    cut = half // 2
    left = wide(both[0, :, :, :cut]) + wide(to_partner(both[1, :, :, :cut], 2))
    right = wide(both[:, 0, :, cut:]) + wide(to_side(both[:, 1, :, cut:]))
    left_sum = left[0] + wide(to_side(narrow(left[1])))
    right_sum = right[0] + wide(to_partner(narrow(right[1]), 2))
    normed_grad = jnp.concatenate([left_sum, right_sum], axis=1)
    own_hidden = wide(hidden)
    own_gain = lax.dynamic_slice_in_dim(norm_gain, tensor * half, half, 0)
    own_inverse = lax.dynamic_slice_in_dim(inverse, group * rows, rows, 0)[:, :1]
    part = jnp.sum(normed_grad * own_gain[None, :] * own_hidden, axis=1)[None, :]
    projection = (part + to_side(part)).reshape(rows, 1)
    grad_hidden = (
        own_inverse * own_gain[None, :] * normed_grad
        - own_hidden * (own_inverse * own_inverse * own_inverse) * projection / D
    ).astype(jnp.bfloat16)
    return (grad_hidden, grad_wkey)


def per_device(hidden, norm_gain, w_query, w_key, w_value, upstream, cached, lengths):
    members = w_key.shape[1] // HD
    devices = lax.axis_size("dp")
    grouped = (
        lax.axis_size("tensor") == 2
        and members == 4
        and devices == 4 * members
        and members * hidden.shape[0] == LONGEST
    )
    run = grouped_device if grouped else plain_device
    return run(hidden, norm_gain, w_query, w_key, w_value, upstream, cached, lengths)


def solution(mesh):
    placed = (
        P("dp", "tensor"),
        P(),
        P("dp", "tensor"),
        P("dp", "tensor"),
        P("dp", "tensor"),
        P("dp", "tensor"),
        P(None, "tensor"),
        P(),
    )
    return jax.shard_map(
        per_device,
        mesh=mesh,
        in_specs=placed,
        out_specs=(P("dp", "tensor"), P("dp", "tensor")),
        check_vma=False,
    )
```

```python
from functools import partial

import jax
import jax.numpy as jnp
from jax import lax
from jax.experimental import pallas as pl
from jax.experimental.pallas import tpu as pltpu
from jax.sharding import PartitionSpec as P


D = 4096
HD = 128
HOPS = 4
LONGEST = 512


EPSILON = 1e-05
ROPE_BASE = 500000.0


def from_behind(block, axis, distance):
    devices = range(lax.axis_size(axis))
    route = [(i - distance, i) for i in devices if i - distance in devices]
    return lax.ppermute(block, axis, route)


def document_info(lengths, positions_global):
    doc_ends = jnp.cumsum(lengths)
    documents = jnp.sum((positions_global[:, None] >= doc_ends[None, :]).astype(jnp.int32), axis=1)
    doc_slots = jnp.arange(lengths.shape[0], dtype=jnp.int32)
    onehot = documents[:, None] == doc_slots[None, :]
    doc_len = jnp.sum(jnp.where(onehot, lengths[None, :], 0), axis=1)
    doc_end = jnp.sum(jnp.where(onehot, doc_ends[None, :], 0), axis=1)
    return (documents, doc_len, positions_global - doc_end + doc_len, onehot)


def block_mask(lengths, query_positions, key_positions):
    query_docs = document_info(lengths, query_positions)[0]
    key_docs = document_info(lengths, key_positions)[0]
    return (
        (key_positions[None, :] >= 0)
        & (key_docs[None, :] == query_docs[:, None])
        & (key_positions[None, :] <= query_positions[:, None])
    )


def rope_tables(positions):
    half_width = HD // 2
    frequency = ROPE_BASE ** (-(jnp.arange(half_width, dtype=jnp.float32) * 2.0 / HD))
    angles = positions.astype(jnp.float32)[:, None] * frequency[None, :]
    angles = jnp.concatenate([angles, angles], axis=1)
    return (jnp.cos(angles), jnp.sin(angles))


def rotate(values, cosine_table, sine_table):
    half_width = values.shape[-1] // 2
    turned = jnp.concatenate([-values[..., half_width:], values[..., :half_width]], axis=-1)
    return values * cosine_table[:, None, :] + turned * sine_table[:, None, :]


def unrotate(gradient, cosine_table, sine_table):
    half_width = gradient.shape[-1] // 2
    scaled = gradient * sine_table[:, None, :]
    back_part = jnp.concatenate([scaled[..., half_width:], -scaled[..., :half_width]], axis=-1)
    return gradient * cosine_table[:, None, :] + back_part


def contract(left, right):
    return lax.dot_general(
        left, right, (((1,), (1,)), ((), ())), preferred_element_type=jnp.float32
    )


def attend_head(queries, key_rows, value_rows, out_grad, allowed):
    score_scale = HD ** (-0.5)
    scores = contract(queries, key_rows) * score_scale
    weights = jnp.where(allowed, jnp.exp(scores), 0.0)
    totals = jnp.sum(weights, axis=1, keepdims=True)
    softmax = weights / totals
    prob_grad = contract(out_grad, value_rows)
    row_delta = jnp.sum(softmax * prob_grad, axis=1, keepdims=True)
    score_grad = (softmax * (prob_grad - row_delta)).astype(jnp.bfloat16)
    query_grad = jnp.dot(score_grad, key_rows, preferred_element_type=jnp.float32) * score_scale
    key_grad = (
        lax.dot_general(
            score_grad, queries, (((0,), (0,)), ((), ())), preferred_element_type=jnp.float32
        )
        * score_scale
    )
    value_grad = lax.dot_general(
        softmax.astype(jnp.bfloat16),
        out_grad,
        (((0,), (0,)), ((), ())),
        preferred_element_type=jnp.float32,
    )
    return (query_grad, key_grad, value_grad, totals, row_delta)


def fold_heads(per_head, kv_count, group_size):
    summed = per_head.reshape(kv_count, group_size, per_head.shape[1], HD).sum(axis=1)
    return jnp.transpose(summed, (1, 0, 2))


def plain_device(hidden, norm_gain, w_query, w_key, w_value, upstream, cached, lengths):
    gathered = lax.all_gather(hidden, "tensor", axis=1, tiled=True)
    row_count = gathered.shape[0]
    query_cols = w_query.shape[1]
    key_cols = w_key.shape[1]
    head_count = query_cols // HD
    kv_count = key_cols // HD
    group_size = head_count // kv_count
    hidden_wide = gathered.astype(jnp.float32)
    inverse_scale = lax.rsqrt(jnp.mean(hidden_wide * hidden_wide, axis=1, keepdims=True) + EPSILON)
    normed = (hidden_wide * inverse_scale * norm_gain[None, :]).astype(jnp.bfloat16)
    dp_index = lax.axis_index("dp")
    own_positions = dp_index * row_count + jnp.arange(row_count, dtype=jnp.int32)
    _, doc_len, positions, onehot = document_info(lengths, own_positions)
    cosine_table, sine_table = rope_tables(positions)
    full_query, full_key, full_value = (
        lax.all_gather(w_query, "dp", axis=0, tiled=True),
        lax.all_gather(w_key, "dp", axis=0, tiled=True),
        lax.all_gather(w_value, "dp", axis=0, tiled=True),
    )
    query_proj = jnp.dot(normed, full_query, preferred_element_type=jnp.float32)
    key_proj = jnp.dot(normed, full_key, preferred_element_type=jnp.float32)
    value_proj = jnp.dot(normed, full_value, preferred_element_type=jnp.float32)
    queries = rotate(
        query_proj.reshape(row_count, head_count, HD), cosine_table, sine_table
    ).astype(jnp.bfloat16)
    key_rows = rotate(key_proj.reshape(row_count, kv_count, HD), cosine_table, sine_table).astype(
        jnp.bfloat16
    )
    value_rows = value_proj.astype(jnp.bfloat16).reshape(row_count, kv_count, HD)
    pooled = (
        jnp.dot(onehot.astype(jnp.float32), cached, precision=lax.Precision.HIGHEST)
        / doc_len.astype(jnp.float32)[:, None]
    )
    out_grad = (
        (upstream.astype(jnp.float32) + pooled)
        .astype(jnp.bfloat16)
        .reshape(row_count, head_count, HD)
    )
    key_list = []
    value_list = []
    for distance in range(HOPS, 0, -1):
        earlier_key, earlier_value = from_behind((key_rows, value_rows), "dp", distance)
        key_list.append(earlier_key)
        value_list.append(earlier_value)
    key_window = jnp.concatenate(key_list + [key_rows], axis=0)
    value_window = jnp.concatenate(value_list + [value_rows], axis=0)
    window = key_window.shape[0]
    window_positions = dp_index * row_count - HOPS * row_count + jnp.arange(window, dtype=jnp.int32)
    allowed = block_mask(lengths, own_positions, window_positions)
    head_queries = jnp.transpose(queries, (1, 0, 2))
    head_grads = jnp.transpose(out_grad, (1, 0, 2))
    head_keys = jnp.transpose(jnp.repeat(key_window, group_size, axis=1), (1, 0, 2))
    head_values = jnp.transpose(jnp.repeat(value_window, group_size, axis=1), (1, 0, 2))

    def one_head(operands):
        return attend_head(operands[0], operands[1], operands[2], operands[3], allowed)

    query_grad, key_grad, value_grad, _, _ = lax.map(
        one_head, (head_queries, head_keys, head_values, head_grads)
    )
    key_sum = fold_heads(key_grad, kv_count, group_size)
    value_sum = fold_heads(value_grad, kv_count, group_size)
    own_key = key_sum[HOPS * row_count :]
    own_value = value_sum[HOPS * row_count :]
    for distance in range(1, HOPS + 1):
        lower = (HOPS - distance) * row_count
        back_key, back_value = (
            from_behind(
                key_sum[lower : lower + row_count].astype(jnp.bfloat16), "dp", -distance
            ).astype(jnp.float32),
            from_behind(
                value_sum[lower : lower + row_count].astype(jnp.bfloat16), "dp", -distance
            ).astype(jnp.float32),
        )
        own_key = own_key + back_key
        own_value = own_value + back_value
    query_done = (
        unrotate(jnp.transpose(query_grad, (1, 0, 2)), cosine_table, sine_table)
        .astype(jnp.bfloat16)
        .reshape(row_count, query_cols)
    )
    key_done = (
        unrotate(own_key, cosine_table, sine_table)
        .astype(jnp.bfloat16)
        .reshape(row_count, key_cols)
    )
    value_done = own_value.astype(jnp.bfloat16).reshape(row_count, key_cols)
    portion = (
        contract(query_done, full_query)
        + contract(key_done, full_key)
        + contract(value_done, full_value)
    )
    own_hidden = hidden.astype(jnp.float32)
    own_cols = hidden.shape[1]
    gain_offset = lax.axis_index("tensor") * own_cols
    own_gain = lax.dynamic_slice_in_dim(norm_gain, gain_offset, own_cols, 0)
    normed_grad = lax.psum_scatter(
        portion.astype(jnp.bfloat16), "tensor", scatter_dimension=1, tiled=True
    ).astype(jnp.float32)
    projection = lax.psum(
        jnp.sum(normed_grad * own_gain[None, :] * own_hidden, axis=1, keepdims=True), "tensor"
    )
    grad_hidden = (
        inverse_scale * own_gain[None, :] * normed_grad
        - own_hidden * (inverse_scale * inverse_scale * inverse_scale) * projection / D
    ).astype(jnp.bfloat16)
    grad_wkey = lax.psum_scatter(
        lax.dot_general(
            normed, key_done, (((0,), (0,)), ((), ())), preferred_element_type=jnp.float32
        ),
        "dp",
        scatter_dimension=0,
        tiled=True,
    )
    return (grad_hidden, grad_wkey)


def after(array, *others):
    return lax.optimization_barrier((array, *others))[0]


def norm_kernel(where, near_ref, far_ref, gain_ref, *outs):
    pieces, inv_ref = outs[:-1], outs[-1]
    ring, tensor = where[0], where[2]
    ring_size = len(pieces)
    members = where.shape[0] - 3
    step = pieces[0].shape[1] // members

    def write(ref):
        total = jnp.zeros((ref.shape[2], 1), jnp.float32)
        for half in range(2):
            wide = ref[0, half].astype(jnp.float32)
            total = total + jnp.sum(wide * wide, axis=1, keepdims=True)
        inverse = lax.rsqrt(total / D + EPSILON)
        inv_ref[...] = jnp.broadcast_to(inverse, inv_ref.shape)
        planes_per_half = ring_size // 2
        for s in range(ring_size):
            plane = lax.rem(ring - s + ring_size, ring_size)
            half = lax.rem(plane // planes_per_half + tensor, 2)
            for d in range(members):
                inner = lax.rem(plane, planes_per_half) * (members * step) + where[3 + d] * step
                inner = pl.multiple_of(inner, step)
                outer = pl.multiple_of((plane * members + where[3 + d]) * step, step)
                wide = ref[0, half, :, pl.ds(inner, step)].astype(jnp.float32)
                scaled = wide * inverse * gain_ref[:, pl.ds(outer, step)]
                pieces[s][:, d * step : (d + 1) * step] = scaled.astype(jnp.bfloat16)

    @pl.when(pl.program_id(1) == 0)
    def _():
        write(near_ref)

    @pl.when(pl.program_id(1) == 1)
    def _():
        write(far_ref)


def norm_pieces(where, near, far, gain, ring_size):
    rows, half = near.shape[2], near.shape[3]
    members = where.shape[0] - 3
    tokens = members * rows
    width = 2 * half // ring_size
    spec = pl.BlockSpec((1, 2, rows, half), lambda u, v, w: (u, 0, 0, 0))

    def out_row(u, v, w):
        return (w[3 + 2 * u + v], 0)

    return pl.pallas_call(
        norm_kernel,
        grid_spec=pltpu.PrefetchScalarGridSpec(
            num_scalar_prefetch=1,
            grid=(2, 2),
            in_specs=[spec, spec, pl.BlockSpec((1, 2 * half), lambda u, v, w: (0, 0))],
            out_specs=[pl.BlockSpec((rows, width), out_row)] * ring_size
            + [pl.BlockSpec((rows, 128), out_row)],
        ),
        out_shape=[jax.ShapeDtypeStruct((tokens, width), jnp.bfloat16)] * ring_size
        + [jax.ShapeDtypeStruct((tokens, 128), jnp.float32)],
        cost_estimate=pl.CostEstimate(
            flops=8 * tokens * 2 * half, bytes_accessed=8 * tokens * half, transcendentals=tokens
        ),
    )(where, near, far, gain)


def attend_kernel(heads, rows, first, q_ref, g_ref, k_ref, kt_ref, v_ref, cos_ref, sin_ref, low_ref,
                  *refs):
    before = None if first else refs[0]
    dq_ref, halo_ref, dkv_ref, qs, gs, ps, ds = refs[0 if first else 1 :]
    scale = HD ** (-0.5)
    window = ps.shape[0]

    @pl.when(pl.program_id(0) == 0)
    def _():
        dkv_ref[...] = jnp.zeros_like(dkv_ref) if first else before[...]

    base = pl.multiple_of(pl.program_id(0) * rows, rows)
    cosine, sine = cos_ref[...], sin_ref[...]
    for h in range(heads):
        lanes = slice(h * HD, (h + 1) * HD)
        there = slice(h * rows, (h + 1) * rows)
        u = q_ref[:, lanes]
        qs[there, :] = (u * cosine + pltpu.roll(u, HD // 2, 1) * sine).astype(jnp.bfloat16)
        gs[there, :] = g_ref[:, lanes]
    keys = k_ref[pl.ds(base, window), :]
    values = v_ref[pl.ds(base, window), :]
    scores = contract(keys, qs[...]) * scale
    prob_grads = contract(values, gs[...])
    key_at = lax.broadcasted_iota(jnp.int32, (window, rows), 0)
    query_at = lax.broadcasted_iota(jnp.int32, (window, rows), 1) + (window - rows)
    allowed = (key_at >= low_ref[...] - base) & (key_at <= query_at)
    for h in range(heads):
        there = slice(h * rows, (h + 1) * rows)
        weights = jnp.where(allowed, jnp.exp(scores[:, there]), 0.0)
        softmax = weights * (1.0 / jnp.sum(weights, axis=0, keepdims=True))
        prob_grad = prob_grads[:, there]
        row_delta = jnp.sum(softmax * prob_grad, axis=0, keepdims=True)
        ps[:, there] = softmax.astype(jnp.bfloat16)
        ds[:, there] = (softmax * (prob_grad - row_delta)).astype(jnp.bfloat16)
    dkv_ref[pl.ds(base, window), :HD] += (
        jnp.dot(ds[...], qs[...], preferred_element_type=jnp.float32) * scale
    )
    dkv_ref[pl.ds(base, window), HD:] += jnp.dot(
        ps[...], gs[...], preferred_element_type=jnp.float32
    )
    turned = jnp.dot(
        kt_ref[:, pl.ds(base, window)], ds[...], preferred_element_type=jnp.float32
    )
    for h in range(heads):
        there = slice(h * rows, (h + 1) * rows)
        grad = turned[:, there].T * scale
        back = grad * cosine - pltpu.roll(grad, HD // 2, 1) * sine
        dq_ref[:, h * HD : (h + 1) * HD] = back.astype(jnp.bfloat16)

    @pl.when(pl.program_id(0) == pl.num_programs(0) - 1)
    def _():
        halo_ref[...] = dkv_ref[: halo_ref.shape[0], :].astype(jnp.bfloat16)


def attend(q_proj, grads, keys, keys_turned, values, cosine, sine, low, before=None):
    tokens, width = q_proj.shape
    heads, rows = width // HD, 128
    total = keys.shape[0]
    window = total - tokens + rows
    whole = lambda a: pl.BlockSpec(a.shape, lambda i: (0, 0))
    by_rows = lambda w: pl.BlockSpec((rows, w), lambda i: (i, 0))
    fixed = lambda n: pl.BlockSpec((n, 2 * HD), lambda i: (0, 0))
    extra = [] if before is None else [before]
    return pl.pallas_call(
        partial(attend_kernel, heads, rows, before is None),
        grid=(tokens // rows,),
        in_specs=[by_rows(width), by_rows(width), whole(keys), whole(keys_turned), whole(values),
                  by_rows(HD), by_rows(HD), pl.BlockSpec((1, rows), lambda i: (0, i))]
        + [fixed(total) for _ in extra],
        out_specs=[by_rows(width), fixed(total - tokens), fixed(total)],
        out_shape=[jax.ShapeDtypeStruct((tokens, width), jnp.bfloat16),
                   jax.ShapeDtypeStruct((total - tokens, 2 * HD), jnp.bfloat16),
                   jax.ShapeDtypeStruct((total, 2 * HD), jnp.float32)],
        scratch_shapes=[pltpu.VMEM((heads * rows, HD), jnp.bfloat16)] * 2
        + [pltpu.VMEM((window, heads * rows), jnp.bfloat16)] * 2,
        cost_estimate=pl.CostEstimate(
            flops=10 * tokens * window * width, bytes_accessed=12 * tokens * width,
            transcendentals=tokens * window * heads,
        ),
    )(q_proj, grads, keys, keys_turned, values, cosine, sine, low, *extra)


def spread_kernel(counts, ring_size, where, *refs):
    grads, weights = refs[: counts[0]], refs[counts[0] : counts[0] + counts[1] * ring_size]
    keep_ref, send_ref, wide, held, arrived = refs[counts[0] + counts[1] * ring_size :]
    members = where.shape[0] - 3
    step = held.shape[1] // members
    rows = keep_ref.shape[2]
    s = pl.program_id(0)

    def copy(source, piece, c):
        width = source.shape[1]
        return pltpu.make_async_copy(
            source, held.at[piece, :, pl.ds(c * width, width)], arrived.at[piece, c]
        )

    @pl.when(s == 0)
    def _():
        for piece in range(ring_size):
            for c in range(counts[1]):
                copy(weights[c * ring_size + piece], piece, c).start()
        for block in range(members):
            partner = (block % (members // 2)) * 2 + block // (members // 2)
            source = pl.multiple_of(where[3 + partner] * rows, rows)
            at = 0
            for grad in grads:
                wide[block * rows : (block + 1) * rows, at : at + grad.shape[1]] = grad[
                    pl.ds(source, rows), :
                ]
                at += grad.shape[1]

    for c in range(counts[1]):
        copy(weights[c * ring_size], s, c).wait()
    for owner in range(members):
        source = pl.multiple_of(where[3 + owner] * step, step)
        total = contract(wide[...], held[s, pl.ds(source, step), :]).astype(jnp.bfloat16)
        columns = slice(owner * step, (owner + 1) * step)
        for u in range(members // 2):
            keep_ref[u, 0, :, columns] = total[u * rows : (u + 1) * rows, :]
            lower = (members // 2 + u) * rows
            send_ref[u, 0, :, columns] = total[lower : lower + rows, :]


def spread(where, grads, weights, ring_size):
    tokens = grads[0].shape[0]
    members = where.shape[0] - 3
    rows = tokens // members
    depth = sum(a.shape[1] for a in grads)
    width = weights[0].shape[0] * ring_size
    planes_per_half = ring_size // 2
    whole = lambda a: pl.BlockSpec(a.shape, lambda i, w: (0, 0))

    def out_at(s, w):
        plane = lax.rem(w[0] - s + ring_size, ring_size)
        half = lax.rem(plane // planes_per_half + w[2], 2)
        return (0, half, 0, lax.rem(plane, planes_per_half))

    shape = (members // 2, 2, rows, width // 2)
    return pl.pallas_call(
        partial(spread_kernel, (len(grads), len(weights) // ring_size), ring_size),
        grid_spec=pltpu.PrefetchScalarGridSpec(
            num_scalar_prefetch=1,
            grid=(ring_size,),
            in_specs=[whole(a) for a in grads]
            + [pl.BlockSpec(memory_space=pl.ANY) for _ in weights],
            out_specs=[pl.BlockSpec((members // 2, 1, rows, width // ring_size), out_at)] * 2,
            scratch_shapes=[
                pltpu.VMEM((tokens, depth), jnp.bfloat16),
                pltpu.VMEM((ring_size, width // ring_size, depth), jnp.bfloat16),
                pltpu.SemaphoreType.DMA((ring_size, len(weights) // ring_size)),
            ],
        ),
        out_shape=[jax.ShapeDtypeStruct(shape, jnp.bfloat16)] * 2,
        cost_estimate=pl.CostEstimate(
            flops=2 * tokens * width * depth,
            bytes_accessed=4 * tokens * width,
            transcendentals=0,
        ),
    )(where, *grads, *weights)


def grouped_device(hidden, norm_gain, w_query, w_key, w_value, upstream, cached, lengths):
    rows, half = hidden.shape
    kv_count = w_key.shape[1] // HD
    query_width = w_query.shape[1] // kv_count
    members = kv_count
    devices, tensors = lax.axis_size("dp"), lax.axis_size("tensor")
    ring_size = devices // members
    tokens = members * rows
    weight_rows = w_key.shape[0]
    me, tensor = lax.axis_index("dp"), lax.axis_index("tensor")
    ring, group = me // members, me % members
    partners = [jnp.bitwise_xor(group, d) for d in range(members)]
    where = jnp.stack([ring, group, tensor] + partners).astype(jnp.int32)

    def to_partner(block, d):
        return lax.ppermute(block, "dp", [(i, i ^ d) for i in range(devices)])

    def to_side(block):
        return lax.ppermute(block, "tensor", [(i, i ^ 1) for i in range(tensors)])

    def to_corner(block, d):
        route = [(i * 2 + t, (i ^ d) * 2 + (t ^ 1)) for i in range(devices) for t in range(2)]
        return lax.ppermute(block, ("dp", "tensor"), route)

    def along(block, distance):
        route = [(i, (i + distance * members) % devices) for i in range(devices)]
        return lax.ppermute(block, "dp", route)

    def columns(array, owner, width):
        return lax.dynamic_slice_in_dim(array, owner * width, width, 1)

    def circulate(own, gate=None):
        pieces = [own]
        for hop in range(1, ring_size):
            block = pieces[-1] if gate is None else gate(hop, pieces[-1])
            pieces.append(along(block, 1))
        return pieces

    k_ring, v_ring = circulate(w_key), circulate(w_value)

    def pack_q(owner):
        return jnp.concatenate(
            [columns(w_query, owner, query_width), columns(upstream, owner, query_width)], axis=0
        )

    q_parts = [pack_q(group)] + [to_partner(pack_q(partners[d]), d) for d in range(1, members)]
    q_own = jnp.concatenate([p[:weight_rows] for p in q_parts], axis=0)
    chunk_width = 2 * HD
    q_chunks = query_width // chunk_width
    q_chunk = [q_own[:, c * chunk_width : (c + 1) * chunk_width] for c in range(q_chunks)]

    def pack_kv(owner):
        pairs = []
        for k, v in zip(k_ring, v_ring):
            cut = [columns(k, owner, HD), columns(v, owner, HD)]
            pairs.append(lax.optimization_barrier(jnp.concatenate(cut, axis=1)))
        return jnp.concatenate(pairs, axis=0)

    across = to_partner(hidden, 2)
    beside, corner = to_side(hidden), to_corner(hidden, 2)
    near = jnp.stack([hidden, beside, across, corner]).reshape(2, 2, rows, half)
    far = to_partner(near, 1)
    *normed, inverse = norm_pieces(where, near, far, norm_gain[None, :], ring_size)

    kv_parts = [pack_kv(group)] + [
        after(to_partner(pack_kv(partners[d]), d), normed[0])
        for d in range(1, members)
    ]
    kv_pieces = [
        jnp.concatenate([p[s * weight_rows : (s + 1) * weight_rows] for p in kv_parts], axis=0)
        for s in range(ring_size)
    ]

    def project(pieces):
        total = None
        for s in range(ring_size):
            term = jnp.dot(normed[s], pieces[s], preferred_element_type=jnp.float32)
            total = term if total is None else total + term
        return total

    first = ring * tokens
    token_positions = first + jnp.arange(tokens, dtype=jnp.int32)
    _, doc_len, positions, onehot = document_info(lengths, token_positions)
    cosine, sine = rope_tables(positions)
    sign = jnp.where(jnp.arange(HD) < HD // 2, -1.0, 1.0).astype(jnp.float32)
    sine = sine * sign[None, :]
    low = (token_positions - positions - first + LONGEST)[None, :]

    def place(parts):
        stacked = jnp.stack(parts)
        return [
            lax.dynamic_index_in_dim(stacked, jnp.bitwise_xor(group, o), 0, keepdims=False)
            for o in range(members)
        ]

    up_own = jnp.concatenate(place([p[weight_rows:] for p in q_parts]), axis=0)
    pooled = (
        jnp.dot(
            onehot.astype(jnp.float32),
            columns(cached, group, query_width),
            precision=lax.Precision.HIGHEST,
        )
        / doc_len.astype(jnp.float32)[:, None]
    )
    out_grad = (up_own.astype(jnp.float32) + pooled).astype(jnp.bfloat16)

    kv_proj = project(kv_pieces)
    key_proj = kv_proj[:, :HD]
    key_own = key_proj * cosine + jnp.roll(key_proj, HD // 2, axis=1) * sine
    kv_rows = jnp.concatenate([key_own, kv_proj[:, HD:]], axis=1).astype(jnp.bfloat16)

    q_pieces = []
    for c in range(q_chunks):
        gate = lambda hop, block, c=c: (
            after(block, q_pieces[c - 1][-1] if c else kv_rows) if hop == ring_size - 1 else block
        )
        q_pieces.append(circulate(q_chunk[c], gate))
    halo = lax.ppermute(kv_rows, "dp", [(i, i + members) for i in range(devices - members)])
    kv_all = jnp.concatenate([halo, kv_rows], axis=0)
    keys, values = kv_all[:, :HD], kv_all[:, HD:]
    keys_turned = keys.T
    query_dones, kv_sum = [], None
    for c in range(q_chunks):
        pieces = q_pieces[c]
        if c:
            pieces = pieces[:-1] + [after(pieces[-1], query_dones[-1])]
        query_done, halo_grad, kv_sum = attend(
            project(pieces),
            out_grad[:, c * chunk_width : (c + 1) * chunk_width],
            keys, keys_turned, values, cosine, sine, low, kv_sum,
        )
        query_dones.append(query_done)
    back = lax.ppermute(halo_grad, "dp", [(i + members, i) for i in range(devices - members)])
    kv_total = kv_sum[LONGEST:] + back.astype(jnp.float32)
    key_grad = kv_total[:, :HD]
    key_done = (key_grad * cosine - jnp.roll(key_grad, HD // 2, axis=1) * sine).astype(jnp.bfloat16)
    value_done = kv_total[:, HD:].astype(jnp.bfloat16)

    key_dones = jnp.concatenate(
        place([key_done] + [to_partner(key_done, d) for d in range(1, members)]),
        axis=1,
    )
    grad_wkey = None
    for s in range(ring_size):
        term = lax.dot_general(
            normed[s][:, :weight_rows],
            key_dones,
            (((0,), (0,)), ((), ())),
            preferred_element_type=jnp.float32,
        )
        if s:
            term = along(term.astype(jnp.bfloat16), -s).astype(jnp.float32)
        grad_wkey = term if grad_wkey is None else grad_wkey + term

    weights = [piece for pieces in q_pieces + [kv_pieces] for piece in pieces]
    keep, send = spread(where, query_dones + [key_done, value_done], weights, ring_size)
    wide = lambda a: a.astype(jnp.float32)
    narrow = lambda a: a.astype(jnp.bfloat16)
    other = to_partner(send, 1)
    both = lambda *at: wide(keep[at]) + wide(other[at])
    cut = half // 2
    low_cut, high_cut, every = slice(0, cut), slice(cut, half), slice(None)
    left_half = to_partner(narrow(both(1, every, every, low_cut)), 2)
    right_half = to_side(narrow(both(every, 1, every, high_cut)))
    left = both(0, every, every, low_cut) + wide(left_half)
    right = both(every, 0, every, high_cut) + wide(right_half)
    left_sum = left[0] + wide(to_side(narrow(left[1])))
    right_sum = right[0] + wide(to_partner(narrow(right[1]), 2))
    normed_grad = jnp.concatenate([left_sum, right_sum], axis=1)
    own_hidden = wide(hidden)
    own_gain = lax.dynamic_slice_in_dim(norm_gain, tensor * half, half, 0)
    own_inverse = lax.dynamic_slice_in_dim(inverse, group * rows, rows, 0)[:, :1]
    part = jnp.sum(normed_grad * own_gain[None, :] * own_hidden, axis=1)[None, :]
    projection = (part + to_side(part)).reshape(rows, 1)
    grad_hidden = (
        own_inverse * own_gain[None, :] * normed_grad
        - own_hidden * (own_inverse * own_inverse * own_inverse) * projection / D
    ).astype(jnp.bfloat16)
    return (grad_hidden, grad_wkey)


def is_grouped(mesh_shape, rows, key_columns):
    members = key_columns // HD
    return (
        mesh_shape["tensor"] == 2
        and members == 4
        and mesh_shape["dp"] == 4 * members
        and members * rows == LONGEST
    )


def per_device(hidden, norm_gain, w_query, w_key, w_value, upstream, cached, lengths):
    arrays = (hidden, norm_gain, w_query, w_key, w_value, upstream, cached, lengths)
    sizes = {axis: lax.axis_size(axis) for axis in ("dp", "tensor")}
    if not is_grouped(sizes, hidden.shape[0], w_key.shape[1]):
        return plain_device(*arrays)
    return grouped_device(*arrays)


def solution(mesh):
    placed = (
        P("dp", "tensor"),
        P(),
        P("dp", "tensor"),
        P("dp", "tensor"),
        P("dp", "tensor"),
        P("dp", "tensor"),
        P(None, "tensor"),
        P(),
    )
    return jax.shard_map(
        per_device,
        mesh=mesh,
        in_specs=placed,
        out_specs=(P("dp", "tensor"), P("dp", "tensor")),
        check_vma=False,
    )
```

```python
from functools import partial

import jax
import jax.numpy as jnp
from jax import lax
from jax.experimental import pallas as pl
from jax.experimental.pallas import tpu as pltpu
from jax.sharding import PartitionSpec as P


D = 4096
HD = 128
HOPS = 4
LONGEST = 512


EPSILON = 1e-05
LOG2_E = 1.4426950408889634
ROPE_BASE = 500000.0


def from_behind(block, axis, distance):
    devices = range(lax.axis_size(axis))
    route = [(i - distance, i) for i in devices if i - distance in devices]
    return lax.ppermute(block, axis, route)


def document_info(lengths, positions_global):
    doc_ends = jnp.cumsum(lengths)
    documents = jnp.sum((positions_global[:, None] >= doc_ends[None, :]).astype(jnp.int32), axis=1)
    doc_slots = jnp.arange(lengths.shape[0], dtype=jnp.int32)
    onehot = documents[:, None] == doc_slots[None, :]
    doc_len = jnp.sum(jnp.where(onehot, lengths[None, :], 0), axis=1)
    doc_end = jnp.sum(jnp.where(onehot, doc_ends[None, :], 0), axis=1)
    return (documents, doc_len, positions_global - doc_end + doc_len, onehot)


def block_mask(lengths, query_positions, key_positions):
    query_docs = document_info(lengths, query_positions)[0]
    key_docs = document_info(lengths, key_positions)[0]
    return (
        (key_positions[None, :] >= 0)
        & (key_docs[None, :] == query_docs[:, None])
        & (key_positions[None, :] <= query_positions[:, None])
    )


def rope_tables(positions):
    half_width = HD // 2
    frequency = ROPE_BASE ** (-(jnp.arange(half_width, dtype=jnp.float32) * 2.0 / HD))
    angles = positions.astype(jnp.float32)[:, None] * frequency[None, :]
    angles = jnp.concatenate([angles, angles], axis=1)
    return (jnp.cos(angles), jnp.sin(angles))


def rotate(values, cosine_table, sine_table):
    half_width = values.shape[-1] // 2
    turned = jnp.concatenate([-values[..., half_width:], values[..., :half_width]], axis=-1)
    return values * cosine_table[:, None, :] + turned * sine_table[:, None, :]


def unrotate(gradient, cosine_table, sine_table):
    half_width = gradient.shape[-1] // 2
    scaled = gradient * sine_table[:, None, :]
    back_part = jnp.concatenate([scaled[..., half_width:], -scaled[..., :half_width]], axis=-1)
    return gradient * cosine_table[:, None, :] + back_part


def contract(left, right):
    return lax.dot_general(
        left, right, (((1,), (1,)), ((), ())), preferred_element_type=jnp.float32
    )


def attend_head(queries, key_rows, value_rows, out_grad, allowed):
    score_scale = HD ** (-0.5)
    scores = contract(queries, key_rows) * score_scale
    weights = jnp.where(allowed, jnp.exp(scores), 0.0)
    totals = jnp.sum(weights, axis=1, keepdims=True)
    softmax = weights / totals
    prob_grad = contract(out_grad, value_rows)
    row_delta = jnp.sum(softmax * prob_grad, axis=1, keepdims=True)
    score_grad = (softmax * (prob_grad - row_delta)).astype(jnp.bfloat16)
    query_grad = jnp.dot(score_grad, key_rows, preferred_element_type=jnp.float32) * score_scale
    key_grad = (
        lax.dot_general(
            score_grad, queries, (((0,), (0,)), ((), ())), preferred_element_type=jnp.float32
        )
        * score_scale
    )
    value_grad = lax.dot_general(
        softmax.astype(jnp.bfloat16),
        out_grad,
        (((0,), (0,)), ((), ())),
        preferred_element_type=jnp.float32,
    )
    return (query_grad, key_grad, value_grad, totals, row_delta)


def fold_heads(per_head, kv_count, group_size):
    summed = per_head.reshape(kv_count, group_size, per_head.shape[1], HD).sum(axis=1)
    return jnp.transpose(summed, (1, 0, 2))


def plain_device(hidden, norm_gain, w_query, w_key, w_value, upstream, cached, lengths):
    gathered = lax.all_gather(hidden, "tensor", axis=1, tiled=True)
    row_count = gathered.shape[0]
    query_cols = w_query.shape[1]
    key_cols = w_key.shape[1]
    head_count = query_cols // HD
    kv_count = key_cols // HD
    group_size = head_count // kv_count
    hidden_wide = gathered.astype(jnp.float32)
    inverse_scale = lax.rsqrt(jnp.mean(hidden_wide * hidden_wide, axis=1, keepdims=True) + EPSILON)
    normed = (hidden_wide * inverse_scale * norm_gain[None, :]).astype(jnp.bfloat16)
    dp_index = lax.axis_index("dp")
    own_positions = dp_index * row_count + jnp.arange(row_count, dtype=jnp.int32)
    _, doc_len, positions, onehot = document_info(lengths, own_positions)
    cosine_table, sine_table = rope_tables(positions)
    full_query, full_key, full_value = (
        lax.all_gather(w_query, "dp", axis=0, tiled=True),
        lax.all_gather(w_key, "dp", axis=0, tiled=True),
        lax.all_gather(w_value, "dp", axis=0, tiled=True),
    )
    query_proj = jnp.dot(normed, full_query, preferred_element_type=jnp.float32)
    key_proj = jnp.dot(normed, full_key, preferred_element_type=jnp.float32)
    value_proj = jnp.dot(normed, full_value, preferred_element_type=jnp.float32)
    queries = rotate(
        query_proj.reshape(row_count, head_count, HD), cosine_table, sine_table
    ).astype(jnp.bfloat16)
    key_rows = rotate(key_proj.reshape(row_count, kv_count, HD), cosine_table, sine_table).astype(
        jnp.bfloat16
    )
    value_rows = value_proj.astype(jnp.bfloat16).reshape(row_count, kv_count, HD)
    pooled = (
        jnp.dot(onehot.astype(jnp.float32), cached, precision=lax.Precision.HIGHEST)
        / doc_len.astype(jnp.float32)[:, None]
    )
    out_grad = (
        (upstream.astype(jnp.float32) + pooled)
        .astype(jnp.bfloat16)
        .reshape(row_count, head_count, HD)
    )
    key_list = []
    value_list = []
    for distance in range(HOPS, 0, -1):
        earlier_key, earlier_value = from_behind((key_rows, value_rows), "dp", distance)
        key_list.append(earlier_key)
        value_list.append(earlier_value)
    key_window = jnp.concatenate(key_list + [key_rows], axis=0)
    value_window = jnp.concatenate(value_list + [value_rows], axis=0)
    window = key_window.shape[0]
    window_positions = dp_index * row_count - HOPS * row_count + jnp.arange(window, dtype=jnp.int32)
    allowed = block_mask(lengths, own_positions, window_positions)
    head_queries = jnp.transpose(queries, (1, 0, 2))
    head_grads = jnp.transpose(out_grad, (1, 0, 2))
    head_keys = jnp.transpose(jnp.repeat(key_window, group_size, axis=1), (1, 0, 2))
    head_values = jnp.transpose(jnp.repeat(value_window, group_size, axis=1), (1, 0, 2))

    def one_head(operands):
        return attend_head(operands[0], operands[1], operands[2], operands[3], allowed)

    query_grad, key_grad, value_grad, _, _ = lax.map(
        one_head, (head_queries, head_keys, head_values, head_grads)
    )
    key_sum = fold_heads(key_grad, kv_count, group_size)
    value_sum = fold_heads(value_grad, kv_count, group_size)
    own_key = key_sum[HOPS * row_count :]
    own_value = value_sum[HOPS * row_count :]
    for distance in range(1, HOPS + 1):
        lower = (HOPS - distance) * row_count
        back_key, back_value = (
            from_behind(
                key_sum[lower : lower + row_count].astype(jnp.bfloat16), "dp", -distance
            ).astype(jnp.float32),
            from_behind(
                value_sum[lower : lower + row_count].astype(jnp.bfloat16), "dp", -distance
            ).astype(jnp.float32),
        )
        own_key = own_key + back_key
        own_value = own_value + back_value
    query_done = (
        unrotate(jnp.transpose(query_grad, (1, 0, 2)), cosine_table, sine_table)
        .astype(jnp.bfloat16)
        .reshape(row_count, query_cols)
    )
    key_done = (
        unrotate(own_key, cosine_table, sine_table)
        .astype(jnp.bfloat16)
        .reshape(row_count, key_cols)
    )
    value_done = own_value.astype(jnp.bfloat16).reshape(row_count, key_cols)
    portion = (
        contract(query_done, full_query)
        + contract(key_done, full_key)
        + contract(value_done, full_value)
    )
    own_hidden = hidden.astype(jnp.float32)
    own_cols = hidden.shape[1]
    gain_offset = lax.axis_index("tensor") * own_cols
    own_gain = lax.dynamic_slice_in_dim(norm_gain, gain_offset, own_cols, 0)
    normed_grad = lax.psum_scatter(
        portion.astype(jnp.bfloat16), "tensor", scatter_dimension=1, tiled=True
    ).astype(jnp.float32)
    projection = lax.psum(
        jnp.sum(normed_grad * own_gain[None, :] * own_hidden, axis=1, keepdims=True), "tensor"
    )
    grad_hidden = (
        inverse_scale * own_gain[None, :] * normed_grad
        - own_hidden * (inverse_scale * inverse_scale * inverse_scale) * projection / D
    ).astype(jnp.bfloat16)
    grad_wkey = lax.psum_scatter(
        lax.dot_general(
            normed, key_done, (((0,), (0,)), ((), ())), preferred_element_type=jnp.float32
        ),
        "dp",
        scatter_dimension=0,
        tiled=True,
    )
    return (grad_hidden, grad_wkey)


def after(array, *others):
    return lax.optimization_barrier((array, *others))[0]


def norm_kernel(where, near_ref, far_ref, gain_ref, *outs):
    pieces, inv_ref = outs[:-1], outs[-1]
    ring, tensor = where[0], where[2]
    ring_size = len(pieces)
    members = where.shape[0] - 3
    step = pieces[0].shape[1] // members

    def write(ref):
        total = jnp.zeros((ref.shape[2], 1), jnp.float32)
        for half in range(2):
            wide = ref[0, half].astype(jnp.float32)
            total = total + jnp.sum(wide * wide, axis=1, keepdims=True)
        inverse = lax.rsqrt(total / D + EPSILON)
        inv_ref[...] = jnp.broadcast_to(inverse, inv_ref.shape)
        planes_per_half = ring_size // 2
        for s in range(ring_size):
            plane = lax.rem(ring - s + ring_size, ring_size)
            half = lax.rem(plane // planes_per_half + tensor, 2)
            for d in range(members):
                inner = lax.rem(plane, planes_per_half) * (members * step) + where[3 + d] * step
                inner = pl.multiple_of(inner, step)
                outer = pl.multiple_of((plane * members + where[3 + d]) * step, step)
                wide = ref[0, half, :, pl.ds(inner, step)].astype(jnp.float32)
                scaled = wide * inverse * gain_ref[:, pl.ds(outer, step)]
                pieces[s][:, d * step : (d + 1) * step] = scaled.astype(jnp.bfloat16)

    @pl.when(pl.program_id(1) == 0)
    def _():
        write(near_ref)

    @pl.when(pl.program_id(1) == 1)
    def _():
        write(far_ref)


def norm_pieces(where, near, far, gain, ring_size):
    rows, half = near.shape[2], near.shape[3]
    members = where.shape[0] - 3
    tokens = members * rows
    width = 2 * half // ring_size
    spec = pl.BlockSpec((1, 2, rows, half), lambda u, v, w: (u, 0, 0, 0))

    def out_row(u, v, w):
        return (w[3 + 2 * u + v], 0)

    return pl.pallas_call(
        norm_kernel,
        grid_spec=pltpu.PrefetchScalarGridSpec(
            num_scalar_prefetch=1,
            grid=(2, 2),
            in_specs=[spec, spec, pl.BlockSpec((1, 2 * half), lambda u, v, w: (0, 0))],
            out_specs=[pl.BlockSpec((rows, width), out_row)] * ring_size
            + [pl.BlockSpec((rows, 128), out_row)],
        ),
        out_shape=[jax.ShapeDtypeStruct((tokens, width), jnp.bfloat16)] * ring_size
        + [jax.ShapeDtypeStruct((tokens, 128), jnp.float32)],
        compiler_params=pltpu.CompilerParams(vmem_limit_bytes=24 << 20),
        cost_estimate=pl.CostEstimate(
            flops=8 * tokens * 2 * half, bytes_accessed=8 * tokens * half, transcendentals=tokens
        ),
    )(where, near, far, gain)


def attend_kernel(heads, rows, terms, first, q_ref, *refs):
    n_refs, w_refs, refs = refs[:terms], refs[terms : 2 * terms], refs[2 * terms :]
    g_ref, k_ref, kt_ref, v_ref, cos_ref, sin_ref, low_ref = refs[:7]
    before = None if first else refs[7]
    dq_ref, key_halo_ref, value_halo_ref, dkv_ref = refs[7 if first else 8 :]
    scale = HD ** (-0.5)
    halo = key_halo_ref.shape[0]
    window = halo + rows
    blocks = q_ref.shape[0] // rows

    @pl.when(pl.program_id(0) == 0)
    def _():
        dkv_ref[...] = jnp.zeros_like(dkv_ref) if first else before[...]

    projected = q_ref[...]
    for n_ref, w_ref in zip(n_refs, w_refs):
        projected += jnp.dot(n_ref[...], w_ref[...], preferred_element_type=jnp.float32)
    key_at = lax.broadcasted_iota(jnp.int32, (window, rows), 0)
    query_at = lax.broadcasted_iota(jnp.int32, (rows, rows), 1)
    causal = key_at[:rows] <= query_at
    staged = []
    for block in range(blocks):
        here = slice(block * rows, (block + 1) * rows)
        base = pl.multiple_of((pl.program_id(0) * blocks + block) * rows, rows)
        cosine, sine = cos_ref[here, :], sin_ref[here, :]
        turned = []
        for h in range(heads):
            u = projected[here, h * HD : (h + 1) * HD]
            turned.append((u * cosine + pltpu.roll(u, HD // 2, 1) * sine).astype(jnp.bfloat16))
        queries = jnp.concatenate(turned, axis=0)
        grads = jnp.concatenate([g_ref[here, h * HD : (h + 1) * HD] for h in range(heads)], axis=0)
        scores = contract(k_ref[pl.ds(base, window), :], queries)
        prob_grads = contract(v_ref[pl.ds(base, window), :], grads)
        staged.append((here, base, cosine, sine, queries, grads, scores, prob_grads))
    for here, base, cosine, sine, queries, grads, scores, prob_grads in staged:
        low = low_ref[:, here] - base
        inside = key_at >= low
        allowed = (inside[:halo], inside[halo:] & causal)
        probs, score_grads = [], []
        for h in range(heads):
            there = slice(h * rows, (h + 1) * rows)
            grown = jnp.exp2(scores[:, there] * (scale * LOG2_E))
            weights = jnp.concatenate(
                [
                    jnp.where(allowed[0], grown[:halo], 0.0),
                    jnp.where(allowed[1], grown[halo:], 0.0),
                ],
                axis=0,
            )
            prob_grad = prob_grads[:, there]
            share = 1.0 / jnp.sum(weights, axis=0, keepdims=True)
            row_delta = jnp.sum(weights * prob_grad, axis=0, keepdims=True) * share
            softmax = weights * share
            probs.append(softmax.astype(jnp.bfloat16))
            score_grads.append((softmax * (prob_grad - row_delta)).astype(jnp.bfloat16))
        probs = jnp.concatenate(probs, axis=1)
        score_grads = jnp.concatenate(score_grads, axis=1)
        dkv_ref[pl.ds(base, window), :HD] += (
            jnp.dot(score_grads, queries, preferred_element_type=jnp.float32) * scale
        )
        dkv_ref[pl.ds(base, window), HD:] += jnp.dot(
            probs, grads, preferred_element_type=jnp.float32
        )
        query_grads = jnp.dot(
            kt_ref[:, pl.ds(base, window)], score_grads, preferred_element_type=jnp.float32
        )
        for h in range(heads):
            grad = query_grads[:, h * rows : (h + 1) * rows].T * scale
            back = grad * cosine - pltpu.roll(grad, HD // 2, 1) * sine
            dq_ref[here, h * HD : (h + 1) * HD] = back.astype(jnp.bfloat16)

    @pl.when(pl.program_id(0) == pl.num_programs(0) - 1)
    def _():
        key_halo_ref[...] = dkv_ref[:halo, :HD].astype(jnp.bfloat16)
        value_halo_ref[...] = dkv_ref[:halo, HD:].astype(jnp.bfloat16)


def attend(q_proj, normed, weights, grads, keys, keys_turned, values, cosine, sine, low, before=None):
    tokens, width = q_proj.shape
    heads, rows = width // HD, 128
    step = 2 * rows
    total = keys.shape[0]
    window = total - tokens + rows
    whole = lambda a: pl.BlockSpec(a.shape, lambda i: (0, 0))
    by_rows = lambda w: pl.BlockSpec((step, w), lambda i: (i, 0))
    fixed = lambda n, w: pl.BlockSpec((n, w), lambda i: (0, 0))
    extra = [] if before is None else [before]
    return pl.pallas_call(
        partial(attend_kernel, heads, rows, len(normed), before is None),
        grid=(tokens // step,),
        in_specs=[by_rows(width)]
        + [by_rows(n.shape[1]) for n in normed]
        + [whole(w) for w in weights]
        + [by_rows(width), whole(keys), whole(keys_turned), whole(values)]
        + [by_rows(HD), by_rows(HD), pl.BlockSpec((1, step), lambda i: (0, i))]
        + [fixed(total, 2 * HD) for _ in extra],
        out_specs=[by_rows(width)] + [fixed(total - tokens, HD)] * 2 + [fixed(total, 2 * HD)],
        out_shape=[jax.ShapeDtypeStruct((tokens, width), jnp.bfloat16),
                   jax.ShapeDtypeStruct((total - tokens, HD), jnp.bfloat16),
                   jax.ShapeDtypeStruct((total - tokens, HD), jnp.bfloat16),
                   jax.ShapeDtypeStruct((total, 2 * HD), jnp.float32)],
        cost_estimate=pl.CostEstimate(
            flops=10 * tokens * window * width, bytes_accessed=12 * tokens * width,
            transcendentals=tokens * window * heads,
        ),
    )(q_proj, *normed, *weights, grads, keys, keys_turned, values, cosine, sine, low, *extra)


def spread_blocks(where, wide, grads, rows):
    members = where.shape[0] - 3
    for block in range(members):
        partner = (block % (members // 2)) * 2 + block // (members // 2)
        source = pl.multiple_of(where[3 + partner] * rows, rows)
        at = 0
        for grad in grads:
            wide[block * rows : (block + 1) * rows, at : at + grad.shape[1]] = grad[
                pl.ds(source, rows), :
            ]
            at += grad.shape[1]


def spread_first_kernel(counts, ring_size, where, *refs):
    grads, weights = refs[: counts[0]], refs[counts[0] : counts[0] + counts[1] * ring_size]
    out_ref, wide, held, arrived = refs[counts[0] + counts[1] * ring_size :]
    members = where.shape[0] - 3
    step = held.shape[1] // members
    s = pl.program_id(0)

    def copy(source, piece, c):
        width = source.shape[1]
        return pltpu.make_async_copy(
            source, held.at[piece, :, pl.ds(c * width, width)], arrived.at[piece, c]
        )

    @pl.when(s == 0)
    def _():
        for piece in range(ring_size):
            for c in range(counts[1]):
                copy(weights[c * ring_size + piece], piece, c).start()
        spread_blocks(where, wide, grads, wide.shape[0] // members)

    for c in range(counts[1]):
        copy(weights[c * ring_size], s, c).wait()
    for owner in range(members):
        source = pl.multiple_of(where[3 + owner] * step, step)
        out_ref[0, :, owner * step : (owner + 1) * step] = contract(
            wide[...], held[s, pl.ds(source, step), :]
        )


def spread_first(where, grads, weights, ring_size):
    tokens = grads[0].shape[0]
    depth = sum(a.shape[1] for a in grads)
    width = weights[0].shape[0]
    chunks = len(weights) // ring_size
    return pl.pallas_call(
        partial(spread_first_kernel, (len(grads), chunks), ring_size),
        grid_spec=pltpu.PrefetchScalarGridSpec(
            num_scalar_prefetch=1,
            grid=(ring_size,),
            in_specs=[pl.BlockSpec(a.shape, lambda i, w: (0, 0)) for a in grads]
            + [pl.BlockSpec(memory_space=pltpu.HBM) for _ in weights],
            out_specs=pl.BlockSpec((1, tokens, width), lambda i, w: (i, 0, 0)),
            scratch_shapes=[
                pltpu.VMEM((tokens, depth), jnp.bfloat16),
                pltpu.VMEM((ring_size, width, depth), jnp.bfloat16),
                pltpu.SemaphoreType.DMA((ring_size, chunks)),
            ],
        ),
        out_shape=jax.ShapeDtypeStruct((ring_size, tokens, width), jnp.float32),
        compiler_params=pltpu.CompilerParams(vmem_limit_bytes=24 << 20),
        cost_estimate=pl.CostEstimate(
            flops=2 * tokens * width * ring_size * depth,
            bytes_accessed=4 * tokens * width * ring_size,
            transcendentals=0,
        ),
    )(where, *grads, *weights)


def spread_last_kernel(count, where, so_far, *refs):
    grads, weights = refs[:count], refs[count:-3]
    keep_ref, send_ref, wide = refs[-3:]
    members = where.shape[0] - 3
    step = weights[0].shape[0] // members
    rows = keep_ref.shape[2]
    s = pl.program_id(0)

    @pl.when(s == 0)
    def _():
        spread_blocks(where, wide, grads, rows)

    for piece, weight in enumerate(weights):

        @pl.when(s == piece)
        def _():
            for owner in range(members):
                source = pl.multiple_of(where[3 + owner] * step, step)
                lanes = slice(owner * step, (owner + 1) * step)
                total = so_far[0, :, lanes] + contract(wide[...], weight[pl.ds(source, step), :])
                total = total.astype(jnp.bfloat16)
                for u in range(members // 2):
                    keep_ref[u, 0, :, lanes] = total[u * rows : (u + 1) * rows, :]
                    lower = (members // 2 + u) * rows
                    send_ref[u, 0, :, lanes] = total[lower : lower + rows, :]


def spread_last(where, so_far, grads, weights, ring_size):
    tokens = grads[0].shape[0]
    members = where.shape[0] - 3
    rows = tokens // members
    depth = sum(a.shape[1] for a in grads)
    width = weights[0].shape[0]
    planes_per_half = ring_size // 2
    whole = lambda a: pl.BlockSpec(a.shape, lambda i, w: (0, 0))

    def out_at(s, w):
        plane = lax.rem(w[0] - s + ring_size, ring_size)
        half = lax.rem(plane // planes_per_half + w[2], 2)
        return (0, half, 0, lax.rem(plane, planes_per_half))

    shape = (members // 2, 2, rows, width * planes_per_half)
    return pl.pallas_call(
        partial(spread_last_kernel, len(grads)),
        grid_spec=pltpu.PrefetchScalarGridSpec(
            num_scalar_prefetch=1,
            grid=(ring_size,),
            in_specs=[pl.BlockSpec((1, tokens, width), lambda i, w: (i, 0, 0))]
            + [whole(a) for a in grads]
            + [pl.BlockSpec(memory_space=pltpu.VMEM) for a in weights],
            out_specs=[pl.BlockSpec((members // 2, 1, rows, width), out_at)] * 2,
            scratch_shapes=[pltpu.VMEM((tokens, depth), jnp.bfloat16)],
        ),
        out_shape=[jax.ShapeDtypeStruct(shape, jnp.bfloat16)] * 2,
        compiler_params=pltpu.CompilerParams(vmem_limit_bytes=24 << 20),
        cost_estimate=pl.CostEstimate(
            flops=2 * tokens * width * ring_size * depth,
            bytes_accessed=4 * tokens * width * ring_size,
            transcendentals=0,
        ),
    )(where, so_far, *grads, *weights)


def key_weights_kernel(ring_size, where, *refs):
    members = where.shape[0] - 3
    normed, grads = refs[:ring_size], refs[ring_size : ring_size + members]
    out_refs, wide = refs[ring_size + members : -1], refs[-1]
    width = grads[0].shape[1]
    for owner in range(members):
        for d in range(members):

            @pl.when(where[3 + owner] == d)
            def _():
                wide[:, owner * width : (owner + 1) * width] = grads[d][...]

    for n_ref, out_ref in zip(normed, out_refs):
        out_ref[...] = lax.dot_general(
            n_ref[...], wide[...], (((0,), (0,)), ((), ())), preferred_element_type=jnp.float32
        ).astype(out_ref.dtype)


def key_weights(where, normed, grads, rows):
    tokens, members = grads[0].shape[0], len(grads)
    width = members * grads[0].shape[1]
    shape = (rows, width)
    return pl.pallas_call(
        partial(key_weights_kernel, len(normed)),
        grid_spec=pltpu.PrefetchScalarGridSpec(
            num_scalar_prefetch=1,
            grid=(1,),
            in_specs=[pl.BlockSpec((tokens, rows), lambda i, w: (0, 0)) for _ in normed]
            + [pl.BlockSpec(g.shape, lambda i, w: (0, 0)) for g in grads],
            out_specs=[pl.BlockSpec(shape, lambda i, w: (0, 0))] * len(normed),
            scratch_shapes=[pltpu.VMEM((tokens, width), jnp.bfloat16)],
        ),
        out_shape=[jax.ShapeDtypeStruct(shape, jnp.float32)]
        + [jax.ShapeDtypeStruct(shape, jnp.bfloat16)] * (len(normed) - 1),
        compiler_params=pltpu.CompilerParams(vmem_limit_bytes=16 << 20),
        cost_estimate=pl.CostEstimate(
            flops=2 * tokens * width * rows * len(normed),
            bytes_accessed=2 * tokens * (width + rows * len(normed)),
            transcendentals=0,
        ),
    )(where, *normed, *grads)


def grouped_device(hidden, norm_gain, w_query, w_key, w_value, upstream, cached, lengths):
    rows, half = hidden.shape
    kv_count = w_key.shape[1] // HD
    query_width = w_query.shape[1] // kv_count
    members = kv_count
    devices, tensors = lax.axis_size("dp"), lax.axis_size("tensor")
    ring_size = devices // members
    tokens = members * rows
    weight_rows = w_key.shape[0]
    me, tensor = lax.axis_index("dp"), lax.axis_index("tensor")
    ring, group = me // members, me % members
    partners = [jnp.bitwise_xor(group, d) for d in range(members)]
    where = jnp.stack([ring, group, tensor] + partners).astype(jnp.int32)

    def to_partner(block, d):
        return lax.ppermute(block, "dp", [(i, i ^ d) for i in range(devices)])

    def to_side(block):
        return lax.ppermute(block, "tensor", [(i, i ^ 1) for i in range(tensors)])

    def to_corner(block, d):
        route = [(i * 2 + t, (i ^ d) * 2 + (t ^ 1)) for i in range(devices) for t in range(2)]
        return lax.ppermute(block, ("dp", "tensor"), route)

    def along(block, distance):
        route = [(i, (i + distance * members) % devices) for i in range(devices)]
        return lax.ppermute(block, "dp", route)

    def columns(array, owner, width):
        return lax.dynamic_slice_in_dim(array, owner * width, width, 1)

    def circulate(own, gate=None):
        pieces = [own]
        for hop in range(1, ring_size):
            block = pieces[-1] if gate is None else gate(hop, pieces[-1])
            pieces.append(along(block, 1))
        return pieces

    k_ring, v_ring = circulate(w_key), circulate(w_value)

    def pack_q(owner):
        return jnp.concatenate(
            [columns(w_query, owner, query_width), columns(upstream, owner, query_width)], axis=0
        )

    q_parts = [pack_q(group)] + [to_partner(pack_q(partners[d]), d) for d in range(1, members)]
    q_own = jnp.concatenate([p[:weight_rows] for p in q_parts], axis=0)
    chunk_width = 2 * HD
    q_chunks = query_width // chunk_width
    q_chunk = [q_own[:, c * chunk_width : (c + 1) * chunk_width] for c in range(q_chunks)]

    def pack_kv(owner):
        pairs = []
        for k, v in zip(k_ring, v_ring):
            cut = [columns(k, owner, HD), columns(v, owner, HD)]
            pairs.append(lax.optimization_barrier(jnp.concatenate(cut, axis=1)))
        return jnp.concatenate(pairs, axis=0)

    across = to_partner(hidden, 2)
    beside, corner = to_side(hidden), to_corner(hidden, 2)
    near = jnp.stack([hidden, beside, across, corner]).reshape(2, 2, rows, half)
    far = to_partner(near, 1)
    *normed, inverse = norm_pieces(where, near, far, norm_gain[None, :], ring_size)

    kv_parts = [pack_kv(group)] + [
        after(to_partner(pack_kv(partners[d]), d), normed[0])
        for d in range(1, members)
    ]
    kv_pieces = [
        jnp.concatenate([p[s * weight_rows : (s + 1) * weight_rows] for p in kv_parts], axis=0)
        for s in range(ring_size)
    ]

    def project(pieces):
        total = None
        for s, piece in enumerate(pieces):
            term = jnp.dot(normed[s], piece, preferred_element_type=jnp.float32)
            total = term if total is None else total + term
        return total

    first = ring * tokens
    token_positions = first + jnp.arange(tokens, dtype=jnp.int32)
    _, doc_len, positions, onehot = document_info(lengths, token_positions)
    cosine, sine = rope_tables(positions)
    sign = jnp.where(jnp.arange(HD) < HD // 2, -1.0, 1.0).astype(jnp.float32)
    sine = sine * sign[None, :]
    low = (token_positions - positions - first + LONGEST)[None, :]

    def place(parts):
        stacked = jnp.stack(parts)
        return [
            lax.dynamic_index_in_dim(stacked, jnp.bitwise_xor(group, o), 0, keepdims=False)
            for o in range(members)
        ]

    up_own = jnp.concatenate(place([p[weight_rows:] for p in q_parts]), axis=0)
    pooled = (
        jnp.dot(
            onehot.astype(jnp.float32),
            columns(cached, group, query_width),
            precision=lax.Precision.HIGHEST,
        )
        / doc_len.astype(jnp.float32)[:, None]
    )
    out_grad = (up_own.astype(jnp.float32) + pooled).astype(jnp.bfloat16)

    kv_proj = project(kv_pieces)
    key_proj = kv_proj[:, :HD]
    key_own = key_proj * cosine + jnp.roll(key_proj, HD // 2, axis=1) * sine
    kv_rows = jnp.concatenate([key_own, kv_proj[:, HD:]], axis=1).astype(jnp.bfloat16)

    q_pieces = []
    for c in range(q_chunks):
        gate = lambda hop, block, c=c: after(block, kv_rows) if c and hop == ring_size - 1 else block
        q_pieces.append(circulate(q_chunk[c], gate))
    halo = lax.ppermute(kv_rows, "dp", [(i, i + members) for i in range(devices - members)])
    kv_all = jnp.concatenate([halo, kv_rows], axis=0)
    keys, values = kv_all[:, :HD], kv_all[:, HD:]
    keys_turned = keys.T
    query_dones, kv_sum = [], None
    for c in range(q_chunks):
        early = lax.optimization_barrier(project(q_pieces[c][:-1]))
        query_done, key_halo, value_halo, kv_sum = attend(
            early, normed[-1:], q_pieces[c][-1:],
            out_grad[:, c * chunk_width : (c + 1) * chunk_width],
            keys, keys_turned, values, cosine, sine, low, kv_sum,
        )
        query_dones.append(query_done)
    later = [(i + members, i) for i in range(devices - members)]
    key_back = lax.ppermute(key_halo, "dp", later)
    value_back = lax.ppermute(value_halo, "dp", later)
    key_grad = kv_sum[LONGEST:, :HD] + key_back.astype(jnp.float32)
    turned = jnp.roll(key_grad, HD // 2, axis=1)
    key_done = (key_grad * cosine - turned * sine).astype(jnp.bfloat16)
    value_grad = after(kv_sum[LONGEST:, HD:], key_done) + value_back.astype(jnp.float32)
    value_done = value_grad.astype(jnp.bfloat16)

    key_dones = [key_done] + [to_partner(key_done, d) for d in range(1, members)]
    grad_wkey, *others = key_weights(where, normed, key_dones, weight_rows)
    for s in range(1, ring_size):
        term = along(others[s - 1], -s)
        grad_wkey = grad_wkey + term.astype(jnp.float32)

    weights = [
        pltpu.with_memory_space_constraint(piece, pltpu.HBM)
        for pieces in q_pieces
        for piece in pieces
    ]
    so_far = spread_first(where, query_dones, weights, ring_size)
    keep, send = spread_last(where, so_far, [key_done, value_done], kv_pieces, ring_size)
    wide = lambda a: a.astype(jnp.float32)
    narrow = lambda a: a.astype(jnp.bfloat16)
    other = to_partner(send, 1)
    both = lambda *at: wide(keep[at]) + wide(other[at])
    cut = half // 2
    low_cut, high_cut, every = slice(0, cut), slice(cut, half), slice(None)
    left_half = narrow(both(1, every, every, low_cut))
    right_half = narrow(both(every, 1, every, high_cut))
    left_half = to_partner(left_half, 2)
    right_half = to_side(right_half)
    left = both(0, every, every, low_cut) + wide(left_half)
    right = both(every, 0, every, high_cut) + wide(right_half)
    left_sum = left[0] + wide(to_side(narrow(left[1])))
    right_sum = right[0] + wide(to_partner(narrow(right[1]), 2))
    normed_grad = jnp.concatenate([left_sum, right_sum], axis=1)
    own_hidden = wide(hidden)
    own_gain = lax.dynamic_slice_in_dim(norm_gain, tensor * half, half, 0)
    own_inverse = lax.dynamic_slice_in_dim(inverse, group * rows, rows, 0)[:, :1]
    part = jnp.sum(normed_grad * own_gain[None, :] * own_hidden, axis=1)[None, :]
    projection = (part + to_side(part)).reshape(rows, 1)
    grad_hidden = (
        own_inverse * own_gain[None, :] * normed_grad
        - own_hidden * (own_inverse * own_inverse * own_inverse) * projection / D
    ).astype(jnp.bfloat16)
    return (grad_hidden, grad_wkey)


def is_grouped(mesh_shape, rows, key_columns):
    members = key_columns // HD
    return (
        mesh_shape["tensor"] == 2
        and members == 4
        and mesh_shape["dp"] == 4 * members
        and members * rows == LONGEST
    )


def per_device(hidden, norm_gain, w_query, w_key, w_value, upstream, cached, lengths):
    arrays = (hidden, norm_gain, w_query, w_key, w_value, upstream, cached, lengths)
    sizes = {axis: lax.axis_size(axis) for axis in ("dp", "tensor")}
    if not is_grouped(sizes, hidden.shape[0], w_key.shape[1]):
        return plain_device(*arrays)
    return grouped_device(*arrays)


def solution(mesh):
    placed = (
        P("dp", "tensor"),
        P(),
        P("dp", "tensor"),
        P("dp", "tensor"),
        P("dp", "tensor"),
        P("dp", "tensor"),
        P(None, "tensor"),
        P(),
    )
    return jax.shard_map(
        per_device,
        mesh=mesh,
        in_specs=placed,
        out_specs=(P("dp", "tensor"), P("dp", "tensor")),
        check_vma=False,
    )
```

```python
from functools import partial

import jax
import jax.numpy as jnp
from jax import lax
from jax.experimental import pallas as pl
from jax.experimental.pallas import tpu as pltpu
from jax.sharding import PartitionSpec as P


D = 4096
HD = 128
HOPS = 4
LONGEST = 512
CHUNKS = (2, 2)


EPSILON = 1e-05
LOG2_E = 1.4426950408889634
ROPE_BASE = 500000.0


def from_behind(block, axis, distance):
    devices = range(lax.axis_size(axis))
    route = [(i - distance, i) for i in devices if i - distance in devices]
    return lax.ppermute(block, axis, route)


def document_info(lengths, positions_global):
    doc_ends = jnp.cumsum(lengths)
    documents = jnp.sum((positions_global[:, None] >= doc_ends[None, :]).astype(jnp.int32), axis=1)
    doc_slots = jnp.arange(lengths.shape[0], dtype=jnp.int32)
    onehot = documents[:, None] == doc_slots[None, :]
    doc_len = jnp.sum(jnp.where(onehot, lengths[None, :], 0), axis=1)
    doc_end = jnp.sum(jnp.where(onehot, doc_ends[None, :], 0), axis=1)
    return (documents, doc_len, positions_global - doc_end + doc_len, onehot)


def block_mask(lengths, query_positions, key_positions):
    query_docs = document_info(lengths, query_positions)[0]
    key_docs = document_info(lengths, key_positions)[0]
    return (
        (key_positions[None, :] >= 0)
        & (key_docs[None, :] == query_docs[:, None])
        & (key_positions[None, :] <= query_positions[:, None])
    )


def rope_tables(positions):
    half_width = HD // 2
    frequency = ROPE_BASE ** (-(jnp.arange(half_width, dtype=jnp.float32) * 2.0 / HD))
    angles = positions.astype(jnp.float32)[:, None] * frequency[None, :]
    angles = jnp.concatenate([angles, angles], axis=1)
    return (jnp.cos(angles), jnp.sin(angles))


def rotate(values, cosine_table, sine_table):
    half_width = values.shape[-1] // 2
    turned = jnp.concatenate([-values[..., half_width:], values[..., :half_width]], axis=-1)
    return values * cosine_table[:, None, :] + turned * sine_table[:, None, :]


def unrotate(gradient, cosine_table, sine_table):
    half_width = gradient.shape[-1] // 2
    scaled = gradient * sine_table[:, None, :]
    back_part = jnp.concatenate([scaled[..., half_width:], -scaled[..., :half_width]], axis=-1)
    return gradient * cosine_table[:, None, :] + back_part


def contract(left, right):
    return lax.dot_general(
        left, right, (((1,), (1,)), ((), ())), preferred_element_type=jnp.float32
    )


def attend_head(queries, key_rows, value_rows, out_grad, allowed):
    score_scale = HD ** (-0.5)
    scores = contract(queries, key_rows) * score_scale
    weights = jnp.where(allowed, jnp.exp(scores), 0.0)
    totals = jnp.sum(weights, axis=1, keepdims=True)
    softmax = weights / totals
    prob_grad = contract(out_grad, value_rows)
    row_delta = jnp.sum(softmax * prob_grad, axis=1, keepdims=True)
    score_grad = (softmax * (prob_grad - row_delta)).astype(jnp.bfloat16)
    query_grad = jnp.dot(score_grad, key_rows, preferred_element_type=jnp.float32) * score_scale
    key_grad = (
        lax.dot_general(
            score_grad, queries, (((0,), (0,)), ((), ())), preferred_element_type=jnp.float32
        )
        * score_scale
    )
    value_grad = lax.dot_general(
        softmax.astype(jnp.bfloat16),
        out_grad,
        (((0,), (0,)), ((), ())),
        preferred_element_type=jnp.float32,
    )
    return (query_grad, key_grad, value_grad, totals, row_delta)


def fold_heads(per_head, kv_count, group_size):
    summed = per_head.reshape(kv_count, group_size, per_head.shape[1], HD).sum(axis=1)
    return jnp.transpose(summed, (1, 0, 2))


def plain_device(hidden, norm_gain, w_query, w_key, w_value, upstream, cached, lengths):
    gathered = lax.all_gather(hidden, "tensor", axis=1, tiled=True)
    row_count = gathered.shape[0]
    query_cols = w_query.shape[1]
    key_cols = w_key.shape[1]
    head_count = query_cols // HD
    kv_count = key_cols // HD
    group_size = head_count // kv_count
    hidden_wide = gathered.astype(jnp.float32)
    inverse_scale = lax.rsqrt(jnp.mean(hidden_wide * hidden_wide, axis=1, keepdims=True) + EPSILON)
    normed = (hidden_wide * inverse_scale * norm_gain[None, :]).astype(jnp.bfloat16)
    dp_index = lax.axis_index("dp")
    own_positions = dp_index * row_count + jnp.arange(row_count, dtype=jnp.int32)
    _, doc_len, positions, onehot = document_info(lengths, own_positions)
    cosine_table, sine_table = rope_tables(positions)
    full_query, full_key, full_value = (
        lax.all_gather(w_query, "dp", axis=0, tiled=True),
        lax.all_gather(w_key, "dp", axis=0, tiled=True),
        lax.all_gather(w_value, "dp", axis=0, tiled=True),
    )
    query_proj = jnp.dot(normed, full_query, preferred_element_type=jnp.float32)
    key_proj = jnp.dot(normed, full_key, preferred_element_type=jnp.float32)
    value_proj = jnp.dot(normed, full_value, preferred_element_type=jnp.float32)
    queries = rotate(
        query_proj.reshape(row_count, head_count, HD), cosine_table, sine_table
    ).astype(jnp.bfloat16)
    key_rows = rotate(key_proj.reshape(row_count, kv_count, HD), cosine_table, sine_table).astype(
        jnp.bfloat16
    )
    value_rows = value_proj.astype(jnp.bfloat16).reshape(row_count, kv_count, HD)
    pooled = (
        jnp.dot(onehot.astype(jnp.float32), cached, precision=lax.Precision.HIGHEST)
        / doc_len.astype(jnp.float32)[:, None]
    )
    out_grad = (
        (upstream.astype(jnp.float32) + pooled)
        .astype(jnp.bfloat16)
        .reshape(row_count, head_count, HD)
    )
    key_list = []
    value_list = []
    for distance in range(HOPS, 0, -1):
        earlier_key, earlier_value = from_behind((key_rows, value_rows), "dp", distance)
        key_list.append(earlier_key)
        value_list.append(earlier_value)
    key_window = jnp.concatenate(key_list + [key_rows], axis=0)
    value_window = jnp.concatenate(value_list + [value_rows], axis=0)
    window = key_window.shape[0]
    window_positions = dp_index * row_count - HOPS * row_count + jnp.arange(window, dtype=jnp.int32)
    allowed = block_mask(lengths, own_positions, window_positions)
    head_queries = jnp.transpose(queries, (1, 0, 2))
    head_grads = jnp.transpose(out_grad, (1, 0, 2))
    head_keys = jnp.transpose(jnp.repeat(key_window, group_size, axis=1), (1, 0, 2))
    head_values = jnp.transpose(jnp.repeat(value_window, group_size, axis=1), (1, 0, 2))

    def one_head(operands):
        return attend_head(operands[0], operands[1], operands[2], operands[3], allowed)

    query_grad, key_grad, value_grad, _, _ = lax.map(
        one_head, (head_queries, head_keys, head_values, head_grads)
    )
    key_sum = fold_heads(key_grad, kv_count, group_size)
    value_sum = fold_heads(value_grad, kv_count, group_size)
    own_key = key_sum[HOPS * row_count :]
    own_value = value_sum[HOPS * row_count :]
    for distance in range(1, HOPS + 1):
        lower = (HOPS - distance) * row_count
        back_key, back_value = (
            from_behind(
                key_sum[lower : lower + row_count].astype(jnp.bfloat16), "dp", -distance
            ).astype(jnp.float32),
            from_behind(
                value_sum[lower : lower + row_count].astype(jnp.bfloat16), "dp", -distance
            ).astype(jnp.float32),
        )
        own_key = own_key + back_key
        own_value = own_value + back_value
    query_done = (
        unrotate(jnp.transpose(query_grad, (1, 0, 2)), cosine_table, sine_table)
        .astype(jnp.bfloat16)
        .reshape(row_count, query_cols)
    )
    key_done = (
        unrotate(own_key, cosine_table, sine_table)
        .astype(jnp.bfloat16)
        .reshape(row_count, key_cols)
    )
    value_done = own_value.astype(jnp.bfloat16).reshape(row_count, key_cols)
    portion = (
        contract(query_done, full_query)
        + contract(key_done, full_key)
        + contract(value_done, full_value)
    )
    own_hidden = hidden.astype(jnp.float32)
    own_cols = hidden.shape[1]
    gain_offset = lax.axis_index("tensor") * own_cols
    own_gain = lax.dynamic_slice_in_dim(norm_gain, gain_offset, own_cols, 0)
    normed_grad = lax.psum_scatter(
        portion.astype(jnp.bfloat16), "tensor", scatter_dimension=1, tiled=True
    ).astype(jnp.float32)
    projection = lax.psum(
        jnp.sum(normed_grad * own_gain[None, :] * own_hidden, axis=1, keepdims=True), "tensor"
    )
    grad_hidden = (
        inverse_scale * own_gain[None, :] * normed_grad
        - own_hidden * (inverse_scale * inverse_scale * inverse_scale) * projection / D
    ).astype(jnp.bfloat16)
    grad_wkey = lax.psum_scatter(
        lax.dot_general(
            normed, key_done, (((0,), (0,)), ((), ())), preferred_element_type=jnp.float32
        ),
        "dp",
        scatter_dimension=0,
        tiled=True,
    )
    return (grad_hidden, grad_wkey)


def after(array, *others):
    return lax.optimization_barrier((array, *others))[0]


def norm_kernel(where, near_ref, far_ref, gain_ref, *outs):
    pieces, inv_ref = outs[:-1], outs[-1]
    ring, tensor = where[0], where[2]
    ring_size = len(pieces)
    members = where.shape[0] - 3
    step = pieces[0].shape[1] // members

    def write(ref):
        total = jnp.zeros((ref.shape[2], 1), jnp.float32)
        for half in range(2):
            wide = ref[0, half].astype(jnp.float32)
            total = total + jnp.sum(wide * wide, axis=1, keepdims=True)
        inverse = lax.rsqrt(total / D + EPSILON)
        inv_ref[...] = jnp.broadcast_to(inverse, inv_ref.shape)
        planes_per_half = ring_size // 2
        for s in range(ring_size):
            plane = lax.rem(ring - s + ring_size, ring_size)
            half = lax.rem(plane // planes_per_half + tensor, 2)
            for d in range(members):
                inner = lax.rem(plane, planes_per_half) * (members * step) + where[3 + d] * step
                inner = pl.multiple_of(inner, step)
                outer = pl.multiple_of((plane * members + where[3 + d]) * step, step)
                wide = ref[0, half, :, pl.ds(inner, step)].astype(jnp.float32)
                scaled = wide * inverse * gain_ref[:, pl.ds(outer, step)]
                pieces[s][:, d * step : (d + 1) * step] = scaled.astype(jnp.bfloat16)

    @pl.when(pl.program_id(1) == 0)
    def _():
        write(near_ref)

    @pl.when(pl.program_id(1) == 1)
    def _():
        write(far_ref)


def norm_pieces(where, near, far, gain, ring_size):
    rows, half = near.shape[2], near.shape[3]
    members = where.shape[0] - 3
    tokens = members * rows
    width = 2 * half // ring_size
    spec = pl.BlockSpec((1, 2, rows, half), lambda u, v, w: (u, 0, 0, 0))

    def out_row(u, v, w):
        return (w[3 + 2 * u + v], 0)

    return pl.pallas_call(
        norm_kernel,
        grid_spec=pltpu.PrefetchScalarGridSpec(
            num_scalar_prefetch=1,
            grid=(2, 2),
            in_specs=[spec, spec, pl.BlockSpec((1, 2 * half), lambda u, v, w: (0, 0))],
            out_specs=[pl.BlockSpec((rows, width), out_row)] * ring_size
            + [pl.BlockSpec((rows, 128), out_row)],
        ),
        out_shape=[jax.ShapeDtypeStruct((tokens, width), jnp.bfloat16)] * ring_size
        + [jax.ShapeDtypeStruct((tokens, 128), jnp.float32)],
        compiler_params=pltpu.CompilerParams(vmem_limit_bytes=24 << 20),
        cost_estimate=pl.CostEstimate(
            flops=8 * tokens * 2 * half, bytes_accessed=8 * tokens * half, transcendentals=tokens
        ),
    )(where, near, far, gain)


def attend_kernel(heads, rows, terms, first, q_ref, *refs):
    n_refs, w_refs, refs = refs[:terms], refs[terms : 2 * terms], refs[2 * terms :]
    g_ref, k_ref, kt_ref, v_ref, cos_ref, sin_ref, low_ref = refs[:7]
    before = None if first else refs[7]
    dq_ref, halo_ref, own_ref, dkv_ref = refs[7 if first else 8 :]
    scale = HD ** (-0.5)
    halo = halo_ref.shape[0]
    window = halo + rows
    blocks = q_ref.shape[0] // rows

    @pl.when(pl.program_id(0) == 0)
    def _():
        dkv_ref[...] = jnp.zeros_like(dkv_ref)

    projected = q_ref[...]
    for n_ref, w_ref in zip(n_refs, w_refs):
        projected += jnp.dot(n_ref[...], w_ref[...], preferred_element_type=jnp.float32)
    key_at = lax.broadcasted_iota(jnp.int32, (window, rows), 0)
    query_at = lax.broadcasted_iota(jnp.int32, (rows, rows), 1)
    causal = key_at[:rows] <= query_at
    staged = []
    for block in range(blocks):
        here = slice(block * rows, (block + 1) * rows)
        base = pl.multiple_of((pl.program_id(0) * blocks + block) * rows, rows)
        cosine, sine = cos_ref[here, :], sin_ref[here, :]
        turned = []
        for h in range(heads):
            u = projected[here, h * HD : (h + 1) * HD]
            turned.append((u * cosine + pltpu.roll(u, HD // 2, 1) * sine).astype(jnp.bfloat16))
        queries = jnp.concatenate(turned, axis=0)
        grads = jnp.concatenate([g_ref[here, h * HD : (h + 1) * HD] for h in range(heads)], axis=0)
        scores = contract(k_ref[pl.ds(base, window), :], queries)
        prob_grads = contract(v_ref[pl.ds(base, window), :], grads)
        staged.append((here, base, cosine, sine, queries, grads, scores, prob_grads))
    for here, base, cosine, sine, queries, grads, scores, prob_grads in staged:
        low = low_ref[:, here] - base
        inside = key_at >= low
        allowed = (inside[:halo], inside[halo:] & causal)
        probs, score_grads = [], []
        for h in range(heads):
            there = slice(h * rows, (h + 1) * rows)
            grown = jnp.exp2(scores[:, there] * (scale * LOG2_E))
            weights = jnp.concatenate(
                [
                    jnp.where(allowed[0], grown[:halo], 0.0),
                    jnp.where(allowed[1], grown[halo:], 0.0),
                ],
                axis=0,
            )
            prob_grad = prob_grads[:, there]
            softmax = weights / jnp.sum(weights, axis=0, keepdims=True)
            row_delta = jnp.sum(softmax * prob_grad, axis=0, keepdims=True)
            probs.append(softmax.astype(jnp.bfloat16))
            score_grads.append((softmax * (prob_grad - row_delta)).astype(jnp.bfloat16))
        probs = jnp.concatenate(probs, axis=1)
        score_grads = jnp.concatenate(score_grads, axis=1)
        dkv_ref[pl.ds(base, window), :HD] += (
            jnp.dot(score_grads, queries, preferred_element_type=jnp.float32) * scale
        )
        dkv_ref[pl.ds(base, window), HD:] += jnp.dot(
            probs, grads, preferred_element_type=jnp.float32
        )
        query_grads = jnp.dot(
            kt_ref[:, pl.ds(base, window)], score_grads, preferred_element_type=jnp.float32
        )
        for h in range(heads):
            grad = query_grads[:, h * rows : (h + 1) * rows].T * scale
            back = grad * cosine - pltpu.roll(grad, HD // 2, 1) * sine
            dq_ref[here, h * HD : (h + 1) * HD] = back.astype(jnp.bfloat16)

    @pl.when(pl.program_id(0) == pl.num_programs(0) - 1)
    def _():
        halo_sum = dkv_ref[:halo, :]
        halo_ref[...] = halo_sum if first else (halo_sum + before[...]).astype(jnp.bfloat16)
        own_ref[...] = dkv_ref[halo:, :]


def attend(q_proj, normed, weights, grads, keys, keys_turned, values, cosine, sine, low, before=None):
    tokens, width = q_proj.shape
    heads, rows = width // HD, 128
    step = 2 * rows
    total = keys.shape[0]
    window = total - tokens + rows
    whole = lambda a: pl.BlockSpec(a.shape, lambda i: (0, 0))
    by_rows = lambda w: pl.BlockSpec((step, w), lambda i: (i, 0))
    fixed = lambda n, w: pl.BlockSpec((n, w), lambda i: (0, 0))
    extra = [] if before is None else [before]
    return pl.pallas_call(
        partial(attend_kernel, heads, rows, len(normed), before is None),
        grid=(tokens // step,),
        in_specs=[by_rows(width)]
        + [by_rows(n.shape[1]) for n in normed]
        + [whole(w) for w in weights]
        + [by_rows(width), whole(keys), whole(keys_turned), whole(values)]
        + [by_rows(HD), by_rows(HD), pl.BlockSpec((1, step), lambda i: (0, i))]
        + [fixed(total - tokens, 2 * HD) for _ in extra],
        out_specs=[by_rows(width), fixed(total - tokens, 2 * HD), fixed(tokens, 2 * HD)],
        out_shape=[jax.ShapeDtypeStruct((tokens, width), jnp.bfloat16),
                   jax.ShapeDtypeStruct(
                       (total - tokens, 2 * HD), jnp.float32 if before is None else jnp.bfloat16
                   ),
                   jax.ShapeDtypeStruct((tokens, 2 * HD), jnp.float32)],
        scratch_shapes=[pltpu.VMEM((total, 2 * HD), jnp.float32)],
        cost_estimate=pl.CostEstimate(
            flops=10 * tokens * window * width, bytes_accessed=12 * tokens * width,
            transcendentals=tokens * window * heads,
        ),
    )(q_proj, *normed, *weights, grads, keys, keys_turned, values, cosine, sine, low, *extra)


def spread_blocks(where, wide, grads, rows):
    members = where.shape[0] - 3
    for block in range(members):
        partner = (block % (members // 2)) * 2 + block // (members // 2)
        source = pl.multiple_of(where[3 + partner] * rows, rows)
        at = 0
        for grad in grads:
            wide[block * rows : (block + 1) * rows, at : at + grad.shape[1]] = grad[
                pl.ds(source, rows), :
            ]
            at += grad.shape[1]


def spread_first_kernel(counts, ring_size, where, *refs):
    grads, weights = refs[: counts[0]], refs[counts[0] : counts[0] + counts[1] * ring_size]
    out_ref, wide, held, arrived = refs[counts[0] + counts[1] * ring_size :]
    members = where.shape[0] - 3
    step = held.shape[1] // members
    s = pl.program_id(0)

    def copy(source, piece, c):
        width = source.shape[1]
        return pltpu.make_async_copy(
            source, held.at[piece, :, pl.ds(c * width, width)], arrived.at[piece, c]
        )

    @pl.when(s == 0)
    def _():
        for piece in range(ring_size):
            for c in range(counts[1]):
                copy(weights[c * ring_size + piece], piece, c).start()
        spread_blocks(where, wide, grads, wide.shape[0] // members)

    for c in range(counts[1]):
        copy(weights[c * ring_size], s, c).wait()
    for owner in range(members):
        source = pl.multiple_of(where[3 + owner] * step, step)
        out_ref[0, :, owner * step : (owner + 1) * step] = contract(
            wide[...], held[s, pl.ds(source, step), :]
        )


def spread_first(where, grads, weights, ring_size):
    tokens = grads[0].shape[0]
    depth = sum(a.shape[1] for a in grads)
    width = weights[0].shape[0]
    chunks = len(weights) // ring_size
    return pl.pallas_call(
        partial(spread_first_kernel, (len(grads), chunks), ring_size),
        grid_spec=pltpu.PrefetchScalarGridSpec(
            num_scalar_prefetch=1,
            grid=(ring_size,),
            in_specs=[pl.BlockSpec(a.shape, lambda i, w: (0, 0)) for a in grads]
            + [pl.BlockSpec(memory_space=pltpu.HBM) for _ in weights],
            out_specs=pl.BlockSpec((1, tokens, width), lambda i, w: (i, 0, 0)),
            scratch_shapes=[
                pltpu.VMEM((tokens, depth), jnp.bfloat16),
                pltpu.VMEM((ring_size, width, depth), jnp.bfloat16),
                pltpu.SemaphoreType.DMA((ring_size, chunks)),
            ],
        ),
        out_shape=jax.ShapeDtypeStruct((ring_size, tokens, width), jnp.float32),
        compiler_params=pltpu.CompilerParams(vmem_limit_bytes=24 << 20),
        cost_estimate=pl.CostEstimate(
            flops=2 * tokens * width * ring_size * depth,
            bytes_accessed=4 * tokens * width * ring_size,
            transcendentals=0,
        ),
    )(where, *grads, *weights)


def spread_last_kernel(parts, where, so_far, *refs):
    owns, (back_ref, cos_ref, sin_ref) = refs[:parts], refs[parts : parts + 3]
    weights = refs[parts + 3 : -4]
    key_ref, keep_ref, send_ref, wide = refs[-4:]
    members = where.shape[0] - 3
    step = weights[0].shape[0] // members
    rows = keep_ref.shape[2]
    s = pl.program_id(0)

    @pl.when(s == 0)
    def _():
        for block in range(members):
            partner = (block % (members // 2)) * 2 + block // (members // 2)
            lines = pl.ds(pl.multiple_of(where[3 + partner] * rows, rows), rows)
            grad = back_ref[lines, :].astype(jnp.float32)
            for own in owns:
                grad += own[lines, :]
            key_grad = grad[:, :HD]
            turned = pltpu.roll(key_grad, HD // 2, 1)
            key_done = key_grad * cos_ref[lines, :] - turned * sin_ref[lines, :]
            key_ref[lines, :] = key_done.astype(jnp.bfloat16)
            here = slice(block * rows, (block + 1) * rows)
            wide[here, :HD] = key_done.astype(jnp.bfloat16)
            wide[here, HD:] = grad[:, HD:].astype(jnp.bfloat16)

    for piece, weight in enumerate(weights):

        @pl.when(s == piece)
        def _():
            for owner in range(members):
                source = pl.multiple_of(where[3 + owner] * step, step)
                lanes = slice(owner * step, (owner + 1) * step)
                total = so_far[0, :, lanes] + contract(wide[...], weight[pl.ds(source, step), :])
                total = total.astype(jnp.bfloat16)
                for u in range(members // 2):
                    keep_ref[u, 0, :, lanes] = total[u * rows : (u + 1) * rows, :]
                    lower = (members // 2 + u) * rows
                    send_ref[u, 0, :, lanes] = total[lower : lower + rows, :]


def spread_last(where, so_far, owns, back, cosine, sine, weights, ring_size):
    tokens = back.shape[0]
    members = where.shape[0] - 3
    rows = tokens // members
    width = weights[0].shape[0]
    planes_per_half = ring_size // 2
    whole = lambda a: pl.BlockSpec(a.shape, lambda i, w: (0, 0))

    def out_at(s, w):
        plane = lax.rem(w[0] - s + ring_size, ring_size)
        half = lax.rem(plane // planes_per_half + w[2], 2)
        return (0, half, 0, lax.rem(plane, planes_per_half))

    shape = (members // 2, 2, rows, width * planes_per_half)
    small = [*owns, back, cosine, sine]
    return pl.pallas_call(
        partial(spread_last_kernel, len(owns)),
        grid_spec=pltpu.PrefetchScalarGridSpec(
            num_scalar_prefetch=1,
            grid=(ring_size,),
            in_specs=[pl.BlockSpec((1, tokens, width), lambda i, w: (i, 0, 0))]
            + [whole(a) for a in small]
            + [pl.BlockSpec(memory_space=pltpu.VMEM) for a in weights],
            out_specs=[pl.BlockSpec((tokens, HD), lambda i, w: (0, 0))]
            + [pl.BlockSpec((members // 2, 1, rows, width), out_at)] * 2,
            scratch_shapes=[pltpu.VMEM((tokens, 2 * HD), jnp.bfloat16)],
        ),
        out_shape=[jax.ShapeDtypeStruct((tokens, HD), jnp.bfloat16)]
        + [jax.ShapeDtypeStruct(shape, jnp.bfloat16)] * 2,
        compiler_params=pltpu.CompilerParams(vmem_limit_bytes=28 << 20),
        cost_estimate=pl.CostEstimate(
            flops=4 * tokens * width * ring_size * HD,
            bytes_accessed=4 * tokens * width * ring_size,
            transcendentals=0,
        ),
    )(where, so_far, *small, *weights)


def key_weights_kernel(ring_size, where, *refs):
    members = where.shape[0] - 3
    normed, grads = refs[:ring_size], refs[ring_size : ring_size + members]
    out_refs, wide = refs[ring_size + members : -1], refs[-1]
    width = grads[0].shape[1]
    for owner in range(members):
        for d in range(members):

            @pl.when(where[3 + owner] == d)
            def _():
                wide[:, owner * width : (owner + 1) * width] = grads[d][...]

    for n_ref, out_ref in zip(normed, out_refs):
        out_ref[...] = lax.dot_general(
            n_ref[...], wide[...], (((0,), (0,)), ((), ())), preferred_element_type=jnp.float32
        ).astype(out_ref.dtype)


def key_weights(where, normed, grads, rows):
    tokens, members = grads[0].shape[0], len(grads)
    width = members * grads[0].shape[1]
    shape = (rows, width)
    return pl.pallas_call(
        partial(key_weights_kernel, len(normed)),
        grid_spec=pltpu.PrefetchScalarGridSpec(
            num_scalar_prefetch=1,
            grid=(1,),
            in_specs=[pl.BlockSpec((tokens, rows), lambda i, w: (0, 0)) for _ in normed]
            + [pl.BlockSpec(g.shape, lambda i, w: (0, 0)) for g in grads],
            out_specs=[pl.BlockSpec(shape, lambda i, w: (0, 0))] * len(normed),
            scratch_shapes=[pltpu.VMEM((tokens, width), jnp.bfloat16)],
        ),
        out_shape=[jax.ShapeDtypeStruct(shape, jnp.float32)]
        + [jax.ShapeDtypeStruct(shape, jnp.bfloat16)] * (len(normed) - 1),
        compiler_params=pltpu.CompilerParams(vmem_limit_bytes=16 << 20),
        cost_estimate=pl.CostEstimate(
            flops=2 * tokens * width * rows * len(normed),
            bytes_accessed=2 * tokens * (width + rows * len(normed)),
            transcendentals=0,
        ),
    )(where, *normed, *grads)


def grouped_device(hidden, norm_gain, w_query, w_key, w_value, upstream, cached, lengths):
    rows, half = hidden.shape
    kv_count = w_key.shape[1] // HD
    query_width = w_query.shape[1] // kv_count
    members = kv_count
    devices, tensors = lax.axis_size("dp"), lax.axis_size("tensor")
    ring_size = devices // members
    tokens = members * rows
    weight_rows = w_key.shape[0]
    me, tensor = lax.axis_index("dp"), lax.axis_index("tensor")
    ring, group = me // members, me % members
    partners = [jnp.bitwise_xor(group, d) for d in range(members)]
    where = jnp.stack([ring, group, tensor] + partners).astype(jnp.int32)

    def to_partner(block, d):
        return lax.ppermute(block, "dp", [(i, i ^ d) for i in range(devices)])

    def to_side(block):
        return lax.ppermute(block, "tensor", [(i, i ^ 1) for i in range(tensors)])

    def along(block, distance):
        route = [(i, (i + distance * members) % devices) for i in range(devices)]
        return lax.ppermute(block, "dp", route)

    def columns(array, owner, width):
        return lax.dynamic_slice_in_dim(array, owner * width, width, 1)

    def circulate(own, gate=None):
        pieces = [own]
        for hop in range(1, ring_size):
            block = pieces[-1] if gate is None else gate(hop, pieces[-1])
            pieces.append(along(block, 1))
        return pieces

    k_ring, v_ring = circulate(w_key), circulate(w_value)

    def pack_q(owner):
        return jnp.concatenate(
            [columns(w_query, owner, query_width), columns(upstream, owner, query_width)], axis=0
        )

    q_parts = [pack_q(group)] + [to_partner(pack_q(partners[d]), d) for d in range(1, members)]
    q_own = jnp.concatenate([p[:weight_rows] for p in q_parts], axis=0)
    ends = [sum(CHUNKS[: c + 1]) * HD for c in range(len(CHUNKS))]
    spans = [slice(end - count * HD, end) for end, count in zip(ends, CHUNKS)]
    q_chunk = [q_own[:, span] for span in spans]

    def pack_kv(owner):
        pairs = []
        for k, v in zip(k_ring, v_ring):
            cut = [columns(k, owner, HD), columns(v, owner, HD)]
            pairs.append(lax.optimization_barrier(jnp.concatenate(cut, axis=1)))
        return jnp.concatenate(pairs, axis=0)

    across = to_partner(hidden, 2)
    beside = to_side(hidden)
    corner = to_side(across)
    near = jnp.stack([hidden, beside, across, corner]).reshape(2, 2, rows, half)
    far = to_partner(near, 1)
    *normed, inverse = norm_pieces(where, near, far, norm_gain[None, :], ring_size)

    kv_parts = [pack_kv(group)] + [
        after(to_partner(pack_kv(partners[d]), d), normed[0])
        for d in range(1, members)
    ]
    kv_pieces = [
        jnp.concatenate([p[s * weight_rows : (s + 1) * weight_rows] for p in kv_parts], axis=0)
        for s in range(ring_size)
    ]

    def project(pieces):
        total = None
        for s, piece in enumerate(pieces):
            term = jnp.dot(normed[s], piece, preferred_element_type=jnp.float32)
            total = term if total is None else total + term
        return total

    first = ring * tokens
    token_positions = first + jnp.arange(tokens, dtype=jnp.int32)
    _, doc_len, positions, onehot = document_info(lengths, token_positions)
    cosine, sine = rope_tables(positions)
    sign = jnp.where(jnp.arange(HD) < HD // 2, -1.0, 1.0).astype(jnp.float32)
    sine = sine * sign[None, :]
    low = (token_positions - positions - first + LONGEST)[None, :]

    def place(parts):
        stacked = jnp.stack(parts)
        return [
            lax.dynamic_index_in_dim(stacked, jnp.bitwise_xor(group, o), 0, keepdims=False)
            for o in range(members)
        ]

    up_own = jnp.concatenate(place([p[weight_rows:] for p in q_parts]), axis=0)
    pooled = (
        jnp.dot(
            onehot.astype(jnp.float32),
            columns(cached, group, query_width),
            precision=lax.Precision.HIGHEST,
        )
        / doc_len.astype(jnp.float32)[:, None]
    )
    out_grad = (up_own.astype(jnp.float32) + pooled).astype(jnp.bfloat16)

    kv_proj = project(kv_pieces)
    key_proj = kv_proj[:, :HD]
    key_own = key_proj * cosine + jnp.roll(key_proj, HD // 2, axis=1) * sine
    kv_rows = jnp.concatenate([key_own, kv_proj[:, HD:]], axis=1).astype(jnp.bfloat16)

    q_pieces = []
    for c in range(len(CHUNKS)):
        gate = lambda hop, block, c=c: after(block, kv_rows) if c and hop == ring_size - 1 else block
        q_pieces.append(circulate(q_chunk[c], gate))
    halo = lax.ppermute(kv_rows, "dp", [(i, i + members) for i in range(devices - members)])
    kv_all = jnp.concatenate([halo, kv_rows], axis=0)
    keys, values = kv_all[:, :HD], kv_all[:, HD:]
    keys_turned = keys.T
    query_dones, owns, halo_grad = [], [], None
    for c in range(len(CHUNKS)):
        early = lax.optimization_barrier(project(q_pieces[c][:-1]))
        query_done, halo_grad, own_grad = attend(
            early, normed[-1:], q_pieces[c][-1:],
            out_grad[:, spans[c]],
            keys, keys_turned, values, cosine, sine, low, halo_grad,
        )
        query_dones.append(query_done)
        owns.append(own_grad)
    later = [(i + members, i) for i in range(devices - members)]
    back = lax.ppermute(halo_grad, "dp", later)

    weights = [
        pltpu.with_memory_space_constraint(piece, pltpu.HBM)
        for pieces in q_pieces
        for piece in pieces
    ]
    so_far = spread_first(where, query_dones, weights, ring_size)
    in_hbm = [pltpu.with_memory_space_constraint(a, pltpu.HBM) for a in (*owns, cosine, sine)]
    key_done, keep, send = spread_last(
        where, so_far, in_hbm[:-2], back, *in_hbm[-2:], kv_pieces, ring_size
    )

    key_dones = [key_done] + [to_partner(key_done, d) for d in range(1, members)]
    grad_wkey, *others = key_weights(where, normed, key_dones, weight_rows)
    for s in range(1, ring_size):
        term = along(others[s - 1], -s)
        grad_wkey = grad_wkey + term.astype(jnp.float32)

    wide = lambda a: a.astype(jnp.float32)
    narrow = lambda a: a.astype(jnp.bfloat16)
    other = to_partner(send, 1)
    both = lambda *at: wide(keep[at]) + wide(other[at])
    cut = half // 2
    low_cut, high_cut, every = slice(0, cut), slice(cut, half), slice(None)
    left_half = narrow(both(1, every, every, low_cut))
    right_half = narrow(both(every, 1, every, high_cut))
    left_half = to_partner(left_half, 2)
    right_half = to_side(right_half)
    left = both(0, every, every, low_cut) + wide(left_half)
    right = both(every, 0, every, high_cut) + wide(right_half)
    left_sum = left[0] + wide(to_side(narrow(left[1])))
    right_sum = right[0] + wide(to_partner(narrow(right[1]), 2))
    normed_grad = jnp.concatenate([left_sum, right_sum], axis=1)
    own_hidden = wide(hidden)
    own_gain = lax.dynamic_slice_in_dim(norm_gain, tensor * half, half, 0)
    own_inverse = lax.dynamic_slice_in_dim(inverse, group * rows, rows, 0)[:, :1]
    part = jnp.sum(normed_grad * own_gain[None, :] * own_hidden, axis=1)[None, :]
    projection = (part + to_side(part)).reshape(rows, 1)
    grad_hidden = (
        own_inverse * own_gain[None, :] * normed_grad
        - own_hidden * (own_inverse * own_inverse * own_inverse) * projection / D
    ).astype(jnp.bfloat16)
    return (grad_hidden, grad_wkey)


def is_grouped(mesh_shape, rows, key_columns):
    members = key_columns // HD
    return (
        mesh_shape["tensor"] == 2
        and members == 4
        and mesh_shape["dp"] == 4 * members
        and members * rows == LONGEST
    )


def per_device(hidden, norm_gain, w_query, w_key, w_value, upstream, cached, lengths):
    arrays = (hidden, norm_gain, w_query, w_key, w_value, upstream, cached, lengths)
    sizes = {axis: lax.axis_size(axis) for axis in ("dp", "tensor")}
    if not is_grouped(sizes, hidden.shape[0], w_key.shape[1]):
        return plain_device(*arrays)
    return grouped_device(*arrays)


def solution(mesh):
    placed = (
        P("dp", "tensor"),
        P(),
        P("dp", "tensor"),
        P("dp", "tensor"),
        P("dp", "tensor"),
        P("dp", "tensor"),
        P(None, "tensor"),
        P(),
    )
    return jax.shard_map(
        per_device,
        mesh=mesh,
        in_specs=placed,
        out_specs=(P("dp", "tensor"), P("dp", "tensor")),
        check_vma=False,
    )
```

```python
from functools import partial

import jax
import jax.numpy as jnp
from jax import lax
from jax.experimental import pallas as pl
from jax.experimental.pallas import tpu as pltpu
from jax.sharding import PartitionSpec as P


D = 4096
HD = 128
HOPS = 4
LONGEST = 512
CHUNKS = (2, 2)


EPSILON = 1e-05
LOG2_E = 1.4426950408889634
ROPE_BASE = 500000.0


def from_behind(block, axis, distance):
    devices = range(lax.axis_size(axis))
    route = [(i - distance, i) for i in devices if i - distance in devices]
    return lax.ppermute(block, axis, route)


def document_info(lengths, positions_global):
    doc_ends = jnp.cumsum(lengths)
    documents = jnp.sum((positions_global[:, None] >= doc_ends[None, :]).astype(jnp.int32), axis=1)
    doc_slots = jnp.arange(lengths.shape[0], dtype=jnp.int32)
    onehot = documents[:, None] == doc_slots[None, :]
    doc_len = jnp.sum(jnp.where(onehot, lengths[None, :], 0), axis=1)
    doc_end = jnp.sum(jnp.where(onehot, doc_ends[None, :], 0), axis=1)
    return (documents, doc_len, positions_global - doc_end + doc_len, onehot)


def block_mask(lengths, query_positions, key_positions):
    query_docs = document_info(lengths, query_positions)[0]
    key_docs = document_info(lengths, key_positions)[0]
    return (
        (key_positions[None, :] >= 0)
        & (key_docs[None, :] == query_docs[:, None])
        & (key_positions[None, :] <= query_positions[:, None])
    )


def rope_tables(positions):
    half_width = HD // 2
    frequency = ROPE_BASE ** (-(jnp.arange(half_width, dtype=jnp.float32) * 2.0 / HD))
    angles = positions.astype(jnp.float32)[:, None] * frequency[None, :]
    angles = jnp.concatenate([angles, angles], axis=1)
    return (jnp.cos(angles), jnp.sin(angles))


def rotate(values, cosine_table, sine_table):
    half_width = values.shape[-1] // 2
    turned = jnp.concatenate([-values[..., half_width:], values[..., :half_width]], axis=-1)
    return values * cosine_table[:, None, :] + turned * sine_table[:, None, :]


def unrotate(gradient, cosine_table, sine_table):
    half_width = gradient.shape[-1] // 2
    scaled = gradient * sine_table[:, None, :]
    back_part = jnp.concatenate([scaled[..., half_width:], -scaled[..., :half_width]], axis=-1)
    return gradient * cosine_table[:, None, :] + back_part


def contract(left, right):
    return lax.dot_general(
        left, right, (((1,), (1,)), ((), ())), preferred_element_type=jnp.float32
    )


def attend_head(queries, key_rows, value_rows, out_grad, allowed):
    score_scale = HD ** (-0.5)
    scores = contract(queries, key_rows) * score_scale
    weights = jnp.where(allowed, jnp.exp(scores), 0.0)
    totals = jnp.sum(weights, axis=1, keepdims=True)
    softmax = weights / totals
    prob_grad = contract(out_grad, value_rows)
    row_delta = jnp.sum(softmax * prob_grad, axis=1, keepdims=True)
    score_grad = (softmax * (prob_grad - row_delta)).astype(jnp.bfloat16)
    query_grad = jnp.dot(score_grad, key_rows, preferred_element_type=jnp.float32) * score_scale
    key_grad = (
        lax.dot_general(
            score_grad, queries, (((0,), (0,)), ((), ())), preferred_element_type=jnp.float32
        )
        * score_scale
    )
    value_grad = lax.dot_general(
        softmax.astype(jnp.bfloat16),
        out_grad,
        (((0,), (0,)), ((), ())),
        preferred_element_type=jnp.float32,
    )
    return (query_grad, key_grad, value_grad, totals, row_delta)


def fold_heads(per_head, kv_count, group_size):
    summed = per_head.reshape(kv_count, group_size, per_head.shape[1], HD).sum(axis=1)
    return jnp.transpose(summed, (1, 0, 2))


def plain_device(hidden, norm_gain, w_query, w_key, w_value, upstream, cached, lengths):
    gathered = lax.all_gather(hidden, "tensor", axis=1, tiled=True)
    row_count = gathered.shape[0]
    query_cols = w_query.shape[1]
    key_cols = w_key.shape[1]
    head_count = query_cols // HD
    kv_count = key_cols // HD
    group_size = head_count // kv_count
    hidden_wide = gathered.astype(jnp.float32)
    inverse_scale = lax.rsqrt(jnp.mean(hidden_wide * hidden_wide, axis=1, keepdims=True) + EPSILON)
    normed = (hidden_wide * inverse_scale * norm_gain[None, :]).astype(jnp.bfloat16)
    dp_index = lax.axis_index("dp")
    own_positions = dp_index * row_count + jnp.arange(row_count, dtype=jnp.int32)
    _, doc_len, positions, onehot = document_info(lengths, own_positions)
    cosine_table, sine_table = rope_tables(positions)
    full_query, full_key, full_value = (
        lax.all_gather(w_query, "dp", axis=0, tiled=True),
        lax.all_gather(w_key, "dp", axis=0, tiled=True),
        lax.all_gather(w_value, "dp", axis=0, tiled=True),
    )
    query_proj = jnp.dot(normed, full_query, preferred_element_type=jnp.float32)
    key_proj = jnp.dot(normed, full_key, preferred_element_type=jnp.float32)
    value_proj = jnp.dot(normed, full_value, preferred_element_type=jnp.float32)
    queries = rotate(
        query_proj.reshape(row_count, head_count, HD), cosine_table, sine_table
    ).astype(jnp.bfloat16)
    key_rows = rotate(key_proj.reshape(row_count, kv_count, HD), cosine_table, sine_table).astype(
        jnp.bfloat16
    )
    value_rows = value_proj.astype(jnp.bfloat16).reshape(row_count, kv_count, HD)
    pooled = (
        jnp.dot(onehot.astype(jnp.float32), cached, precision=lax.Precision.HIGHEST)
        / doc_len.astype(jnp.float32)[:, None]
    )
    out_grad = (
        (upstream.astype(jnp.float32) + pooled)
        .astype(jnp.bfloat16)
        .reshape(row_count, head_count, HD)
    )
    key_list = []
    value_list = []
    for distance in range(HOPS, 0, -1):
        earlier_key, earlier_value = from_behind((key_rows, value_rows), "dp", distance)
        key_list.append(earlier_key)
        value_list.append(earlier_value)
    key_window = jnp.concatenate(key_list + [key_rows], axis=0)
    value_window = jnp.concatenate(value_list + [value_rows], axis=0)
    window = key_window.shape[0]
    window_positions = dp_index * row_count - HOPS * row_count + jnp.arange(window, dtype=jnp.int32)
    allowed = block_mask(lengths, own_positions, window_positions)
    head_queries = jnp.transpose(queries, (1, 0, 2))
    head_grads = jnp.transpose(out_grad, (1, 0, 2))
    head_keys = jnp.transpose(jnp.repeat(key_window, group_size, axis=1), (1, 0, 2))
    head_values = jnp.transpose(jnp.repeat(value_window, group_size, axis=1), (1, 0, 2))

    def one_head(operands):
        return attend_head(operands[0], operands[1], operands[2], operands[3], allowed)

    query_grad, key_grad, value_grad, _, _ = lax.map(
        one_head, (head_queries, head_keys, head_values, head_grads)
    )
    key_sum = fold_heads(key_grad, kv_count, group_size)
    value_sum = fold_heads(value_grad, kv_count, group_size)
    own_key = key_sum[HOPS * row_count :]
    own_value = value_sum[HOPS * row_count :]
    for distance in range(1, HOPS + 1):
        lower = (HOPS - distance) * row_count
        back_key, back_value = (
            from_behind(
                key_sum[lower : lower + row_count].astype(jnp.bfloat16), "dp", -distance
            ).astype(jnp.float32),
            from_behind(
                value_sum[lower : lower + row_count].astype(jnp.bfloat16), "dp", -distance
            ).astype(jnp.float32),
        )
        own_key = own_key + back_key
        own_value = own_value + back_value
    query_done = (
        unrotate(jnp.transpose(query_grad, (1, 0, 2)), cosine_table, sine_table)
        .astype(jnp.bfloat16)
        .reshape(row_count, query_cols)
    )
    key_done = (
        unrotate(own_key, cosine_table, sine_table)
        .astype(jnp.bfloat16)
        .reshape(row_count, key_cols)
    )
    value_done = own_value.astype(jnp.bfloat16).reshape(row_count, key_cols)
    portion = (
        contract(query_done, full_query)
        + contract(key_done, full_key)
        + contract(value_done, full_value)
    )
    own_hidden = hidden.astype(jnp.float32)
    own_cols = hidden.shape[1]
    gain_offset = lax.axis_index("tensor") * own_cols
    own_gain = lax.dynamic_slice_in_dim(norm_gain, gain_offset, own_cols, 0)
    normed_grad = lax.psum_scatter(
        portion.astype(jnp.bfloat16), "tensor", scatter_dimension=1, tiled=True
    ).astype(jnp.float32)
    projection = lax.psum(
        jnp.sum(normed_grad * own_gain[None, :] * own_hidden, axis=1, keepdims=True), "tensor"
    )
    grad_hidden = (
        inverse_scale * own_gain[None, :] * normed_grad
        - own_hidden * (inverse_scale * inverse_scale * inverse_scale) * projection / D
    ).astype(jnp.bfloat16)
    grad_wkey = lax.psum_scatter(
        lax.dot_general(
            normed, key_done, (((0,), (0,)), ((), ())), preferred_element_type=jnp.float32
        ),
        "dp",
        scatter_dimension=0,
        tiled=True,
    )
    return (grad_hidden, grad_wkey)


def after(array, *others):
    return lax.optimization_barrier((array, *others))[0]


def norm_kernel(where, near_ref, far_ref, gain_ref, *outs):
    pieces, inv_ref = outs[:-1], outs[-1]
    ring, tensor = where[0], where[2]
    ring_size = len(pieces)
    members = where.shape[0] - 3
    step = pieces[0].shape[1] // members

    def write(ref):
        total = jnp.zeros((ref.shape[2], 1), jnp.float32)
        for half in range(2):
            wide = ref[0, half].astype(jnp.float32)
            total = total + jnp.sum(wide * wide, axis=1, keepdims=True)
        inverse = lax.rsqrt(total / D + EPSILON)
        inv_ref[...] = jnp.broadcast_to(inverse, inv_ref.shape)
        planes_per_half = ring_size // 2
        for s in range(ring_size):
            plane = lax.rem(ring - s + ring_size, ring_size)
            half = lax.rem(plane // planes_per_half + tensor, 2)
            for d in range(members):
                inner = lax.rem(plane, planes_per_half) * (members * step) + where[3 + d] * step
                inner = pl.multiple_of(inner, step)
                outer = pl.multiple_of((plane * members + where[3 + d]) * step, step)
                wide = ref[0, half, :, pl.ds(inner, step)].astype(jnp.float32)
                scaled = wide * inverse * gain_ref[:, pl.ds(outer, step)]
                pieces[s][:, d * step : (d + 1) * step] = scaled.astype(jnp.bfloat16)

    @pl.when(pl.program_id(1) == 0)
    def _():
        write(near_ref)

    @pl.when(pl.program_id(1) == 1)
    def _():
        write(far_ref)


def norm_pieces(where, near, far, gain, ring_size):
    rows, half = near.shape[2], near.shape[3]
    members = where.shape[0] - 3
    tokens = members * rows
    width = 2 * half // ring_size
    spec = pl.BlockSpec((1, 2, rows, half), lambda u, v, w: (u, 0, 0, 0))

    def out_row(u, v, w):
        return (w[3 + 2 * u + v], 0)

    return pl.pallas_call(
        norm_kernel,
        grid_spec=pltpu.PrefetchScalarGridSpec(
            num_scalar_prefetch=1,
            grid=(2, 2),
            in_specs=[spec, spec, pl.BlockSpec((1, 2 * half), lambda u, v, w: (0, 0))],
            out_specs=[pl.BlockSpec((rows, width), out_row)] * ring_size
            + [pl.BlockSpec((rows, 128), out_row)],
        ),
        out_shape=[jax.ShapeDtypeStruct((tokens, width), jnp.bfloat16)] * ring_size
        + [jax.ShapeDtypeStruct((tokens, 128), jnp.float32)],
        compiler_params=pltpu.CompilerParams(vmem_limit_bytes=14 << 20),
        cost_estimate=pl.CostEstimate(
            flops=8 * tokens * 2 * half, bytes_accessed=8 * tokens * half, transcendentals=tokens
        ),
    )(where, near, far, gain)


def attend_kernel(heads, rows, terms, first, q_ref, *refs):
    n_refs, w_refs, refs = refs[:terms], refs[terms : 2 * terms], refs[2 * terms :]
    g_ref, k_ref, kt_ref, v_ref, cos_ref, sin_ref, low_ref = refs[:7]
    before = None if first else refs[7]
    dq_ref, halo_ref, own_ref, dkv_ref = refs[7 if first else 8 :]
    scale = HD ** (-0.5)
    halo = halo_ref.shape[0]
    window = halo + rows
    blocks = q_ref.shape[0] // rows

    @pl.when(pl.program_id(0) == 0)
    def _():
        dkv_ref[...] = jnp.zeros_like(dkv_ref)

    projected = q_ref[...]
    for n_ref, w_ref in zip(n_refs, w_refs):
        projected += jnp.dot(n_ref[...], w_ref[...], preferred_element_type=jnp.float32)
    key_at = lax.broadcasted_iota(jnp.int32, (window, rows), 0)
    query_at = lax.broadcasted_iota(jnp.int32, (rows, rows), 1)
    causal = key_at[:rows] <= query_at
    staged = []
    for block in range(blocks):
        here = slice(block * rows, (block + 1) * rows)
        base = pl.multiple_of((pl.program_id(0) * blocks + block) * rows, rows)
        cosine, sine = cos_ref[here, :], sin_ref[here, :]
        turned = []
        for h in range(heads):
            u = projected[here, h * HD : (h + 1) * HD]
            turned.append((u * cosine + pltpu.roll(u, HD // 2, 1) * sine).astype(jnp.bfloat16))
        queries = jnp.concatenate(turned, axis=0)
        grads = jnp.concatenate([g_ref[here, h * HD : (h + 1) * HD] for h in range(heads)], axis=0)
        scores = contract(k_ref[pl.ds(base, window), :], queries)
        prob_grads = contract(v_ref[pl.ds(base, window), :], grads)
        staged.append((here, base, cosine, sine, queries, grads, scores, prob_grads))
    for here, base, cosine, sine, queries, grads, scores, prob_grads in staged:
        low = low_ref[:, here] - base
        inside = key_at >= low
        allowed = (inside[:halo], inside[halo:] & causal)
        probs, score_grads = [], []
        for h in range(heads):
            there = slice(h * rows, (h + 1) * rows)
            grown = jnp.exp2(scores[:, there] * (scale * LOG2_E))
            weights = jnp.concatenate(
                [
                    jnp.where(allowed[0], grown[:halo], 0.0),
                    jnp.where(allowed[1], grown[halo:], 0.0),
                ],
                axis=0,
            )
            prob_grad = prob_grads[:, there]
            softmax = weights / jnp.sum(weights, axis=0, keepdims=True)
            row_delta = jnp.sum(softmax * prob_grad, axis=0, keepdims=True)
            probs.append(softmax.astype(jnp.bfloat16))
            score_grads.append((softmax * (prob_grad - row_delta)).astype(jnp.bfloat16))
        probs = jnp.concatenate(probs, axis=1)
        score_grads = jnp.concatenate(score_grads, axis=1)
        dkv_ref[pl.ds(base, window), :HD] += (
            jnp.dot(score_grads, queries, preferred_element_type=jnp.float32) * scale
        )
        dkv_ref[pl.ds(base, window), HD:] += jnp.dot(
            probs, grads, preferred_element_type=jnp.float32
        )
        query_grads = jnp.dot(
            kt_ref[:, pl.ds(base, window)], score_grads, preferred_element_type=jnp.float32
        )
        for h in range(heads):
            grad = query_grads[:, h * rows : (h + 1) * rows].T * scale
            back = grad * cosine - pltpu.roll(grad, HD // 2, 1) * sine
            dq_ref[here, h * HD : (h + 1) * HD] = back.astype(jnp.bfloat16)

    @pl.when(pl.program_id(0) == pl.num_programs(0) - 1)
    def _():
        halo_sum = dkv_ref[:halo, :]
        halo_ref[...] = halo_sum if first else (halo_sum + before[...]).astype(jnp.bfloat16)
        own_ref[...] = dkv_ref[halo:, :]


def attend(q_proj, normed, weights, grads, keys, keys_turned, values, cosine, sine, low, before=None):
    tokens, width = q_proj.shape
    heads, rows = width // HD, 128
    step = 2 * rows
    total = keys.shape[0]
    window = total - tokens + rows
    whole = lambda a: pl.BlockSpec(a.shape, lambda i: (0, 0))
    by_rows = lambda w: pl.BlockSpec((step, w), lambda i: (i, 0))
    fixed = lambda n, w: pl.BlockSpec((n, w), lambda i: (0, 0))
    extra = [] if before is None else [before]
    return pl.pallas_call(
        partial(attend_kernel, heads, rows, len(normed), before is None),
        grid=(tokens // step,),
        in_specs=[by_rows(width)]
        + [by_rows(n.shape[1]) for n in normed]
        + [whole(w) for w in weights]
        + [by_rows(width), whole(keys), whole(keys_turned), whole(values)]
        + [by_rows(HD), by_rows(HD), pl.BlockSpec((1, step), lambda i: (0, i))]
        + [fixed(total - tokens, 2 * HD) for _ in extra],
        out_specs=[by_rows(width), fixed(total - tokens, 2 * HD), fixed(tokens, 2 * HD)],
        out_shape=[jax.ShapeDtypeStruct((tokens, width), jnp.bfloat16),
                   jax.ShapeDtypeStruct(
                       (total - tokens, 2 * HD), jnp.float32 if before is None else jnp.bfloat16
                   ),
                   jax.ShapeDtypeStruct((tokens, 2 * HD), jnp.float32)],
        scratch_shapes=[pltpu.VMEM((total, 2 * HD), jnp.float32)],
        cost_estimate=pl.CostEstimate(
            flops=10 * tokens * window * width, bytes_accessed=12 * tokens * width,
            transcendentals=tokens * window * heads,
        ),
    )(q_proj, *normed, *weights, grads, keys, keys_turned, values, cosine, sine, low, *extra)


def spread_blocks(where, wide, grads, rows):
    members = where.shape[0] - 3
    for block in range(members):
        partner = (block % (members // 2)) * 2 + block // (members // 2)
        source = pl.multiple_of(where[3 + partner] * rows, rows)
        at = 0
        for grad in grads:
            wide[block * rows : (block + 1) * rows, at : at + grad.shape[1]] = grad[
                pl.ds(source, rows), :
            ]
            at += grad.shape[1]


def spread_first_kernel(counts, ring_size, where, *refs):
    grads, weights = refs[: counts[0]], refs[counts[0] : counts[0] + counts[1] * ring_size]
    out_ref, wide, held, arrived = refs[counts[0] + counts[1] * ring_size :]
    members = where.shape[0] - 3
    step = held.shape[1] // members
    s = pl.program_id(0)

    def copy(source, piece, c):
        width = source.shape[1]
        return pltpu.make_async_copy(
            source, held.at[piece, :, pl.ds(c * width, width)], arrived.at[piece, c]
        )

    @pl.when(s == 0)
    def _():
        for piece in range(ring_size):
            for c in range(counts[1]):
                copy(weights[c * ring_size + piece], piece, c).start()
        spread_blocks(where, wide, grads, wide.shape[0] // members)

    for c in range(counts[1]):
        copy(weights[c * ring_size], s, c).wait()
    for owner in range(members):
        source = pl.multiple_of(where[3 + owner] * step, step)
        out_ref[0, :, owner * step : (owner + 1) * step] = contract(
            wide[...], held[s, pl.ds(source, step), :]
        )


def spread_first(where, grads, weights, ring_size):
    tokens = grads[0].shape[0]
    depth = sum(a.shape[1] for a in grads)
    width = weights[0].shape[0]
    chunks = len(weights) // ring_size
    return pl.pallas_call(
        partial(spread_first_kernel, (len(grads), chunks), ring_size),
        grid_spec=pltpu.PrefetchScalarGridSpec(
            num_scalar_prefetch=1,
            grid=(ring_size,),
            in_specs=[pl.BlockSpec(a.shape, lambda i, w: (0, 0)) for a in grads]
            + [pl.BlockSpec(memory_space=pltpu.HBM) for _ in weights],
            out_specs=pl.BlockSpec((1, tokens, width), lambda i, w: (i, 0, 0)),
            scratch_shapes=[
                pltpu.VMEM((tokens, depth), jnp.bfloat16),
                pltpu.VMEM((ring_size, width, depth), jnp.bfloat16),
                pltpu.SemaphoreType.DMA((ring_size, chunks)),
            ],
        ),
        out_shape=jax.ShapeDtypeStruct((ring_size, tokens, width), jnp.float32),
        compiler_params=pltpu.CompilerParams(vmem_limit_bytes=14 << 20),
        cost_estimate=pl.CostEstimate(
            flops=2 * tokens * width * ring_size * depth,
            bytes_accessed=4 * tokens * width * ring_size,
            transcendentals=0,
        ),
    )(where, *grads, *weights)


def spread_last_kernel(parts, where, so_far, *refs):
    owns, (back_ref, cos_ref, sin_ref) = refs[:parts], refs[parts : parts + 3]
    weights = refs[parts + 3 : -4]
    key_ref, keep_ref, send_ref, wide = refs[-4:]
    members = where.shape[0] - 3
    step = weights[0].shape[0] // members
    rows = keep_ref.shape[2]
    s = pl.program_id(0)

    @pl.when(s == 0)
    def _():
        for block in range(members):
            partner = (block % (members // 2)) * 2 + block // (members // 2)
            lines = pl.ds(pl.multiple_of(where[3 + partner] * rows, rows), rows)
            grad = back_ref[lines, :].astype(jnp.float32)
            for own in owns:
                grad += own[lines, :]
            key_grad = grad[:, :HD]
            turned = pltpu.roll(key_grad, HD // 2, 1)
            key_done = key_grad * cos_ref[lines, :] - turned * sin_ref[lines, :]
            key_ref[lines, :] = key_done.astype(jnp.bfloat16)
            here = slice(block * rows, (block + 1) * rows)
            wide[here, :HD] = key_done.astype(jnp.bfloat16)
            wide[here, HD:] = grad[:, HD:].astype(jnp.bfloat16)

    for piece, weight in enumerate(weights):

        @pl.when(s == piece)
        def _():
            for owner in range(members):
                source = pl.multiple_of(where[3 + owner] * step, step)
                lanes = slice(owner * step, (owner + 1) * step)
                total = so_far[0, :, lanes] + contract(wide[...], weight[pl.ds(source, step), :])
                total = total.astype(jnp.bfloat16)
                for u in range(members // 2):
                    keep_ref[u, 0, :, lanes] = total[u * rows : (u + 1) * rows, :]
                    lower = (members // 2 + u) * rows
                    send_ref[u, 0, :, lanes] = total[lower : lower + rows, :]


def spread_last(where, so_far, owns, back, cosine, sine, weights, ring_size):
    tokens = back.shape[0]
    members = where.shape[0] - 3
    rows = tokens // members
    width = weights[0].shape[0]
    planes_per_half = ring_size // 2
    whole = lambda a: pl.BlockSpec(a.shape, lambda i, w: (0, 0))

    def out_at(s, w):
        plane = lax.rem(w[0] - s + ring_size, ring_size)
        half = lax.rem(plane // planes_per_half + w[2], 2)
        return (0, half, 0, lax.rem(plane, planes_per_half))

    shape = (members // 2, 2, rows, width * planes_per_half)
    small = [*owns, back, cosine, sine]
    return pl.pallas_call(
        partial(spread_last_kernel, len(owns)),
        grid_spec=pltpu.PrefetchScalarGridSpec(
            num_scalar_prefetch=1,
            grid=(ring_size,),
            in_specs=[pl.BlockSpec((1, tokens, width), lambda i, w: (i, 0, 0))]
            + [whole(a) for a in small]
            + [pl.BlockSpec(memory_space=pltpu.VMEM) for a in weights],
            out_specs=[pl.BlockSpec((tokens, HD), lambda i, w: (0, 0))]
            + [pl.BlockSpec((members // 2, 1, rows, width), out_at)] * 2,
            scratch_shapes=[pltpu.VMEM((tokens, 2 * HD), jnp.bfloat16)],
        ),
        out_shape=[jax.ShapeDtypeStruct((tokens, HD), jnp.bfloat16)]
        + [jax.ShapeDtypeStruct(shape, jnp.bfloat16)] * 2,
        compiler_params=pltpu.CompilerParams(vmem_limit_bytes=14 << 20),
        cost_estimate=pl.CostEstimate(
            flops=4 * tokens * width * ring_size * HD,
            bytes_accessed=4 * tokens * width * ring_size,
            transcendentals=0,
        ),
    )(where, so_far, *small, *weights)


def key_weights_kernel(ring_size, where, *refs):
    members = where.shape[0] - 3
    normed, grads = refs[:ring_size], refs[ring_size : ring_size + members]
    out_refs, wide = refs[ring_size + members : -1], refs[-1]
    width = grads[0].shape[1]
    for owner in range(members):
        for d in range(members):

            @pl.when(where[3 + owner] == d)
            def _():
                wide[:, owner * width : (owner + 1) * width] = grads[d][...]

    for n_ref, out_ref in zip(normed, out_refs):
        out_ref[...] = lax.dot_general(
            n_ref[...], wide[...], (((0,), (0,)), ((), ())), preferred_element_type=jnp.float32
        ).astype(out_ref.dtype)


def key_weights(where, normed, grads, rows, dtype):
    tokens, members = grads[0].shape[0], len(grads)
    width = members * grads[0].shape[1]
    shape = (rows, width)
    return pl.pallas_call(
        partial(key_weights_kernel, len(normed)),
        grid_spec=pltpu.PrefetchScalarGridSpec(
            num_scalar_prefetch=1,
            grid=(1,),
            in_specs=[pl.BlockSpec((tokens, rows), lambda i, w: (0, 0)) for _ in normed]
            + [pl.BlockSpec(g.shape, lambda i, w: (0, 0)) for g in grads],
            out_specs=[pl.BlockSpec(shape, lambda i, w: (0, 0))] * len(normed),
            scratch_shapes=[pltpu.VMEM((tokens, width), jnp.bfloat16)],
        ),
        out_shape=[jax.ShapeDtypeStruct(shape, dtype)] * len(normed),
        compiler_params=pltpu.CompilerParams(vmem_limit_bytes=10 << 20),
        cost_estimate=pl.CostEstimate(
            flops=2 * tokens * width * rows * len(normed),
            bytes_accessed=2 * tokens * (width + rows * len(normed)),
            transcendentals=0,
        ),
    )(where, *normed, *grads)


def grouped_device(hidden, norm_gain, w_query, w_key, w_value, upstream, cached, lengths):
    rows, half = hidden.shape
    kv_count = w_key.shape[1] // HD
    query_width = w_query.shape[1] // kv_count
    members = kv_count
    devices, tensors = lax.axis_size("dp"), lax.axis_size("tensor")
    ring_size = devices // members
    tokens = members * rows
    weight_rows = w_key.shape[0]
    me, tensor = lax.axis_index("dp"), lax.axis_index("tensor")
    ring, group = me // members, me % members
    partners = [jnp.bitwise_xor(group, d) for d in range(members)]
    where = jnp.stack([ring, group, tensor] + partners).astype(jnp.int32)

    def to_partner(block, d):
        return lax.ppermute(block, "dp", [(i, i ^ d) for i in range(devices)])

    def to_side(block):
        return lax.ppermute(block, "tensor", [(i, i ^ 1) for i in range(tensors)])

    def along(block, distance):
        route = [(i, (i + distance * members) % devices) for i in range(devices)]
        return lax.ppermute(block, "dp", route)

    def columns(array, owner, width):
        return lax.dynamic_slice_in_dim(array, owner * width, width, 1)

    def circulate(own, gate=None):
        pieces = [own]
        for hop in range(1, ring_size):
            block = pieces[-1] if gate is None else gate(hop, pieces[-1])
            pieces.append(along(block, 1))
        return pieces

    k_ring, v_ring = circulate(w_key), circulate(w_value)

    def pack_q(owner):
        return jnp.concatenate(
            [columns(w_query, owner, query_width), columns(upstream, owner, query_width)], axis=0
        )

    q_parts = [pack_q(group)] + [to_partner(pack_q(partners[d]), d) for d in range(1, members)]
    q_own = jnp.concatenate([p[:weight_rows] for p in q_parts], axis=0)
    ends = [sum(CHUNKS[: c + 1]) * HD for c in range(len(CHUNKS))]
    spans = [slice(end - count * HD, end) for end, count in zip(ends, CHUNKS)]
    q_chunk = [q_own[:, span] for span in spans]

    def pack_kv(owner):
        pairs = []
        for k, v in zip(k_ring, v_ring):
            cut = [columns(k, owner, HD), columns(v, owner, HD)]
            pairs.append(lax.optimization_barrier(jnp.concatenate(cut, axis=1)))
        return jnp.concatenate(pairs, axis=0)

    across = to_partner(hidden, 2)
    beside = to_side(hidden)
    corner = to_side(across)
    near = jnp.stack([hidden, beside, across, corner]).reshape(2, 2, rows, half)
    far = to_partner(near, 1)
    *normed, inverse = norm_pieces(where, near, far, norm_gain[None, :], ring_size)

    kv_parts = [pack_kv(group)] + [
        after(to_partner(pack_kv(partners[d]), d), normed[0])
        for d in range(1, members)
    ]
    kv_pieces = [
        jnp.concatenate([p[s * weight_rows : (s + 1) * weight_rows] for p in kv_parts], axis=0)
        for s in range(ring_size)
    ]

    def project(pieces):
        total = None
        for s, piece in enumerate(pieces):
            term = jnp.dot(normed[s], piece, preferred_element_type=jnp.float32)
            total = term if total is None else total + term
        return total

    first = ring * tokens
    token_positions = first + jnp.arange(tokens, dtype=jnp.int32)
    _, doc_len, positions, onehot = document_info(lengths, token_positions)
    cosine, sine = rope_tables(positions)
    sign = jnp.where(jnp.arange(HD) < HD // 2, -1.0, 1.0).astype(jnp.float32)
    sine = sine * sign[None, :]
    low = (token_positions - positions - first + LONGEST)[None, :]

    def place(parts):
        stacked = jnp.stack(parts)
        return [
            lax.dynamic_index_in_dim(stacked, jnp.bitwise_xor(group, o), 0, keepdims=False)
            for o in range(members)
        ]

    up_own = jnp.concatenate(place([p[weight_rows:] for p in q_parts]), axis=0)
    pooled = (
        jnp.dot(
            onehot.astype(jnp.float32),
            columns(cached, group, query_width),
            precision=lax.Precision.HIGHEST,
        )
        / doc_len.astype(jnp.float32)[:, None]
    )
    out_grad = (up_own.astype(jnp.float32) + pooled).astype(jnp.bfloat16)

    kv_proj = project(kv_pieces)
    key_proj = kv_proj[:, :HD]
    key_own = key_proj * cosine + jnp.roll(key_proj, HD // 2, axis=1) * sine
    kv_rows = jnp.concatenate([key_own, kv_proj[:, HD:]], axis=1).astype(jnp.bfloat16)

    q_pieces = []
    for c in range(len(CHUNKS)):
        gate = lambda hop, block, c=c: after(block, kv_rows) if c and hop == ring_size - 1 else block
        q_pieces.append(circulate(q_chunk[c], gate))
    halo = lax.ppermute(kv_rows, "dp", [(i, i + members) for i in range(devices - members)])
    kv_all = jnp.concatenate([halo, kv_rows], axis=0)
    keys, values = kv_all[:, :HD], kv_all[:, HD:]
    keys_turned = keys.T
    query_dones, owns, halo_grad = [], [], None
    for c in range(len(CHUNKS)):
        early = lax.optimization_barrier(project(q_pieces[c][:-1]))
        query_done, halo_grad, own_grad = attend(
            early, normed[-1:], q_pieces[c][-1:],
            out_grad[:, spans[c]],
            keys, keys_turned, values, cosine, sine, low, halo_grad,
        )
        query_dones.append(query_done)
        owns.append(own_grad)
    later = [(i + members, i) for i in range(devices - members)]
    back = lax.ppermute(halo_grad, "dp", later)

    weights = [
        pltpu.with_memory_space_constraint(piece, pltpu.HBM)
        for pieces in q_pieces
        for piece in pieces
    ]
    so_far = spread_first(where, query_dones, weights, ring_size)
    in_hbm = [pltpu.with_memory_space_constraint(a, pltpu.HBM) for a in (*owns, cosine, sine)]
    key_done, keep, send = spread_last(
        where, so_far, in_hbm[:-2], back, *in_hbm[-2:], kv_pieces, ring_size
    )

    key_dones = [key_done] + [to_partner(key_done, d) for d in range(1, members)]
    others = key_weights(where, normed[1:], key_dones, weight_rows, jnp.bfloat16)
    (grad_wkey,) = key_weights(where, normed[:1], key_dones, weight_rows, jnp.float32)
    for s in range(1, ring_size):
        term = along(others[s - 1], -s)
        grad_wkey = grad_wkey + term.astype(jnp.float32)

    wide = lambda a: a.astype(jnp.float32)
    narrow = lambda a: a.astype(jnp.bfloat16)
    other = to_partner(send, 1)
    both = lambda *at: wide(keep[at]) + wide(other[at])
    cut = half // 2
    low_cut, high_cut, every = slice(0, cut), slice(cut, half), slice(None)
    left_half = narrow(both(1, every, every, low_cut))
    right_half = narrow(both(every, 1, every, high_cut))
    left_half = to_partner(left_half, 2)
    right_half = to_side(right_half)
    left_next = narrow(both(0, 1, every, low_cut) + wide(left_half[1]))
    right_next = narrow(both(1, 0, every, high_cut) + wide(right_half[1]))
    left_next, right_next = lax.optimization_barrier((left_next, right_next))
    right_next = to_partner(right_next, 2)
    left_next = to_side(left_next)
    left_sum = both(0, 0, every, low_cut) + wide(left_half[0]) + wide(left_next)
    right_sum = both(0, 0, every, high_cut) + wide(right_half[0]) + wide(right_next)
    normed_grad = jnp.concatenate([left_sum, right_sum], axis=1)
    own_hidden = wide(hidden)
    own_gain = lax.dynamic_slice_in_dim(norm_gain, tensor * half, half, 0)
    own_inverse = lax.dynamic_slice_in_dim(inverse, group * rows, rows, 0)[:, :1]
    part = jnp.sum(normed_grad * own_gain[None, :] * own_hidden, axis=1)[None, :]
    projection = (part + to_side(part)).reshape(rows, 1)
    grad_hidden = (
        own_inverse * own_gain[None, :] * normed_grad
        - own_hidden * (own_inverse * own_inverse * own_inverse) * projection / D
    ).astype(jnp.bfloat16)
    return (grad_hidden, grad_wkey)


def is_grouped(mesh_shape, rows, key_columns):
    members = key_columns // HD
    return (
        mesh_shape["tensor"] == 2
        and members == 4
        and mesh_shape["dp"] == 4 * members
        and members * rows == LONGEST
    )


def per_device(hidden, norm_gain, w_query, w_key, w_value, upstream, cached, lengths):
    arrays = (hidden, norm_gain, w_query, w_key, w_value, upstream, cached, lengths)
    sizes = {axis: lax.axis_size(axis) for axis in ("dp", "tensor")}
    if not is_grouped(sizes, hidden.shape[0], w_key.shape[1]):
        return plain_device(*arrays)
    return grouped_device(*arrays)


def solution(mesh):
    placed = (
        P("dp", "tensor"),
        P(),
        P("dp", "tensor"),
        P("dp", "tensor"),
        P("dp", "tensor"),
        P("dp", "tensor"),
        P(None, "tensor"),
        P(),
    )
    return jax.shard_map(
        per_device,
        mesh=mesh,
        in_specs=placed,
        out_specs=(P("dp", "tensor"), P("dp", "tensor")),
        check_vma=False,
    )
```

```python
from functools import partial

import jax
import jax.numpy as jnp
from jax import lax
from jax.experimental import pallas as pl
from jax.experimental.pallas import tpu as pltpu
from jax.sharding import PartitionSpec as P


D = 4096
HD = 128
HOPS = 4
LONGEST = 512
CHUNKS = (2, 2)


EPSILON = 1e-05
LOG2_E = 1.4426950408889634
ROPE_BASE = 500000.0


def from_behind(block, axis, distance):
    devices = range(lax.axis_size(axis))
    route = [(i - distance, i) for i in devices if i - distance in devices]
    return lax.ppermute(block, axis, route)


def document_info(lengths, positions_global):
    doc_ends = jnp.cumsum(lengths)
    documents = jnp.sum((positions_global[:, None] >= doc_ends[None, :]).astype(jnp.int32), axis=1)
    doc_slots = jnp.arange(lengths.shape[0], dtype=jnp.int32)
    onehot = documents[:, None] == doc_slots[None, :]
    doc_len = jnp.sum(jnp.where(onehot, lengths[None, :], 0), axis=1)
    doc_end = jnp.sum(jnp.where(onehot, doc_ends[None, :], 0), axis=1)
    return (documents, doc_len, positions_global - doc_end + doc_len, onehot)


def block_mask(lengths, query_positions, key_positions):
    query_docs = document_info(lengths, query_positions)[0]
    key_docs = document_info(lengths, key_positions)[0]
    return (
        (key_positions[None, :] >= 0)
        & (key_docs[None, :] == query_docs[:, None])
        & (key_positions[None, :] <= query_positions[:, None])
    )


def rope_tables(positions):
    half_width = HD // 2
    frequency = ROPE_BASE ** (-(jnp.arange(half_width, dtype=jnp.float32) * 2.0 / HD))
    angles = positions.astype(jnp.float32)[:, None] * frequency[None, :]
    angles = jnp.concatenate([angles, angles], axis=1)
    return (jnp.cos(angles), jnp.sin(angles))


def rotate(values, cosine_table, sine_table):
    half_width = values.shape[-1] // 2
    turned = jnp.concatenate([-values[..., half_width:], values[..., :half_width]], axis=-1)
    return values * cosine_table[:, None, :] + turned * sine_table[:, None, :]


def unrotate(gradient, cosine_table, sine_table):
    half_width = gradient.shape[-1] // 2
    scaled = gradient * sine_table[:, None, :]
    back_part = jnp.concatenate([scaled[..., half_width:], -scaled[..., :half_width]], axis=-1)
    return gradient * cosine_table[:, None, :] + back_part


def contract(left, right):
    return lax.dot_general(
        left, right, (((1,), (1,)), ((), ())), preferred_element_type=jnp.float32
    )


def attend_head(queries, key_rows, value_rows, out_grad, allowed):
    score_scale = HD ** (-0.5)
    scores = contract(queries, key_rows) * score_scale
    weights = jnp.where(allowed, jnp.exp(scores), 0.0)
    totals = jnp.sum(weights, axis=1, keepdims=True)
    softmax = weights / totals
    prob_grad = contract(out_grad, value_rows)
    row_delta = jnp.sum(softmax * prob_grad, axis=1, keepdims=True)
    score_grad = (softmax * (prob_grad - row_delta)).astype(jnp.bfloat16)
    query_grad = jnp.dot(score_grad, key_rows, preferred_element_type=jnp.float32) * score_scale
    key_grad = (
        lax.dot_general(
            score_grad, queries, (((0,), (0,)), ((), ())), preferred_element_type=jnp.float32
        )
        * score_scale
    )
    value_grad = lax.dot_general(
        softmax.astype(jnp.bfloat16),
        out_grad,
        (((0,), (0,)), ((), ())),
        preferred_element_type=jnp.float32,
    )
    return (query_grad, key_grad, value_grad, totals, row_delta)


def fold_heads(per_head, kv_count, group_size):
    summed = per_head.reshape(kv_count, group_size, per_head.shape[1], HD).sum(axis=1)
    return jnp.transpose(summed, (1, 0, 2))


def plain_device(hidden, norm_gain, w_query, w_key, w_value, upstream, cached, lengths):
    gathered = lax.all_gather(hidden, "tensor", axis=1, tiled=True)
    row_count = gathered.shape[0]
    query_cols = w_query.shape[1]
    key_cols = w_key.shape[1]
    head_count = query_cols // HD
    kv_count = key_cols // HD
    group_size = head_count // kv_count
    hidden_wide = gathered.astype(jnp.float32)
    inverse_scale = lax.rsqrt(jnp.mean(hidden_wide * hidden_wide, axis=1, keepdims=True) + EPSILON)
    normed = (hidden_wide * inverse_scale * norm_gain[None, :]).astype(jnp.bfloat16)
    dp_index = lax.axis_index("dp")
    own_positions = dp_index * row_count + jnp.arange(row_count, dtype=jnp.int32)
    _, doc_len, positions, onehot = document_info(lengths, own_positions)
    cosine_table, sine_table = rope_tables(positions)
    full_query, full_key, full_value = (
        lax.all_gather(w_query, "dp", axis=0, tiled=True),
        lax.all_gather(w_key, "dp", axis=0, tiled=True),
        lax.all_gather(w_value, "dp", axis=0, tiled=True),
    )
    query_proj = jnp.dot(normed, full_query, preferred_element_type=jnp.float32)
    key_proj = jnp.dot(normed, full_key, preferred_element_type=jnp.float32)
    value_proj = jnp.dot(normed, full_value, preferred_element_type=jnp.float32)
    queries = rotate(
        query_proj.reshape(row_count, head_count, HD), cosine_table, sine_table
    ).astype(jnp.bfloat16)
    key_rows = rotate(key_proj.reshape(row_count, kv_count, HD), cosine_table, sine_table).astype(
        jnp.bfloat16
    )
    value_rows = value_proj.astype(jnp.bfloat16).reshape(row_count, kv_count, HD)
    pooled = (
        jnp.dot(onehot.astype(jnp.float32), cached, precision=lax.Precision.HIGHEST)
        / doc_len.astype(jnp.float32)[:, None]
    )
    out_grad = (
        (upstream.astype(jnp.float32) + pooled)
        .astype(jnp.bfloat16)
        .reshape(row_count, head_count, HD)
    )
    key_list = []
    value_list = []
    for distance in range(HOPS, 0, -1):
        earlier_key, earlier_value = from_behind((key_rows, value_rows), "dp", distance)
        key_list.append(earlier_key)
        value_list.append(earlier_value)
    key_window = jnp.concatenate(key_list + [key_rows], axis=0)
    value_window = jnp.concatenate(value_list + [value_rows], axis=0)
    window = key_window.shape[0]
    window_positions = dp_index * row_count - HOPS * row_count + jnp.arange(window, dtype=jnp.int32)
    allowed = block_mask(lengths, own_positions, window_positions)
    head_queries = jnp.transpose(queries, (1, 0, 2))
    head_grads = jnp.transpose(out_grad, (1, 0, 2))
    head_keys = jnp.transpose(jnp.repeat(key_window, group_size, axis=1), (1, 0, 2))
    head_values = jnp.transpose(jnp.repeat(value_window, group_size, axis=1), (1, 0, 2))

    def one_head(operands):
        return attend_head(operands[0], operands[1], operands[2], operands[3], allowed)

    query_grad, key_grad, value_grad, _, _ = lax.map(
        one_head, (head_queries, head_keys, head_values, head_grads)
    )
    key_sum = fold_heads(key_grad, kv_count, group_size)
    value_sum = fold_heads(value_grad, kv_count, group_size)
    own_key = key_sum[HOPS * row_count :]
    own_value = value_sum[HOPS * row_count :]
    for distance in range(1, HOPS + 1):
        lower = (HOPS - distance) * row_count
        back_key, back_value = (
            from_behind(
                key_sum[lower : lower + row_count].astype(jnp.bfloat16), "dp", -distance
            ).astype(jnp.float32),
            from_behind(
                value_sum[lower : lower + row_count].astype(jnp.bfloat16), "dp", -distance
            ).astype(jnp.float32),
        )
        own_key = own_key + back_key
        own_value = own_value + back_value
    query_done = (
        unrotate(jnp.transpose(query_grad, (1, 0, 2)), cosine_table, sine_table)
        .astype(jnp.bfloat16)
        .reshape(row_count, query_cols)
    )
    key_done = (
        unrotate(own_key, cosine_table, sine_table)
        .astype(jnp.bfloat16)
        .reshape(row_count, key_cols)
    )
    value_done = own_value.astype(jnp.bfloat16).reshape(row_count, key_cols)
    portion = (
        contract(query_done, full_query)
        + contract(key_done, full_key)
        + contract(value_done, full_value)
    )
    own_hidden = hidden.astype(jnp.float32)
    own_cols = hidden.shape[1]
    gain_offset = lax.axis_index("tensor") * own_cols
    own_gain = lax.dynamic_slice_in_dim(norm_gain, gain_offset, own_cols, 0)
    normed_grad = lax.psum_scatter(
        portion.astype(jnp.bfloat16), "tensor", scatter_dimension=1, tiled=True
    ).astype(jnp.float32)
    projection = lax.psum(
        jnp.sum(normed_grad * own_gain[None, :] * own_hidden, axis=1, keepdims=True), "tensor"
    )
    grad_hidden = (
        inverse_scale * own_gain[None, :] * normed_grad
        - own_hidden * (inverse_scale * inverse_scale * inverse_scale) * projection / D
    ).astype(jnp.bfloat16)
    grad_wkey = lax.psum_scatter(
        lax.dot_general(
            normed, key_done, (((0,), (0,)), ((), ())), preferred_element_type=jnp.float32
        ),
        "dp",
        scatter_dimension=0,
        tiled=True,
    )
    return (grad_hidden, grad_wkey)


def after(array, *others):
    return lax.optimization_barrier((array, *others))[0]


def norm_kernel(where, near_ref, far_ref, gain_ref, *outs):
    pieces, inv_ref = outs[:-1], outs[-1]
    ring, tensor = where[0], where[2]
    ring_size = len(pieces)
    members = where.shape[0] - 3
    step = pieces[0].shape[1] // members

    def write(ref):
        total = jnp.zeros((ref.shape[2], 1), jnp.float32)
        for half in range(2):
            wide = ref[0, half].astype(jnp.float32)
            total = total + jnp.sum(wide * wide, axis=1, keepdims=True)
        inverse = lax.rsqrt(total / D + EPSILON)
        inv_ref[...] = jnp.broadcast_to(inverse, inv_ref.shape)
        planes_per_half = ring_size // 2
        for s in range(ring_size):
            plane = lax.rem(ring - s + ring_size, ring_size)
            half = lax.rem(plane // planes_per_half + tensor, 2)
            for d in range(members):
                inner = lax.rem(plane, planes_per_half) * (members * step) + where[3 + d] * step
                inner = pl.multiple_of(inner, step)
                outer = pl.multiple_of((plane * members + where[3 + d]) * step, step)
                wide = ref[0, half, :, pl.ds(inner, step)].astype(jnp.float32)
                scaled = wide * inverse * gain_ref[:, pl.ds(outer, step)]
                pieces[s][:, d * step : (d + 1) * step] = scaled.astype(jnp.bfloat16)

    @pl.when(pl.program_id(1) == 0)
    def _():
        write(near_ref)

    @pl.when(pl.program_id(1) == 1)
    def _():
        write(far_ref)


def norm_pieces(where, near, far, gain, ring_size):
    rows, half = near.shape[2], near.shape[3]
    members = where.shape[0] - 3
    tokens = members * rows
    width = 2 * half // ring_size
    spec = pl.BlockSpec((1, 2, rows, half), lambda u, v, w: (u, 0, 0, 0))

    def out_row(u, v, w):
        return (w[3 + 2 * u + v], 0)

    return pl.pallas_call(
        norm_kernel,
        grid_spec=pltpu.PrefetchScalarGridSpec(
            num_scalar_prefetch=1,
            grid=(2, 2),
            in_specs=[spec, spec, pl.BlockSpec((1, 2 * half), lambda u, v, w: (0, 0))],
            out_specs=[pl.BlockSpec((rows, width), out_row)] * ring_size
            + [pl.BlockSpec((rows, 128), out_row)],
        ),
        out_shape=[jax.ShapeDtypeStruct((tokens, width), jnp.bfloat16)] * ring_size
        + [jax.ShapeDtypeStruct((tokens, 128), jnp.float32)],
        compiler_params=pltpu.CompilerParams(vmem_limit_bytes=14 << 20),
        cost_estimate=pl.CostEstimate(
            flops=8 * tokens * 2 * half, bytes_accessed=8 * tokens * half, transcendentals=tokens
        ),
    )(where, near, far, gain)


def attend_kernel(heads, rows, terms, first, q_ref, *refs):
    n_refs, w_refs, refs = refs[:terms], refs[terms : 2 * terms], refs[2 * terms :]
    g_ref, k_ref, kt_ref, v_ref, cos_ref, sin_ref, low_ref = refs[:7]
    before = None if first else refs[7]
    dq_ref, halo_ref, own_ref, dkv_ref = refs[7 if first else 8 :]
    scale = HD ** (-0.5)
    halo = halo_ref.shape[0]
    window = halo + rows
    blocks = q_ref.shape[0] // rows

    @pl.when(pl.program_id(0) == 0)
    def _():
        dkv_ref[...] = jnp.zeros_like(dkv_ref)

    projected = q_ref[...]
    for n_ref, w_ref in zip(n_refs, w_refs):
        projected += jnp.dot(n_ref[...], w_ref[...], preferred_element_type=jnp.float32)
    key_at = lax.broadcasted_iota(jnp.int32, (window, rows), 0)
    query_at = lax.broadcasted_iota(jnp.int32, (rows, rows), 1)
    causal = key_at[:rows] <= query_at
    staged = []
    for block in range(blocks):
        here = slice(block * rows, (block + 1) * rows)
        base = pl.multiple_of((pl.program_id(0) * blocks + block) * rows, rows)
        cosine, sine = cos_ref[here, :], sin_ref[here, :]
        turned = []
        for h in range(heads):
            u = projected[here, h * HD : (h + 1) * HD]
            turned.append((u * cosine + pltpu.roll(u, HD // 2, 1) * sine).astype(jnp.bfloat16))
        queries = jnp.concatenate(turned, axis=0)
        grads = jnp.concatenate([g_ref[here, h * HD : (h + 1) * HD] for h in range(heads)], axis=0)
        scores = contract(k_ref[pl.ds(base, window), :], queries)
        prob_grads = contract(v_ref[pl.ds(base, window), :], grads)
        staged.append((here, base, cosine, sine, queries, grads, scores, prob_grads))
    for here, base, cosine, sine, queries, grads, scores, prob_grads in staged:
        low = low_ref[:, here] - base
        inside = key_at >= low
        allowed = (inside[:halo], inside[halo:] & causal)
        probs, score_grads = [], []
        for h in range(heads):
            there = slice(h * rows, (h + 1) * rows)
            grown = jnp.exp2(scores[:, there] * (scale * LOG2_E))
            weights = jnp.concatenate(
                [
                    jnp.where(allowed[0], grown[:halo], 0.0),
                    jnp.where(allowed[1], grown[halo:], 0.0),
                ],
                axis=0,
            )
            prob_grad = prob_grads[:, there]
            softmax = weights / jnp.sum(weights, axis=0, keepdims=True)
            row_delta = jnp.sum(softmax * prob_grad, axis=0, keepdims=True)
            probs.append(softmax.astype(jnp.bfloat16))
            score_grads.append((softmax * (prob_grad - row_delta)).astype(jnp.bfloat16))
        probs = jnp.concatenate(probs, axis=1)
        score_grads = jnp.concatenate(score_grads, axis=1)
        dkv_ref[pl.ds(base, window), :HD] += (
            jnp.dot(score_grads, queries, preferred_element_type=jnp.float32) * scale
        )
        dkv_ref[pl.ds(base, window), HD:] += jnp.dot(
            probs, grads, preferred_element_type=jnp.float32
        )
        query_grads = jnp.dot(
            kt_ref[:, pl.ds(base, window)], score_grads, preferred_element_type=jnp.float32
        )
        for h in range(heads):
            grad = query_grads[:, h * rows : (h + 1) * rows].T * scale
            back = grad * cosine - pltpu.roll(grad, HD // 2, 1) * sine
            dq_ref[here, h * HD : (h + 1) * HD] = back.astype(jnp.bfloat16)

    @pl.when(pl.program_id(0) == pl.num_programs(0) - 1)
    def _():
        halo_sum = dkv_ref[:halo, :]
        halo_ref[...] = halo_sum if first else (halo_sum + before[...]).astype(jnp.bfloat16)
        own_ref[...] = dkv_ref[halo:, :]


def attend(q_proj, normed, weights, grads, keys, keys_turned, values, cosine, sine, low, before=None):
    tokens, width = q_proj.shape
    heads, rows = width // HD, 128
    step = 2 * rows
    total = keys.shape[0]
    window = total - tokens + rows
    whole = lambda a: pl.BlockSpec(a.shape, lambda i: (0, 0))
    by_rows = lambda w: pl.BlockSpec((step, w), lambda i: (i, 0))
    fixed = lambda n, w: pl.BlockSpec((n, w), lambda i: (0, 0))
    extra = [] if before is None else [before]
    operands = [q_proj, *normed, *weights, grads, keys, keys_turned, values, cosine, sine, low]
    operands = [pltpu.with_memory_space_constraint(a, pltpu.HBM) for a in operands + extra]
    return pl.pallas_call(
        partial(attend_kernel, heads, rows, len(normed), before is None),
        grid=(tokens // step,),
        in_specs=[by_rows(width)]
        + [by_rows(n.shape[1]) for n in normed]
        + [whole(w) for w in weights]
        + [by_rows(width), whole(keys), whole(keys_turned), whole(values)]
        + [by_rows(HD), by_rows(HD), pl.BlockSpec((1, step), lambda i: (0, i))]
        + [fixed(total - tokens, 2 * HD) for _ in extra],
        out_specs=[by_rows(width), fixed(total - tokens, 2 * HD), fixed(tokens, 2 * HD)],
        out_shape=[jax.ShapeDtypeStruct((tokens, width), jnp.bfloat16),
                   jax.ShapeDtypeStruct(
                       (total - tokens, 2 * HD), jnp.float32 if before is None else jnp.bfloat16
                   ),
                   jax.ShapeDtypeStruct((tokens, 2 * HD), jnp.float32)],
        scratch_shapes=[pltpu.VMEM((total, 2 * HD), jnp.float32)],
        compiler_params=pltpu.CompilerParams(vmem_limit_bytes=24 << 20),
        cost_estimate=pl.CostEstimate(
            flops=10 * tokens * window * width, bytes_accessed=12 * tokens * width,
            transcendentals=tokens * window * heads,
        ),
    )(*operands)


def spread_blocks(where, wide, grads, rows):
    members = where.shape[0] - 3
    for block in range(members):
        partner = (block % (members // 2)) * 2 + block // (members // 2)
        source = pl.multiple_of(where[3 + partner] * rows, rows)
        at = 0
        for grad in grads:
            wide[block * rows : (block + 1) * rows, at : at + grad.shape[1]] = grad[
                pl.ds(source, rows), :
            ]
            at += grad.shape[1]


def spread_first_kernel(counts, ring_size, where, *refs):
    grads, weights = refs[: counts[0]], refs[counts[0] : counts[0] + counts[1] * ring_size]
    out_ref, wide, held, arrived = refs[counts[0] + counts[1] * ring_size :]
    members = where.shape[0] - 3
    step = held.shape[1] // members
    s = pl.program_id(0)

    def copy(source, piece, c):
        width = source.shape[1]
        return pltpu.make_async_copy(
            source, held.at[piece, :, pl.ds(c * width, width)], arrived.at[piece, c]
        )

    @pl.when(s == 0)
    def _():
        for piece in range(ring_size):
            for c in range(counts[1]):
                copy(weights[c * ring_size + piece], piece, c).start()
        spread_blocks(where, wide, grads, wide.shape[0] // members)

    for c in range(counts[1]):
        copy(weights[c * ring_size], s, c).wait()
    for owner in range(members):
        source = pl.multiple_of(where[3 + owner] * step, step)
        out_ref[0, :, owner * step : (owner + 1) * step] = contract(
            wide[...], held[s, pl.ds(source, step), :]
        )


def spread_first(where, grads, weights, ring_size):
    tokens = grads[0].shape[0]
    depth = sum(a.shape[1] for a in grads)
    width = weights[0].shape[0]
    chunks = len(weights) // ring_size
    return pl.pallas_call(
        partial(spread_first_kernel, (len(grads), chunks), ring_size),
        grid_spec=pltpu.PrefetchScalarGridSpec(
            num_scalar_prefetch=1,
            grid=(ring_size,),
            in_specs=[pl.BlockSpec(a.shape, lambda i, w: (0, 0)) for a in grads]
            + [pl.BlockSpec(memory_space=pltpu.HBM) for _ in weights],
            out_specs=pl.BlockSpec((1, tokens, width), lambda i, w: (i, 0, 0)),
            scratch_shapes=[
                pltpu.VMEM((tokens, depth), jnp.bfloat16),
                pltpu.VMEM((ring_size, width, depth), jnp.bfloat16),
                pltpu.SemaphoreType.DMA((ring_size, chunks)),
            ],
        ),
        out_shape=jax.ShapeDtypeStruct((ring_size, tokens, width), jnp.float32),
        compiler_params=pltpu.CompilerParams(vmem_limit_bytes=14 << 20),
        cost_estimate=pl.CostEstimate(
            flops=2 * tokens * width * ring_size * depth,
            bytes_accessed=4 * tokens * width * ring_size,
            transcendentals=0,
        ),
    )(where, *grads, *weights)


def spread_last_kernel(parts, where, so_far, *refs):
    owns, (back_ref, cos_ref, sin_ref) = refs[:parts], refs[parts : parts + 3]
    weights = refs[parts + 3 : -4]
    key_ref, keep_ref, send_ref, wide = refs[-4:]
    members = where.shape[0] - 3
    step = weights[0].shape[0] // members
    rows = keep_ref.shape[2]
    s = pl.program_id(0)

    @pl.when(s == 0)
    def _():
        for block in range(members):
            partner = (block % (members // 2)) * 2 + block // (members // 2)
            lines = pl.ds(pl.multiple_of(where[3 + partner] * rows, rows), rows)
            grad = back_ref[lines, :].astype(jnp.float32)
            for own in owns:
                grad += own[lines, :]
            key_grad = grad[:, :HD]
            turned = pltpu.roll(key_grad, HD // 2, 1)
            key_done = key_grad * cos_ref[lines, :] - turned * sin_ref[lines, :]
            key_ref[lines, :] = key_done.astype(jnp.bfloat16)
            here = slice(block * rows, (block + 1) * rows)
            wide[here, :HD] = key_done.astype(jnp.bfloat16)
            wide[here, HD:] = grad[:, HD:].astype(jnp.bfloat16)

    for piece, weight in enumerate(weights):

        @pl.when(s == piece)
        def _():
            for owner in range(members):
                source = pl.multiple_of(where[3 + owner] * step, step)
                lanes = slice(owner * step, (owner + 1) * step)
                total = so_far[0, :, lanes] + contract(wide[...], weight[pl.ds(source, step), :])
                total = total.astype(jnp.bfloat16)
                for u in range(members // 2):
                    keep_ref[u, 0, :, lanes] = total[u * rows : (u + 1) * rows, :]
                    lower = (members // 2 + u) * rows
                    send_ref[u, 0, :, lanes] = total[lower : lower + rows, :]


def spread_last(where, so_far, owns, back, cosine, sine, weights, ring_size):
    tokens = back.shape[0]
    members = where.shape[0] - 3
    rows = tokens // members
    width = weights[0].shape[0]
    planes_per_half = ring_size // 2
    whole = lambda a: pl.BlockSpec(a.shape, lambda i, w: (0, 0))

    def out_at(s, w):
        plane = lax.rem(w[0] - s + ring_size, ring_size)
        half = lax.rem(plane // planes_per_half + w[2], 2)
        return (0, half, 0, lax.rem(plane, planes_per_half))

    shape = (members // 2, 2, rows, width * planes_per_half)
    small = [*owns, back, cosine, sine]
    return pl.pallas_call(
        partial(spread_last_kernel, len(owns)),
        grid_spec=pltpu.PrefetchScalarGridSpec(
            num_scalar_prefetch=1,
            grid=(ring_size,),
            in_specs=[pl.BlockSpec((1, tokens, width), lambda i, w: (i, 0, 0))]
            + [whole(a) for a in small]
            + [pl.BlockSpec(memory_space=pltpu.VMEM) for a in weights],
            out_specs=[pl.BlockSpec((tokens, HD), lambda i, w: (0, 0))]
            + [pl.BlockSpec((members // 2, 1, rows, width), out_at)] * 2,
            scratch_shapes=[pltpu.VMEM((tokens, 2 * HD), jnp.bfloat16)],
        ),
        out_shape=[jax.ShapeDtypeStruct((tokens, HD), jnp.bfloat16)]
        + [jax.ShapeDtypeStruct(shape, jnp.bfloat16)] * 2,
        compiler_params=pltpu.CompilerParams(vmem_limit_bytes=14 << 20),
        cost_estimate=pl.CostEstimate(
            flops=4 * tokens * width * ring_size * HD,
            bytes_accessed=4 * tokens * width * ring_size,
            transcendentals=0,
        ),
    )(where, so_far, *small, *weights)


def key_weights_kernel(ring_size, where, *refs):
    members = where.shape[0] - 3
    normed, grads = refs[:ring_size], refs[ring_size : ring_size + members]
    out_refs, wide = refs[ring_size + members : -1], refs[-1]
    width = grads[0].shape[1]
    for owner in range(members):
        for d in range(members):

            @pl.when(where[3 + owner] == d)
            def _():
                wide[:, owner * width : (owner + 1) * width] = grads[d][...]

    for n_ref, out_ref in zip(normed, out_refs):
        out_ref[...] = lax.dot_general(
            n_ref[...], wide[...], (((0,), (0,)), ((), ())), preferred_element_type=jnp.float32
        ).astype(out_ref.dtype)


def key_weights(where, normed, grads, rows, dtype):
    tokens, members = grads[0].shape[0], len(grads)
    width = members * grads[0].shape[1]
    shape = (rows, width)
    return pl.pallas_call(
        partial(key_weights_kernel, len(normed)),
        grid_spec=pltpu.PrefetchScalarGridSpec(
            num_scalar_prefetch=1,
            grid=(1,),
            in_specs=[pl.BlockSpec((tokens, rows), lambda i, w: (0, 0)) for _ in normed]
            + [pl.BlockSpec(g.shape, lambda i, w: (0, 0)) for g in grads],
            out_specs=[pl.BlockSpec(shape, lambda i, w: (0, 0))] * len(normed),
            scratch_shapes=[pltpu.VMEM((tokens, width), jnp.bfloat16)],
        ),
        out_shape=[jax.ShapeDtypeStruct(shape, dtype)] * len(normed),
        compiler_params=pltpu.CompilerParams(vmem_limit_bytes=10 << 20),
        cost_estimate=pl.CostEstimate(
            flops=2 * tokens * width * rows * len(normed),
            bytes_accessed=2 * tokens * (width + rows * len(normed)),
            transcendentals=0,
        ),
    )(where, *normed, *grads)


def grouped_device(hidden, norm_gain, w_query, w_key, w_value, upstream, cached, lengths):
    rows, half = hidden.shape
    kv_count = w_key.shape[1] // HD
    query_width = w_query.shape[1] // kv_count
    members = kv_count
    devices, tensors = lax.axis_size("dp"), lax.axis_size("tensor")
    ring_size = devices // members
    tokens = members * rows
    weight_rows = w_key.shape[0]
    me, tensor = lax.axis_index("dp"), lax.axis_index("tensor")
    ring, group = me // members, me % members
    partners = [jnp.bitwise_xor(group, d) for d in range(members)]
    where = jnp.stack([ring, group, tensor] + partners).astype(jnp.int32)

    def to_partner(block, d):
        return lax.ppermute(block, "dp", [(i, i ^ d) for i in range(devices)])

    def to_side(block):
        return lax.ppermute(block, "tensor", [(i, i ^ 1) for i in range(tensors)])

    def along(block, distance):
        route = [(i, (i + distance * members) % devices) for i in range(devices)]
        return lax.ppermute(block, "dp", route)

    def columns(array, owner, width):
        return lax.dynamic_slice_in_dim(array, owner * width, width, 1)

    def circulate(own, gate=None):
        pieces = [own]
        for hop in range(1, ring_size):
            block = pieces[-1] if gate is None else gate(hop, pieces[-1])
            pieces.append(along(block, 1))
        return pieces

    k_ring, v_ring = circulate(w_key), circulate(w_value)

    def pack_q(owner):
        return jnp.concatenate(
            [columns(w_query, owner, query_width), columns(upstream, owner, query_width)], axis=0
        )

    q_parts = [pack_q(group)] + [to_partner(pack_q(partners[d]), d) for d in range(1, members)]
    q_own = jnp.concatenate([p[:weight_rows] for p in q_parts], axis=0)
    ends = [sum(CHUNKS[: c + 1]) * HD for c in range(len(CHUNKS))]
    spans = [slice(end - count * HD, end) for end, count in zip(ends, CHUNKS)]
    q_chunk = [q_own[:, span] for span in spans]

    def pack_kv(owner):
        pairs = []
        for k, v in zip(k_ring, v_ring):
            cut = [columns(k, owner, HD), columns(v, owner, HD)]
            pairs.append(lax.optimization_barrier(jnp.concatenate(cut, axis=1)))
        return jnp.concatenate(pairs, axis=0)

    across = to_partner(hidden, 2)
    beside = to_side(hidden)
    corner = to_side(across)
    near = jnp.stack([hidden, beside, across, corner]).reshape(2, 2, rows, half)
    far = to_partner(near, 1)
    *normed, inverse = norm_pieces(where, near, far, norm_gain[None, :], ring_size)

    kv_parts = [pack_kv(group)] + [
        after(to_partner(pack_kv(partners[d]), d), normed[0])
        for d in range(1, members)
    ]
    kv_pieces = [
        jnp.concatenate([p[s * weight_rows : (s + 1) * weight_rows] for p in kv_parts], axis=0)
        for s in range(ring_size)
    ]

    def project(pieces):
        total = None
        for s, piece in enumerate(pieces):
            term = jnp.dot(normed[s], piece, preferred_element_type=jnp.float32)
            total = term if total is None else total + term
        return total

    first = ring * tokens
    token_positions = first + jnp.arange(tokens, dtype=jnp.int32)
    _, doc_len, positions, onehot = document_info(lengths, token_positions)
    cosine, sine = rope_tables(positions)
    sign = jnp.where(jnp.arange(HD) < HD // 2, -1.0, 1.0).astype(jnp.float32)
    sine = sine * sign[None, :]
    low = (token_positions - positions - first + LONGEST)[None, :]

    def place(parts):
        stacked = jnp.stack(parts)
        return [
            lax.dynamic_index_in_dim(stacked, jnp.bitwise_xor(group, o), 0, keepdims=False)
            for o in range(members)
        ]

    up_own = jnp.concatenate(place([p[weight_rows:] for p in q_parts]), axis=0)
    pooled = (
        jnp.dot(
            onehot.astype(jnp.float32),
            columns(cached, group, query_width),
            precision=lax.Precision.HIGHEST,
        )
        / doc_len.astype(jnp.float32)[:, None]
    )
    out_grad = (up_own.astype(jnp.float32) + pooled).astype(jnp.bfloat16)

    kv_proj = project(kv_pieces)
    key_proj = kv_proj[:, :HD]
    key_own = key_proj * cosine + jnp.roll(key_proj, HD // 2, axis=1) * sine
    kv_rows = jnp.concatenate([key_own, kv_proj[:, HD:]], axis=1).astype(jnp.bfloat16)

    q_pieces = []
    for c in range(len(CHUNKS)):
        gate = lambda hop, block, c=c: after(block, kv_rows) if c and hop == ring_size - 1 else block
        q_pieces.append(circulate(q_chunk[c], gate))
    halo = lax.ppermute(kv_rows, "dp", [(i, i + members) for i in range(devices - members)])
    kv_all = jnp.concatenate([halo, kv_rows], axis=0)
    keys, values = kv_all[:, :HD], kv_all[:, HD:]
    keys_turned = keys.T
    query_dones, owns, halo_grad = [], [], None
    for c in range(len(CHUNKS)):
        early = lax.optimization_barrier(project(q_pieces[c][:-1]))
        query_done, halo_grad, own_grad = attend(
            early, normed[-1:], q_pieces[c][-1:],
            out_grad[:, spans[c]],
            keys, keys_turned, values, cosine, sine, low, halo_grad,
        )
        query_dones.append(query_done)
        owns.append(own_grad)
    later = [(i + members, i) for i in range(devices - members)]
    back = lax.ppermute(halo_grad, "dp", later)

    weights = [
        pltpu.with_memory_space_constraint(piece, pltpu.HBM)
        for pieces in q_pieces
        for piece in pieces
    ]
    so_far = spread_first(where, query_dones, weights, ring_size)
    in_hbm = [pltpu.with_memory_space_constraint(a, pltpu.HBM) for a in (*owns, cosine, sine)]
    key_done, keep, send = spread_last(
        where, so_far, in_hbm[:-2], back, *in_hbm[-2:], kv_pieces, ring_size
    )

    key_dones = [key_done] + [to_partner(key_done, d) for d in range(1, members)]
    others = key_weights(where, normed[1:], key_dones, weight_rows, jnp.bfloat16)
    (grad_wkey,) = key_weights(where, normed[:1], key_dones, weight_rows, jnp.float32)
    for s in range(1, ring_size):
        term = along(others[s - 1], -s)
        grad_wkey = grad_wkey + term.astype(jnp.float32)

    wide = lambda a: a.astype(jnp.float32)
    narrow = lambda a: a.astype(jnp.bfloat16)
    other = to_partner(send, 1)
    both = lambda *at: wide(keep[at]) + wide(other[at])
    cut = half // 2
    low_cut, high_cut, every = slice(0, cut), slice(cut, half), slice(None)
    left_half = narrow(both(1, every, every, low_cut))
    right_half = narrow(both(every, 1, every, high_cut))
    left_half = to_partner(left_half, 2)
    right_half = to_side(right_half)
    left_next = narrow(both(0, 1, every, low_cut) + wide(left_half[1]))
    right_next = narrow(both(1, 0, every, high_cut) + wide(right_half[1]))
    left_next, right_next = lax.optimization_barrier((left_next, right_next))
    right_next = to_partner(right_next, 2)
    left_next = to_side(left_next)
    left_sum = both(0, 0, every, low_cut) + wide(left_half[0]) + wide(left_next)
    right_sum = both(0, 0, every, high_cut) + wide(right_half[0]) + wide(right_next)
    normed_grad = jnp.concatenate([left_sum, right_sum], axis=1)
    own_hidden = wide(hidden)
    own_gain = lax.dynamic_slice_in_dim(norm_gain, tensor * half, half, 0)
    own_inverse = lax.dynamic_slice_in_dim(inverse, group * rows, rows, 0)[:, :1]
    part = jnp.sum(normed_grad * own_gain[None, :] * own_hidden, axis=1)[None, :]
    projection = (part + to_side(part)).reshape(rows, 1)
    grad_hidden = (
        own_inverse * own_gain[None, :] * normed_grad
        - own_hidden * (own_inverse * own_inverse * own_inverse) * projection / D
    ).astype(jnp.bfloat16)
    return (grad_hidden, grad_wkey)


def is_grouped(mesh_shape, rows, key_columns):
    members = key_columns // HD
    return (
        mesh_shape["tensor"] == 2
        and members == 4
        and mesh_shape["dp"] == 4 * members
        and members * rows == LONGEST
    )


def per_device(hidden, norm_gain, w_query, w_key, w_value, upstream, cached, lengths):
    arrays = (hidden, norm_gain, w_query, w_key, w_value, upstream, cached, lengths)
    sizes = {axis: lax.axis_size(axis) for axis in ("dp", "tensor")}
    if not is_grouped(sizes, hidden.shape[0], w_key.shape[1]):
        return plain_device(*arrays)
    return grouped_device(*arrays)


def solution(mesh):
    placed = (
        P("dp", "tensor"),
        P(),
        P("dp", "tensor"),
        P("dp", "tensor"),
        P("dp", "tensor"),
        P("dp", "tensor"),
        P(None, "tensor"),
        P(),
    )
    return jax.shard_map(
        per_device,
        mesh=mesh,
        in_specs=placed,
        out_specs=(P("dp", "tensor"), P("dp", "tensor")),
        check_vma=False,
    )
```

```python
from functools import partial

import jax
import jax.numpy as jnp
from jax import lax
from jax.experimental import pallas as pl
from jax.experimental.pallas import tpu as pltpu
from jax.sharding import PartitionSpec as P


D = 4096
HD = 128
HOPS = 4
LONGEST = 512
CHUNKS = (2, 2)


EPSILON = 1e-05
LOG2_E = 1.4426950408889634
ROPE_BASE = 500000.0


def from_behind(block, axis, distance):
    devices = range(lax.axis_size(axis))
    route = [(i - distance, i) for i in devices if i - distance in devices]
    return lax.ppermute(block, axis, route)


def document_info(lengths, positions_global):
    doc_ends = jnp.cumsum(lengths)
    documents = jnp.sum((positions_global[:, None] >= doc_ends[None, :]).astype(jnp.int32), axis=1)
    doc_slots = jnp.arange(lengths.shape[0], dtype=jnp.int32)
    onehot = documents[:, None] == doc_slots[None, :]
    doc_len = jnp.sum(jnp.where(onehot, lengths[None, :], 0), axis=1)
    doc_end = jnp.sum(jnp.where(onehot, doc_ends[None, :], 0), axis=1)
    return (documents, doc_len, positions_global - doc_end + doc_len, onehot)


def block_mask(lengths, query_positions, key_positions):
    query_docs = document_info(lengths, query_positions)[0]
    key_docs = document_info(lengths, key_positions)[0]
    return (
        (key_positions[None, :] >= 0)
        & (key_docs[None, :] == query_docs[:, None])
        & (key_positions[None, :] <= query_positions[:, None])
    )


def rope_tables(positions):
    half_width = HD // 2
    frequency = ROPE_BASE ** (-(jnp.arange(half_width, dtype=jnp.float32) * 2.0 / HD))
    angles = positions.astype(jnp.float32)[:, None] * frequency[None, :]
    angles = jnp.concatenate([angles, angles], axis=1)
    return (jnp.cos(angles), jnp.sin(angles))


def rotate(values, cosine_table, sine_table):
    half_width = values.shape[-1] // 2
    turned = jnp.concatenate([-values[..., half_width:], values[..., :half_width]], axis=-1)
    return values * cosine_table[:, None, :] + turned * sine_table[:, None, :]


def unrotate(gradient, cosine_table, sine_table):
    half_width = gradient.shape[-1] // 2
    scaled = gradient * sine_table[:, None, :]
    back_part = jnp.concatenate([scaled[..., half_width:], -scaled[..., :half_width]], axis=-1)
    return gradient * cosine_table[:, None, :] + back_part


def contract(left, right):
    return lax.dot_general(
        left, right, (((1,), (1,)), ((), ())), preferred_element_type=jnp.float32
    )


def attend_head(queries, key_rows, value_rows, out_grad, allowed):
    score_scale = HD ** (-0.5)
    scores = contract(queries, key_rows) * score_scale
    weights = jnp.where(allowed, jnp.exp(scores), 0.0)
    totals = jnp.sum(weights, axis=1, keepdims=True)
    softmax = weights / totals
    prob_grad = contract(out_grad, value_rows)
    row_delta = jnp.sum(softmax * prob_grad, axis=1, keepdims=True)
    score_grad = (softmax * (prob_grad - row_delta)).astype(jnp.bfloat16)
    query_grad = jnp.dot(score_grad, key_rows, preferred_element_type=jnp.float32) * score_scale
    key_grad = (
        lax.dot_general(
            score_grad, queries, (((0,), (0,)), ((), ())), preferred_element_type=jnp.float32
        )
        * score_scale
    )
    value_grad = lax.dot_general(
        softmax.astype(jnp.bfloat16),
        out_grad,
        (((0,), (0,)), ((), ())),
        preferred_element_type=jnp.float32,
    )
    return (query_grad, key_grad, value_grad, totals, row_delta)


def fold_heads(per_head, kv_count, group_size):
    summed = per_head.reshape(kv_count, group_size, per_head.shape[1], HD).sum(axis=1)
    return jnp.transpose(summed, (1, 0, 2))


def plain_device(hidden, norm_gain, w_query, w_key, w_value, upstream, cached, lengths):
    gathered = lax.all_gather(hidden, "tensor", axis=1, tiled=True)
    row_count = gathered.shape[0]
    query_cols = w_query.shape[1]
    key_cols = w_key.shape[1]
    head_count = query_cols // HD
    kv_count = key_cols // HD
    group_size = head_count // kv_count
    hidden_wide = gathered.astype(jnp.float32)
    inverse_scale = lax.rsqrt(jnp.mean(hidden_wide * hidden_wide, axis=1, keepdims=True) + EPSILON)
    normed = (hidden_wide * inverse_scale * norm_gain[None, :]).astype(jnp.bfloat16)
    dp_index = lax.axis_index("dp")
    own_positions = dp_index * row_count + jnp.arange(row_count, dtype=jnp.int32)
    _, doc_len, positions, onehot = document_info(lengths, own_positions)
    cosine_table, sine_table = rope_tables(positions)
    full_query, full_key, full_value = (
        lax.all_gather(w_query, "dp", axis=0, tiled=True),
        lax.all_gather(w_key, "dp", axis=0, tiled=True),
        lax.all_gather(w_value, "dp", axis=0, tiled=True),
    )
    query_proj = jnp.dot(normed, full_query, preferred_element_type=jnp.float32)
    key_proj = jnp.dot(normed, full_key, preferred_element_type=jnp.float32)
    value_proj = jnp.dot(normed, full_value, preferred_element_type=jnp.float32)
    queries = rotate(
        query_proj.reshape(row_count, head_count, HD), cosine_table, sine_table
    ).astype(jnp.bfloat16)
    key_rows = rotate(key_proj.reshape(row_count, kv_count, HD), cosine_table, sine_table).astype(
        jnp.bfloat16
    )
    value_rows = value_proj.astype(jnp.bfloat16).reshape(row_count, kv_count, HD)
    pooled = (
        jnp.dot(onehot.astype(jnp.float32), cached, precision=lax.Precision.HIGHEST)
        / doc_len.astype(jnp.float32)[:, None]
    )
    out_grad = (
        (upstream.astype(jnp.float32) + pooled)
        .astype(jnp.bfloat16)
        .reshape(row_count, head_count, HD)
    )
    key_list = []
    value_list = []
    for distance in range(HOPS, 0, -1):
        earlier_key, earlier_value = from_behind((key_rows, value_rows), "dp", distance)
        key_list.append(earlier_key)
        value_list.append(earlier_value)
    key_window = jnp.concatenate(key_list + [key_rows], axis=0)
    value_window = jnp.concatenate(value_list + [value_rows], axis=0)
    window = key_window.shape[0]
    window_positions = dp_index * row_count - HOPS * row_count + jnp.arange(window, dtype=jnp.int32)
    allowed = block_mask(lengths, own_positions, window_positions)
    head_queries = jnp.transpose(queries, (1, 0, 2))
    head_grads = jnp.transpose(out_grad, (1, 0, 2))
    head_keys = jnp.transpose(jnp.repeat(key_window, group_size, axis=1), (1, 0, 2))
    head_values = jnp.transpose(jnp.repeat(value_window, group_size, axis=1), (1, 0, 2))

    def one_head(operands):
        return attend_head(operands[0], operands[1], operands[2], operands[3], allowed)

    query_grad, key_grad, value_grad, _, _ = lax.map(
        one_head, (head_queries, head_keys, head_values, head_grads)
    )
    key_sum = fold_heads(key_grad, kv_count, group_size)
    value_sum = fold_heads(value_grad, kv_count, group_size)
    own_key = key_sum[HOPS * row_count :]
    own_value = value_sum[HOPS * row_count :]
    for distance in range(1, HOPS + 1):
        lower = (HOPS - distance) * row_count
        back_key, back_value = (
            from_behind(
                key_sum[lower : lower + row_count].astype(jnp.bfloat16), "dp", -distance
            ).astype(jnp.float32),
            from_behind(
                value_sum[lower : lower + row_count].astype(jnp.bfloat16), "dp", -distance
            ).astype(jnp.float32),
        )
        own_key = own_key + back_key
        own_value = own_value + back_value
    query_done = (
        unrotate(jnp.transpose(query_grad, (1, 0, 2)), cosine_table, sine_table)
        .astype(jnp.bfloat16)
        .reshape(row_count, query_cols)
    )
    key_done = (
        unrotate(own_key, cosine_table, sine_table)
        .astype(jnp.bfloat16)
        .reshape(row_count, key_cols)
    )
    value_done = own_value.astype(jnp.bfloat16).reshape(row_count, key_cols)
    portion = (
        contract(query_done, full_query)
        + contract(key_done, full_key)
        + contract(value_done, full_value)
    )
    own_hidden = hidden.astype(jnp.float32)
    own_cols = hidden.shape[1]
    gain_offset = lax.axis_index("tensor") * own_cols
    own_gain = lax.dynamic_slice_in_dim(norm_gain, gain_offset, own_cols, 0)
    normed_grad = lax.psum_scatter(
        portion.astype(jnp.bfloat16), "tensor", scatter_dimension=1, tiled=True
    ).astype(jnp.float32)
    projection = lax.psum(
        jnp.sum(normed_grad * own_gain[None, :] * own_hidden, axis=1, keepdims=True), "tensor"
    )
    grad_hidden = (
        inverse_scale * own_gain[None, :] * normed_grad
        - own_hidden * (inverse_scale * inverse_scale * inverse_scale) * projection / D
    ).astype(jnp.bfloat16)
    grad_wkey = lax.psum_scatter(
        lax.dot_general(
            normed, key_done, (((0,), (0,)), ((), ())), preferred_element_type=jnp.float32
        ),
        "dp",
        scatter_dimension=0,
        tiled=True,
    )
    return (grad_hidden, grad_wkey)


def after(array, *others):
    return lax.optimization_barrier((array, *others))[0]


def norm_kernel(where, near_ref, far_ref, gain_ref, *outs):
    pieces, inv_ref = outs[:-1], outs[-1]
    ring, tensor = where[0], where[2]
    ring_size = len(pieces)
    members = where.shape[0] - 3
    step = pieces[0].shape[1] // members

    def write(ref):
        total = jnp.zeros((ref.shape[2], 1), jnp.float32)
        for half in range(2):
            wide = ref[0, half].astype(jnp.float32)
            total = total + jnp.sum(wide * wide, axis=1, keepdims=True)
        inverse = lax.rsqrt(total / D + EPSILON)
        inv_ref[...] = jnp.broadcast_to(inverse, inv_ref.shape)
        planes_per_half = ring_size // 2
        for s in range(ring_size):
            plane = lax.rem(ring - s + ring_size, ring_size)
            half = lax.rem(plane // planes_per_half + tensor, 2)
            for d in range(members):
                inner = lax.rem(plane, planes_per_half) * (members * step) + where[3 + d] * step
                inner = pl.multiple_of(inner, step)
                outer = pl.multiple_of((plane * members + where[3 + d]) * step, step)
                wide = ref[0, half, :, pl.ds(inner, step)].astype(jnp.float32)
                scaled = wide * inverse * gain_ref[:, pl.ds(outer, step)]
                pieces[s][:, d * step : (d + 1) * step] = scaled.astype(jnp.bfloat16)

    @pl.when(pl.program_id(1) == 0)
    def _():
        write(near_ref)

    @pl.when(pl.program_id(1) == 1)
    def _():
        write(far_ref)


def norm_pieces(where, near, far, gain, ring_size):
    rows, half = near.shape[2], near.shape[3]
    members = where.shape[0] - 3
    tokens = members * rows
    width = 2 * half // ring_size
    spec = pl.BlockSpec((1, 2, rows, half), lambda u, v, w: (u, 0, 0, 0))

    def out_row(u, v, w):
        return (w[3 + 2 * u + v], 0)

    return pl.pallas_call(
        norm_kernel,
        grid_spec=pltpu.PrefetchScalarGridSpec(
            num_scalar_prefetch=1,
            grid=(2, 2),
            in_specs=[spec, spec, pl.BlockSpec((1, 2 * half), lambda u, v, w: (0, 0))],
            out_specs=[pl.BlockSpec((rows, width), out_row)] * ring_size
            + [pl.BlockSpec((rows, 128), out_row)],
        ),
        out_shape=[jax.ShapeDtypeStruct((tokens, width), jnp.bfloat16)] * ring_size
        + [jax.ShapeDtypeStruct((tokens, 128), jnp.float32)],
        compiler_params=pltpu.CompilerParams(vmem_limit_bytes=14 << 20),
        cost_estimate=pl.CostEstimate(
            flops=8 * tokens * 2 * half, bytes_accessed=8 * tokens * half, transcendentals=tokens
        ),
    )(where, near, far, gain)


def attend_kernel(heads, rows, terms, first, q_ref, *refs):
    n_refs, w_refs, refs = refs[:terms], refs[terms : 2 * terms], refs[2 * terms :]
    g_ref, k_ref, kt_ref, v_ref, cos_ref, sin_ref, low_ref = refs[:7]
    before = None if first else refs[7]
    dq_ref, halo_ref, own_ref, dkv_ref = refs[7 if first else 8 :]
    scale = HD ** (-0.5)
    halo = halo_ref.shape[0]
    window = halo + rows
    blocks = q_ref.shape[0] // rows

    @pl.when(pl.program_id(0) == 0)
    def _():
        dkv_ref[...] = jnp.zeros_like(dkv_ref)

    projected = q_ref[...]
    for n_ref, w_ref in zip(n_refs, w_refs):
        projected += jnp.dot(n_ref[...], w_ref[...], preferred_element_type=jnp.float32)
    key_at = lax.broadcasted_iota(jnp.int32, (window, rows), 0)
    query_at = lax.broadcasted_iota(jnp.int32, (rows, rows), 1)
    causal = key_at[:rows] <= query_at
    staged = []
    for block in range(blocks):
        here = slice(block * rows, (block + 1) * rows)
        base = pl.multiple_of((pl.program_id(0) * blocks + block) * rows, rows)
        cosine, sine = cos_ref[here, :], sin_ref[here, :]
        turned = []
        for h in range(heads):
            u = projected[here, h * HD : (h + 1) * HD]
            turned.append((u * cosine + pltpu.roll(u, HD // 2, 1) * sine).astype(jnp.bfloat16))
        queries = jnp.concatenate(turned, axis=0)
        grads = jnp.concatenate([g_ref[here, h * HD : (h + 1) * HD] for h in range(heads)], axis=0)
        scores = contract(k_ref[pl.ds(base, window), :], queries)
        prob_grads = contract(v_ref[pl.ds(base, window), :], grads)
        staged.append((here, base, cosine, sine, queries, grads, scores, prob_grads))
    for here, base, cosine, sine, queries, grads, scores, prob_grads in staged:
        low = low_ref[:, here] - base
        inside = key_at >= low
        allowed = (inside[:halo], inside[halo:] & causal)
        probs, score_grads = [], []
        for h in range(heads):
            there = slice(h * rows, (h + 1) * rows)
            grown = jnp.exp2(scores[:, there] * (scale * LOG2_E))
            weights = jnp.concatenate(
                [
                    jnp.where(allowed[0], grown[:halo], 0.0),
                    jnp.where(allowed[1], grown[halo:], 0.0),
                ],
                axis=0,
            )
            prob_grad = prob_grads[:, there]
            softmax = weights / jnp.sum(weights, axis=0, keepdims=True)
            row_delta = jnp.sum(softmax * prob_grad, axis=0, keepdims=True)
            probs.append(softmax.astype(jnp.bfloat16))
            score_grads.append((softmax * (prob_grad - row_delta)).astype(jnp.bfloat16))
        probs = jnp.concatenate(probs, axis=1)
        score_grads = jnp.concatenate(score_grads, axis=1)
        dkv_ref[pl.ds(base, window), :HD] += (
            jnp.dot(score_grads, queries, preferred_element_type=jnp.float32) * scale
        )
        dkv_ref[pl.ds(base, window), HD:] += jnp.dot(
            probs, grads, preferred_element_type=jnp.float32
        )
        query_grads = jnp.dot(
            kt_ref[:, pl.ds(base, window)], score_grads, preferred_element_type=jnp.float32
        )
        for h in range(heads):
            grad = query_grads[:, h * rows : (h + 1) * rows].T * scale
            back = grad * cosine - pltpu.roll(grad, HD // 2, 1) * sine
            dq_ref[here, h * HD : (h + 1) * HD] = back.astype(jnp.bfloat16)

    @pl.when(pl.program_id(0) == pl.num_programs(0) - 1)
    def _():
        halo_sum = dkv_ref[:halo, :]
        halo_ref[...] = halo_sum if first else (halo_sum + before[...]).astype(jnp.bfloat16)
        own_ref[...] = dkv_ref[halo:, :]


def attend(q_proj, normed, weights, grads, keys, keys_turned, values, cosine, sine, low, before=None):
    tokens, width = q_proj.shape
    heads, rows = width // HD, 128
    step = 2 * rows
    total = keys.shape[0]
    window = total - tokens + rows
    whole = lambda a: pl.BlockSpec(a.shape, lambda i: (0, 0))
    by_rows = lambda w: pl.BlockSpec((step, w), lambda i: (i, 0))
    fixed = lambda n, w: pl.BlockSpec((n, w), lambda i: (0, 0))
    extra = [] if before is None else [before]
    operands = [q_proj, *normed, *weights, grads, keys, keys_turned, values, cosine, sine, low]
    operands = [pltpu.with_memory_space_constraint(a, pltpu.HBM) for a in operands + extra]
    return pl.pallas_call(
        partial(attend_kernel, heads, rows, len(normed), before is None),
        grid=(tokens // step,),
        in_specs=[by_rows(width)]
        + [by_rows(n.shape[1]) for n in normed]
        + [whole(w) for w in weights]
        + [by_rows(width), whole(keys), whole(keys_turned), whole(values)]
        + [by_rows(HD), by_rows(HD), pl.BlockSpec((1, step), lambda i: (0, i))]
        + [fixed(total - tokens, 2 * HD) for _ in extra],
        out_specs=[by_rows(width), fixed(total - tokens, 2 * HD), fixed(tokens, 2 * HD)],
        out_shape=[jax.ShapeDtypeStruct((tokens, width), jnp.bfloat16),
                   jax.ShapeDtypeStruct(
                       (total - tokens, 2 * HD), jnp.float32 if before is None else jnp.bfloat16
                   ),
                   jax.ShapeDtypeStruct((tokens, 2 * HD), jnp.float32)],
        scratch_shapes=[pltpu.VMEM((total, 2 * HD), jnp.float32)],
        compiler_params=pltpu.CompilerParams(vmem_limit_bytes=24 << 20),
        cost_estimate=pl.CostEstimate(
            flops=10 * tokens * window * width, bytes_accessed=12 * tokens * width,
            transcendentals=tokens * window * heads,
        ),
    )(*operands)


def spread_blocks(where, wide, grads, rows):
    members = where.shape[0] - 3
    for block in range(members):
        partner = (block % (members // 2)) * 2 + block // (members // 2)
        source = pl.multiple_of(where[3 + partner] * rows, rows)
        at = 0
        for grad in grads:
            wide[block * rows : (block + 1) * rows, at : at + grad.shape[1]] = grad[
                pl.ds(source, rows), :
            ]
            at += grad.shape[1]


def spread_first_kernel(counts, ring_size, where, *refs):
    grads, weights = refs[: counts[0]], refs[counts[0] : counts[0] + counts[1] * ring_size]
    out_ref, wide, held, arrived = refs[counts[0] + counts[1] * ring_size :]
    members = where.shape[0] - 3
    step = held.shape[1] // members
    s = pl.program_id(0)

    def copy(source, piece, c):
        width = source.shape[1]
        return pltpu.make_async_copy(
            source, held.at[piece, :, pl.ds(c * width, width)], arrived.at[piece, c]
        )

    @pl.when(s == 0)
    def _():
        for piece in range(ring_size):
            for c in range(counts[1]):
                copy(weights[c * ring_size + piece], piece, c).start()
        spread_blocks(where, wide, grads, wide.shape[0] // members)

    for c in range(counts[1]):
        copy(weights[c * ring_size], s, c).wait()
    for owner in range(members):
        source = pl.multiple_of(where[3 + owner] * step, step)
        out_ref[0, :, owner * step : (owner + 1) * step] = contract(
            wide[...], held[s, pl.ds(source, step), :]
        )


def spread_first(where, grads, weights, ring_size):
    tokens = grads[0].shape[0]
    depth = sum(a.shape[1] for a in grads)
    width = weights[0].shape[0]
    chunks = len(weights) // ring_size
    return pl.pallas_call(
        partial(spread_first_kernel, (len(grads), chunks), ring_size),
        grid_spec=pltpu.PrefetchScalarGridSpec(
            num_scalar_prefetch=1,
            grid=(ring_size,),
            in_specs=[pl.BlockSpec(a.shape, lambda i, w: (0, 0)) for a in grads]
            + [pl.BlockSpec(memory_space=pltpu.HBM) for _ in weights],
            out_specs=pl.BlockSpec((1, tokens, width), lambda i, w: (i, 0, 0)),
            scratch_shapes=[
                pltpu.VMEM((tokens, depth), jnp.bfloat16),
                pltpu.VMEM((ring_size, width, depth), jnp.bfloat16),
                pltpu.SemaphoreType.DMA((ring_size, chunks)),
            ],
        ),
        out_shape=jax.ShapeDtypeStruct((ring_size, tokens, width), jnp.float32),
        compiler_params=pltpu.CompilerParams(vmem_limit_bytes=14 << 20),
        cost_estimate=pl.CostEstimate(
            flops=2 * tokens * width * ring_size * depth,
            bytes_accessed=4 * tokens * width * ring_size,
            transcendentals=0,
        ),
    )(where, *grads, *weights)


def spread_last_kernel(parts, where, so_far, *refs):
    owns, (back_ref, cos_ref, sin_ref) = refs[:parts], refs[parts : parts + 3]
    weights = refs[parts + 3 : -4]
    key_ref, keep_ref, send_ref, wide = refs[-4:]
    members = where.shape[0] - 3
    step = weights[0].shape[0] // members
    rows = keep_ref.shape[2]
    s = pl.program_id(0)

    @pl.when(s == 0)
    def _():
        for block in range(members):
            partner = (block % (members // 2)) * 2 + block // (members // 2)
            lines = pl.ds(pl.multiple_of(where[3 + partner] * rows, rows), rows)
            grad = back_ref[lines, :].astype(jnp.float32)
            for own in owns:
                grad += own[lines, :]
            key_grad = grad[:, :HD]
            turned = pltpu.roll(key_grad, HD // 2, 1)
            key_done = key_grad * cos_ref[lines, :] - turned * sin_ref[lines, :]
            key_ref[lines, :] = key_done.astype(jnp.bfloat16)
            here = slice(block * rows, (block + 1) * rows)
            wide[here, :HD] = key_done.astype(jnp.bfloat16)
            wide[here, HD:] = grad[:, HD:].astype(jnp.bfloat16)

    for piece, weight in enumerate(weights):

        @pl.when(s == piece)
        def _():
            for owner in range(members):
                source = pl.multiple_of(where[3 + owner] * step, step)
                lanes = slice(owner * step, (owner + 1) * step)
                total = so_far[0, :, lanes] + contract(wide[...], weight[pl.ds(source, step), :])
                total = total.astype(jnp.bfloat16)
                for u in range(members // 2):
                    keep_ref[u, 0, :, lanes] = total[u * rows : (u + 1) * rows, :]
                    lower = (members // 2 + u) * rows
                    send_ref[u, 0, :, lanes] = total[lower : lower + rows, :]


def spread_last(where, so_far, owns, back, cosine, sine, weights, ring_size):
    tokens = back.shape[0]
    members = where.shape[0] - 3
    rows = tokens // members
    width = weights[0].shape[0]
    planes_per_half = ring_size // 2
    whole = lambda a: pl.BlockSpec(a.shape, lambda i, w: (0, 0))

    def out_at(s, w):
        plane = lax.rem(w[0] - s + ring_size, ring_size)
        half = lax.rem(plane // planes_per_half + w[2], 2)
        return (0, half, 0, lax.rem(plane, planes_per_half))

    shape = (members // 2, 2, rows, width * planes_per_half)
    small = [*owns, back, cosine, sine]
    return pl.pallas_call(
        partial(spread_last_kernel, len(owns)),
        grid_spec=pltpu.PrefetchScalarGridSpec(
            num_scalar_prefetch=1,
            grid=(ring_size,),
            in_specs=[pl.BlockSpec((1, tokens, width), lambda i, w: (i, 0, 0))]
            + [whole(a) for a in small]
            + [pl.BlockSpec(memory_space=pltpu.VMEM) for a in weights],
            out_specs=[pl.BlockSpec((tokens, HD), lambda i, w: (0, 0))]
            + [pl.BlockSpec((members // 2, 1, rows, width), out_at)] * 2,
            scratch_shapes=[pltpu.VMEM((tokens, 2 * HD), jnp.bfloat16)],
        ),
        out_shape=[jax.ShapeDtypeStruct((tokens, HD), jnp.bfloat16)]
        + [jax.ShapeDtypeStruct(shape, jnp.bfloat16)] * 2,
        compiler_params=pltpu.CompilerParams(vmem_limit_bytes=14 << 20),
        cost_estimate=pl.CostEstimate(
            flops=4 * tokens * width * ring_size * HD,
            bytes_accessed=4 * tokens * width * ring_size,
            transcendentals=0,
        ),
    )(where, so_far, *small, *weights)


def key_weights_kernel(ring_size, where, *refs):
    members = where.shape[0] - 3
    normed, grads = refs[:ring_size], refs[ring_size : ring_size + members]
    out_refs, wide = refs[ring_size + members : -1], refs[-1]
    width = grads[0].shape[1]
    for owner in range(members):
        for d in range(members):

            @pl.when(where[3 + owner] == d)
            def _():
                wide[:, owner * width : (owner + 1) * width] = grads[d][...]

    for n_ref, out_ref in zip(normed, out_refs):
        out_ref[...] = lax.dot_general(
            n_ref[...], wide[...], (((0,), (0,)), ((), ())), preferred_element_type=jnp.float32
        ).astype(out_ref.dtype)


def key_weights(where, normed, grads, rows, dtype):
    tokens, members = grads[0].shape[0], len(grads)
    width = members * grads[0].shape[1]
    shape = (rows, width)
    return pl.pallas_call(
        partial(key_weights_kernel, len(normed)),
        grid_spec=pltpu.PrefetchScalarGridSpec(
            num_scalar_prefetch=1,
            grid=(1,),
            in_specs=[pl.BlockSpec((tokens, rows), lambda i, w: (0, 0)) for _ in normed]
            + [pl.BlockSpec(g.shape, lambda i, w: (0, 0)) for g in grads],
            out_specs=[pl.BlockSpec(shape, lambda i, w: (0, 0))] * len(normed),
            scratch_shapes=[pltpu.VMEM((tokens, width), jnp.bfloat16)],
        ),
        out_shape=[jax.ShapeDtypeStruct(shape, dtype)] * len(normed),
        compiler_params=pltpu.CompilerParams(vmem_limit_bytes=10 << 20),
        cost_estimate=pl.CostEstimate(
            flops=2 * tokens * width * rows * len(normed),
            bytes_accessed=2 * tokens * (width + rows * len(normed)),
            transcendentals=0,
        ),
    )(where, *normed, *grads)


def grouped_device(hidden, norm_gain, w_query, w_key, w_value, upstream, cached, lengths):
    rows, half = hidden.shape
    kv_count = w_key.shape[1] // HD
    query_width = w_query.shape[1] // kv_count
    members = kv_count
    devices, tensors = lax.axis_size("dp"), lax.axis_size("tensor")
    ring_size = devices // members
    tokens = members * rows
    weight_rows = w_key.shape[0]
    me, tensor = lax.axis_index("dp"), lax.axis_index("tensor")
    ring, group = me // members, me % members
    partners = [jnp.bitwise_xor(group, d) for d in range(members)]
    where = jnp.stack([ring, group, tensor] + partners).astype(jnp.int32)

    def to_partner(block, d):
        return lax.ppermute(block, "dp", [(i, i ^ d) for i in range(devices)])

    def to_side(block):
        return lax.ppermute(block, "tensor", [(i, i ^ 1) for i in range(tensors)])

    def along(block, distance):
        route = [(i, (i + distance * members) % devices) for i in range(devices)]
        return lax.ppermute(block, "dp", route)

    def columns(array, owner, width):
        return lax.dynamic_slice_in_dim(array, owner * width, width, 1)

    def circulate(own, gate=None):
        pieces = [own]
        for hop in range(1, ring_size):
            block = pieces[-1] if gate is None else gate(hop, pieces[-1])
            pieces.append(along(block, 1))
        return pieces

    k_ring, v_ring = circulate(w_key), circulate(w_value)

    def pack_q(owner):
        return jnp.concatenate(
            [columns(w_query, owner, query_width), columns(upstream, owner, query_width)], axis=0
        )

    q_parts = [pack_q(group)] + [to_partner(pack_q(partners[d]), d) for d in range(1, members)]
    q_own = jnp.concatenate([p[:weight_rows] for p in q_parts], axis=0)
    ends = [sum(CHUNKS[: c + 1]) * HD for c in range(len(CHUNKS))]
    spans = [slice(end - count * HD, end) for end, count in zip(ends, CHUNKS)]
    q_chunk = [q_own[:, span] for span in spans]

    def pack_kv(owner):
        pairs = []
        for k, v in zip(k_ring, v_ring):
            cut = [columns(k, owner, HD), columns(v, owner, HD)]
            pairs.append(lax.optimization_barrier(jnp.concatenate(cut, axis=1)))
        return jnp.concatenate(pairs, axis=0)

    across = to_partner(hidden, 2)
    beside = to_side(hidden)
    corner = to_side(across)
    near = jnp.stack([hidden, beside, across, corner]).reshape(2, 2, rows, half)
    far = to_partner(near, 1)
    *normed, inverse = norm_pieces(where, near, far, norm_gain[None, :], ring_size)

    kv_parts = [pack_kv(group)] + [
        after(to_partner(pack_kv(partners[d]), d), normed[0])
        for d in range(1, members)
    ]
    kv_pieces = [
        jnp.concatenate([p[s * weight_rows : (s + 1) * weight_rows] for p in kv_parts], axis=0)
        for s in range(ring_size)
    ]

    def project(pieces):
        total = None
        for s, piece in enumerate(pieces):
            term = jnp.dot(normed[s], piece, preferred_element_type=jnp.float32)
            total = term if total is None else total + term
        return total

    first = ring * tokens
    token_positions = first + jnp.arange(tokens, dtype=jnp.int32)
    _, doc_len, positions, onehot = document_info(lengths, token_positions)
    cosine, sine = rope_tables(positions)
    sign = jnp.where(jnp.arange(HD) < HD // 2, -1.0, 1.0).astype(jnp.float32)
    sine = sine * sign[None, :]
    low = (token_positions - positions - first + LONGEST)[None, :]

    def place(parts):
        stacked = jnp.stack(parts)
        return [
            lax.dynamic_index_in_dim(stacked, jnp.bitwise_xor(group, o), 0, keepdims=False)
            for o in range(members)
        ]

    up_own = jnp.concatenate(place([p[weight_rows:] for p in q_parts]), axis=0)
    pooled = (
        jnp.dot(
            onehot.astype(jnp.float32),
            columns(cached, group, query_width),
            precision=lax.Precision.HIGHEST,
        )
        / doc_len.astype(jnp.float32)[:, None]
    )
    out_grad = (up_own.astype(jnp.float32) + pooled).astype(jnp.bfloat16)

    kv_proj = project(kv_pieces)
    key_proj = kv_proj[:, :HD]
    key_own = key_proj * cosine + jnp.roll(key_proj, HD // 2, axis=1) * sine
    kv_rows = jnp.concatenate([key_own, kv_proj[:, HD:]], axis=1).astype(jnp.bfloat16)

    q_pieces = []
    for c in range(len(CHUNKS)):
        gate = lambda hop, block, c=c: after(block, kv_rows) if c and hop == ring_size - 1 else block
        q_pieces.append(circulate(q_chunk[c], gate))
    halo = lax.ppermute(kv_rows, "dp", [(i, i + members) for i in range(devices - members)])
    kv_all = jnp.concatenate([halo, kv_rows], axis=0)
    keys, values = kv_all[:, :HD], kv_all[:, HD:]
    keys_turned = keys.T
    query_dones, owns, halo_grad = [], [], None
    for c in range(len(CHUNKS)):
        early = lax.optimization_barrier(project(q_pieces[c][:-1]))
        query_done, halo_grad, own_grad = attend(
            early, normed[-1:], q_pieces[c][-1:],
            out_grad[:, spans[c]],
            keys, keys_turned, values, cosine, sine, low, halo_grad,
        )
        query_dones.append(query_done)
        owns.append(own_grad)
    later = [(i + members, i) for i in range(devices - members)]
    back = lax.ppermute(halo_grad, "dp", later)

    weights = [
        pltpu.with_memory_space_constraint(piece, pltpu.HBM)
        for pieces in q_pieces
        for piece in pieces
    ]
    so_far = spread_first(where, query_dones, weights, ring_size)
    own_sum = lax.optimization_barrier(sum(owns[1:], owns[0]))
    in_hbm = [pltpu.with_memory_space_constraint(a, pltpu.HBM) for a in (cosine, sine)]
    key_done, keep, send = spread_last(
        where, so_far, [own_sum], back, *in_hbm, kv_pieces, ring_size
    )

    key_dones = [key_done] + [to_partner(key_done, d) for d in range(1, members)]
    others = key_weights(where, normed[1:], key_dones, weight_rows, jnp.bfloat16)
    (grad_wkey,) = key_weights(where, normed[:1], key_dones, weight_rows, jnp.float32)
    for s in range(1, ring_size):
        term = along(others[s - 1], -s)
        grad_wkey = grad_wkey + term.astype(jnp.float32)

    wide = lambda a: a.astype(jnp.float32)
    narrow = lambda a: a.astype(jnp.bfloat16)
    other = to_partner(send, 1)
    both = lambda *at: wide(keep[at]) + wide(other[at])
    cut = half // 2
    low_cut, high_cut, every = slice(0, cut), slice(cut, half), slice(None)
    left_half = narrow(both(1, every, every, low_cut))
    right_half = narrow(both(every, 1, every, high_cut))
    left_half = to_partner(left_half, 2)
    right_half = to_side(right_half)
    left_next = narrow(both(0, 1, every, low_cut) + wide(left_half[1]))
    right_next = narrow(both(1, 0, every, high_cut) + wide(right_half[1]))
    left_next, right_next = lax.optimization_barrier((left_next, right_next))
    right_next = to_partner(right_next, 2)
    left_next = to_side(left_next)
    left_sum = both(0, 0, every, low_cut) + wide(left_half[0]) + wide(left_next)
    right_sum = both(0, 0, every, high_cut) + wide(right_half[0]) + wide(right_next)
    normed_grad = jnp.concatenate([left_sum, right_sum], axis=1)
    own_hidden = wide(hidden)
    own_gain = lax.dynamic_slice_in_dim(norm_gain, tensor * half, half, 0)
    own_inverse = lax.dynamic_slice_in_dim(inverse, group * rows, rows, 0)[:, :1]
    part = jnp.sum(normed_grad * own_gain[None, :] * own_hidden, axis=1)[None, :]
    projection = (part + to_side(part)).reshape(rows, 1)
    grad_hidden = (
        own_inverse * own_gain[None, :] * normed_grad
        - own_hidden * (own_inverse * own_inverse * own_inverse) * projection / D
    ).astype(jnp.bfloat16)
    return (grad_hidden, grad_wkey)


def is_grouped(mesh_shape, rows, key_columns):
    members = key_columns // HD
    return (
        mesh_shape["tensor"] == 2
        and members == 4
        and mesh_shape["dp"] == 4 * members
        and members * rows == LONGEST
    )


def per_device(hidden, norm_gain, w_query, w_key, w_value, upstream, cached, lengths):
    arrays = (hidden, norm_gain, w_query, w_key, w_value, upstream, cached, lengths)
    sizes = {axis: lax.axis_size(axis) for axis in ("dp", "tensor")}
    if not is_grouped(sizes, hidden.shape[0], w_key.shape[1]):
        return plain_device(*arrays)
    return grouped_device(*arrays)


def solution(mesh):
    placed = (
        P("dp", "tensor"),
        P(),
        P("dp", "tensor"),
        P("dp", "tensor"),
        P("dp", "tensor"),
        P("dp", "tensor"),
        P(None, "tensor"),
        P(),
    )
    return jax.shard_map(
        per_device,
        mesh=mesh,
        in_specs=placed,
        out_specs=(P("dp", "tensor"), P("dp", "tensor")),
        check_vma=False,
    )
```
